32 devices in a mesh: dp: 2 (over y), row: 4 (over x, core), col: 4 (over z).
Axes of the slice: x: 2, y: 2, z: 4, core: 2. Of those that a mesh axis runs over, the one named last changes fastest.
Arguments:
- tokens: bfloat16 [10240, 2048], P(('dp', 'col'), 'row'), may hold values from -6 to 6
- cotangent: bfloat16 [10240, 2048], P(('dp', 'col'), 'row'), may hold values from -6 to 6
- attention_norm_gain: float32 [2048], P('row'), may hold values from 0.5 to 1.5
- feedfwd_norm_gain: float32 [2048], P('row'), may hold values from 0.5 to 1.5
- query_norm_gain: float32 [128], replicated, may hold values from 0.8 to 2
- key_norm_gain: float32 [128], replicated, may hold values from 0.8 to 2
- query_matrix: bfloat16 [2048, 2048], P('row', 'col'), may hold values from -0.125 to 0.125
- key_matrix: bfloat16 [2048, 1024], P('row', 'col'), may hold values from -0.125 to 0.125
- value_matrix: bfloat16 [2048, 1024], P('row', 'col'), may hold values from -0.125 to 0.125
- output_matrix: bfloat16 [2048, 2048], P('col', 'row'), may hold values from -0.5 to 0.5
- gate_matrix: bfloat16 [2048, 6144], P('row', 'col'), may hold values from -0.125 to 0.125
- up_matrix: bfloat16 [2048, 6144], P('row', 'col'), may hold values from -0.125 to 0.125
- down_matrix: bfloat16 [6144, 2048], P('col', 'row'), may hold values from -0.078125 to 0.078125
- query_adapter_inmaps: bfloat16 [2048, 128], P('row'), may hold values from -0.125 to 0.125
- query_adapter_outmaps: bfloat16 [128, 2048], P(None, 'col'), may hold values from -0.75 to 0.75
- key_adapter_inmaps: bfloat16 [2048, 128], P('row'), may hold values from -0.125 to 0.125
- key_adapter_outmaps: bfloat16 [128, 1024], P(None, 'col'), may hold values from -0.75 to 0.75
- value_adapter_inmaps: bfloat16 [2048, 128], P('row'), may hold values from -0.125 to 0.125
- value_adapter_outmaps: bfloat16 [128, 1024], P(None, 'col'), may hold values from -0.75 to 0.75
- output_adapter_inmaps: bfloat16 [2048, 128], P('col'), may hold values from -0.5 to 0.5
- output_adapter_outmaps: bfloat16 [128, 2048], P(None, 'row'), may hold values from -0.75 to 0.75
- gate_adapter_inmaps: bfloat16 [2048, 128], P('row'), may hold values from -0.125 to 0.125
- gate_adapter_outmaps: bfloat16 [128, 6144], P(None, 'col'), may hold values from -0.75 to 0.75
- up_adapter_inmaps: bfloat16 [2048, 128], P('row'), may hold values from -0.125 to 0.125
- up_adapter_outmaps: bfloat16 [128, 6144], P(None, 'col'), may hold values from -0.75 to 0.75
- down_adapter_inmaps: bfloat16 [6144, 128], P('col'), may hold values from -0.078125 to 0.078125
- down_adapter_outmaps: bfloat16 [128, 2048], P(None, 'row'), may hold values from -0.75 to 0.75
- segment: int32 [10240], P('dp'), may hold values from 0 to 12, as said below
- depth: int32 [10240], P('dp'), may hold values from 0 to 2559, as said below
- parent: int32 [2, 13], P('dp'), may hold values from 0 to 4, as said below
- adapter: int32 [2], P('dp'), may hold values from 0 to 7
Outputs:
- output: bfloat16 [10240, 2048], P(('dp', 'col'), 'row')
- input_gradient: float32 [10240, 2048], P(('dp', 'col'), 'row')
- grad_a_q: float32 [2048, 128], P('row')
- grad_b_q: float32 [128, 2048], P(None, 'col')
- grad_a_k: float32 [2048, 128], P('row')
- grad_b_k: float32 [128, 1024], P(None, 'col')
- grad_a_v: float32 [2048, 128], P('row')
- grad_b_v: float32 [128, 1024], P(None, 'col')
- grad_a_o: float32 [2048, 128], P('col')
- grad_b_o: float32 [128, 2048], P(None, 'row')
- grad_a_gate: float32 [2048, 128], P('row')
- grad_b_gate: float32 [128, 6144], P(None, 'col')
- grad_a_up: float32 [2048, 128], P('row')
- grad_b_up: float32 [128, 6144], P(None, 'col')
- grad_a_down: float32 [6144, 128], P('col')
- grad_b_down: float32 [128, 2048], P(None, 'row')
The draws below stay inside these ranges and needn't reach their ends.
Inputs may be any that keep to these rules, and one draw needn't show every extreme that they name: `segment`: in each tree, the first 2048 tokens are node 0, the trunk; the rest are 12 blocks of 256 tokens, one block for each of the nodes 1 to 4 (branches) and 5 onward (leaves), in any order. Trunk tokens have depth 0 to 2047 in order, a branch's tokens 2048 onward, a leaf's tokens 2048 + 256 onward, in order within the block. The trunk and every branch have parent 0; every leaf's parent is a branch, each branch having 8 // 4 leaves.
All inputs are finite; a program needn't handle non-finite values.
Results may differ from the reference program's by a relative error of at most 0.017.
The reference program's roundings to bfloat16 on the way count: a program that leaves them out, or rounds other values in their place, can miss the bound.
Values may be sent and summed in bfloat16 or wider, within the bound.
No kernel may reach another device: no remote copies, remote signals or barrier semaphores. Data moves between devices by JAX's collectives and lax.ppermute only.
A program may use at most 384 MiB of HBM per device.

```python
import math
import jax
import jax.numpy as jnp
from jax import lax

MODEL_WIDTH = 2048
QUERY_HEADS = 16
KEY_VALUE_HEADS = 8
HEAD_SIZE = 128
FEEDFWD_UNITS = 6144
ADAPTER_RANK = 16
NADAPT = 8
ADAPTER_COLUMNS = 128
TRUNK = 2048
SEG_LEN = 256
BRANCHES = 4
LEAVES = 8
TREE_LEN = 5120
TREES = 2
TOK = 10240


def tree_layout(key):
    frozen_product = jax.random.fold_in(key, 7331)
    tree_keys = jax.random.split(frozen_product, TREES)
    order = jax.vmap(lambda item: jax.random.permutation(jax.random.fold_in(item, 1), BRANCHES + LEAVES))(tree_keys) + 1
    leaf_slots = jax.vmap(lambda item: jax.random.permutation(jax.random.fold_in(item, 2), LEAVES))(tree_keys)
    per_branch = LEAVES // BRANCHES
    leaf_parent = (1 + leaf_slots // per_branch).astype(jnp.int32)
    parent = jnp.concatenate([jnp.zeros((TREES, 1 + BRANCHES), jnp.int32), leaf_parent], axis=1)
    node_seg = jnp.repeat(order.astype(jnp.int32), SEG_LEN, axis=1)
    segment = jnp.concatenate([jnp.zeros((TREES, TRUNK), jnp.int32), node_seg], axis=1).reshape(-1)
    inside = jnp.arange((BRANCHES + LEAVES) * SEG_LEN) % SEG_LEN
    node_depth = TRUNK + inside[None, :] + jnp.where(node_seg > BRANCHES, SEG_LEN, 0)
    trunk_depth = jnp.broadcast_to(jnp.arange(TRUNK)[None, :], (TREES, TRUNK))
    depth = jnp.concatenate([trunk_depth, node_depth], axis=1).reshape(-1).astype(jnp.int32)
    return (segment, depth, parent)


def draw_segment(key, part):
    return tree_layout(key)[0]


def draw_depth(key, part):
    return tree_layout(key)[1]


def draw_parent(key, part):
    return tree_layout(key)[2]


def steps_of(key, extent, cuts, least, largest):
    def one(axis_at, parts):
        heights = jax.random.uniform(jax.random.fold_in(jax.random.fold_in(key, 6), axis_at), (parts,), jnp.float32, least / len(cuts), largest / len(cuts))
        return jnp.repeat(jnp.exp(heights), extent[axis_at] // parts).reshape((-1,) + (1,) * (len(extent) - axis_at - 1))

    factor_of = one(*cuts[0])
    for cut in cuts[1:]:
        factor_of = factor_of * one(*cut)
    return factor_of


def noise(own_key, extent, deviation, limit, shards=(), dtype=jnp.bfloat16):
    array = deviation * jax.random.normal(own_key, extent, jnp.float32)
    if shards:
        array = array * steps_of(own_key, extent, shards, -0.22, 0.18)
    return jnp.clip(array, -limit, limit).astype(dtype)


def setup_inputs(seed: int = 0) -> dict:
    splits = jax.random.split(jax.random.key(seed), 32)
    return {
        "tokens": noise(splits[0], (TOK, MODEL_WIDTH), 1.0, 6.0, ((0, 8), (1, 4))),
        "cotangent": noise(splits[1], (TOK, MODEL_WIDTH), 1.0, 6.0, ((0, 8), (1, 4))),
        "attention_norm_gain": jnp.clip(1.0 + 0.1 * jax.random.normal(splits[2], (MODEL_WIDTH,), jnp.float32), 0.5, 1.5),
        "feedfwd_norm_gain": jnp.clip(1.0 + 0.1 * jax.random.normal(splits[3], (MODEL_WIDTH,), jnp.float32), 0.5, 1.5),
        "query_norm_gain": jnp.clip(jnp.exp(jax.random.uniform(splits[4], (HEAD_SIZE,), jnp.float32, math.log(0.8), math.log(2.0))), 0.8, 2.0),
        "key_norm_gain": jnp.clip(jnp.exp(jax.random.uniform(splits[5], (HEAD_SIZE,), jnp.float32, math.log(0.8), math.log(2.0))), 0.8, 2.0),
        "query_matrix": noise(splits[6], (MODEL_WIDTH, QUERY_HEADS * HEAD_SIZE), MODEL_WIDTH ** -0.5, 0.125, ((0, 4), (1, 4))),
        "key_matrix": noise(splits[7], (MODEL_WIDTH, KEY_VALUE_HEADS * HEAD_SIZE), MODEL_WIDTH ** -0.5, 0.125, ((0, 4), (1, 4))),
        "value_matrix": noise(splits[8], (MODEL_WIDTH, KEY_VALUE_HEADS * HEAD_SIZE), MODEL_WIDTH ** -0.5, 0.125, ((0, 4), (1, 4))),
        "output_matrix": noise(splits[9], (QUERY_HEADS * HEAD_SIZE, MODEL_WIDTH), (QUERY_HEADS * HEAD_SIZE // 16) ** -0.5, 0.5, ((0, 4), (1, 4))),
        "gate_matrix": noise(splits[10], (MODEL_WIDTH, FEEDFWD_UNITS), MODEL_WIDTH ** -0.5, 0.125, ((0, 4), (1, 4))),
        "up_matrix": noise(splits[11], (MODEL_WIDTH, FEEDFWD_UNITS), MODEL_WIDTH ** -0.5, 0.125, ((0, 4), (1, 4))),
        "down_matrix": noise(splits[12], (FEEDFWD_UNITS, MODEL_WIDTH), FEEDFWD_UNITS ** -0.5, 0.078125, ((0, 4), (1, 4))),
        "query_adapter_inmaps": noise(splits[13], (MODEL_WIDTH, ADAPTER_COLUMNS), MODEL_WIDTH ** -0.5, 0.125, ((0, 4),)),
        "query_adapter_outmaps": noise(splits[14], (ADAPTER_COLUMNS, QUERY_HEADS * HEAD_SIZE), (4 * ADAPTER_RANK) ** -0.5, 0.75, ((1, 4),)),
        "key_adapter_inmaps": noise(splits[15], (MODEL_WIDTH, ADAPTER_COLUMNS), MODEL_WIDTH ** -0.5, 0.125, ((0, 4),)),
        "key_adapter_outmaps": noise(splits[16], (ADAPTER_COLUMNS, KEY_VALUE_HEADS * HEAD_SIZE), (4 * ADAPTER_RANK) ** -0.5, 0.75, ((1, 4),)),
        "value_adapter_inmaps": noise(splits[17], (MODEL_WIDTH, ADAPTER_COLUMNS), MODEL_WIDTH ** -0.5, 0.125, ((0, 4),)),
        "value_adapter_outmaps": noise(splits[18], (ADAPTER_COLUMNS, KEY_VALUE_HEADS * HEAD_SIZE), (4 * ADAPTER_RANK) ** -0.5, 0.75, ((1, 4),)),
        "output_adapter_inmaps": noise(splits[19], (QUERY_HEADS * HEAD_SIZE, ADAPTER_COLUMNS), (QUERY_HEADS * HEAD_SIZE // 16) ** -0.5, 0.5, ((0, 4),)),
        "output_adapter_outmaps": noise(splits[20], (ADAPTER_COLUMNS, MODEL_WIDTH), (4 * ADAPTER_RANK) ** -0.5, 0.75, ((1, 4),)),
        "gate_adapter_inmaps": noise(splits[21], (MODEL_WIDTH, ADAPTER_COLUMNS), MODEL_WIDTH ** -0.5, 0.125, ((0, 4),)),
        "gate_adapter_outmaps": noise(splits[22], (ADAPTER_COLUMNS, FEEDFWD_UNITS), (4 * ADAPTER_RANK) ** -0.5, 0.75, ((1, 4),)),
        "up_adapter_inmaps": noise(splits[23], (MODEL_WIDTH, ADAPTER_COLUMNS), MODEL_WIDTH ** -0.5, 0.125, ((0, 4),)),
        "up_adapter_outmaps": noise(splits[24], (ADAPTER_COLUMNS, FEEDFWD_UNITS), (4 * ADAPTER_RANK) ** -0.5, 0.75, ((1, 4),)),
        "down_adapter_inmaps": noise(splits[25], (FEEDFWD_UNITS, ADAPTER_COLUMNS), FEEDFWD_UNITS ** -0.5, 0.078125, ((0, 4),)),
        "down_adapter_outmaps": noise(splits[26], (ADAPTER_COLUMNS, MODEL_WIDTH), (4 * ADAPTER_RANK) ** -0.5, 0.75, ((1, 4),)),
        "segment": draw_segment(jax.random.fold_in(splits[31], 71), 0),
        "depth": draw_depth(jax.random.fold_in(splits[31], 71), 0),
        "parent": draw_parent(jax.random.fold_in(splits[31], 71), 0),
        "adapter": jax.random.randint(splits[30], (TREES,), 0, NADAPT).astype(jnp.int32),
    }


@jax.custom_vjp
def low(v):
    return lax.optimization_barrier(v.astype(jnp.bfloat16)).astype(jnp.float32)

@jax.custom_vjp
def reduced_gradient(v):
    return v

def low_keep(v):
    return (low(v), None)

def low_pass(kept, grad):
    return (grad,)

def back_keep(v):
    return (v, None)

def back_low(kept, grad):
    return (low(grad),)
low.defvjp(low_keep, low_pass)
reduced_gradient.defvjp(back_keep, back_low)
EPSILON = 1e-06
THETA = 1000000.0
ADAPTER_FACTOR = 2.0
HIGH = lax.Precision.HIGHEST
NEGATIVE = -1e+30

def matrix_product(left, right):
    return jnp.dot(left, right, precision=HIGH, preferred_element_type=jnp.float32)

def adapter_result(input_rows, weight_matrix, adapter_inmap, adapter_outmap, select_adapter):
    frozen_product = matrix_product(input_rows, weight_matrix)
    return frozen_product + ADAPTER_FACTOR * matrix_product(matrix_product(input_rows, adapter_inmap) * select_adapter, adapter_outmap)

def norm_scale(values):
    return lax.rsqrt(lax.optimization_barrier(jnp.mean(values * values, axis=-1, keepdims=True)) + EPSILON)

def head_norm(values, gain):
    return values * norm_scale(values) * gain

def rotate(values, positions):
    half = HEAD_SIZE // 2
    freqs = THETA ** (-2.0 * jnp.arange(half).astype(jnp.float32) / HEAD_SIZE)
    angle = positions[:, None, None] * freqs[None, None, :]
    cosine = jnp.cos(angle)
    sine = jnp.sin(angle)
    first = values[..., :half]
    second = values[..., half:]
    return jnp.concatenate([first * cosine - second * sine, second * cosine + first * sine], axis=-1)

def prefix_tree_layer(tokens, segment, depth, parent, adapter, weight_tuple, adapter_apply):
    attention_norm_gain, feedfwd_norm_gain, query_norm_gain, key_norm_gain, query_matrix, key_matrix, value_matrix, output_matrix, gate_matrix, up_matrix, down_matrix = weight_tuple
    query_adapter_inmaps, query_adapter_outmaps, key_adapter_inmaps, key_adapter_outmaps, value_adapter_inmaps, value_adapter_outmaps, output_adapter_inmaps, output_adapter_outmaps, gate_adapter_inmaps, gate_adapter_outmaps, up_adapter_inmaps, up_adapter_outmaps, down_adapter_inmaps, down_adapter_outmaps = adapter_apply
    select_adapter = (jnp.arange(ADAPTER_RANK * NADAPT) // ADAPTER_RANK == adapter).astype(jnp.float32)
    length = tokens.shape[0]
    positions = depth.astype(jnp.float32)
    first_up = parent[segment]
    second_up = parent[first_up]
    hidden_state = low(tokens * norm_scale(tokens) * attention_norm_gain)
    query_before_norm = reduced_gradient(adapter_result(hidden_state, query_matrix, query_adapter_inmaps, query_adapter_outmaps, select_adapter))
    key_before_norm = reduced_gradient(adapter_result(hidden_state, key_matrix, key_adapter_inmaps, key_adapter_outmaps, select_adapter))
    value_projected = reduced_gradient(adapter_result(hidden_state, value_matrix, value_adapter_inmaps, value_adapter_outmaps, select_adapter))
    queries = low(rotate(head_norm(query_before_norm.reshape(length, QUERY_HEADS, HEAD_SIZE), query_norm_gain), positions))
    keys = low(rotate(head_norm(key_before_norm.reshape(length, KEY_VALUE_HEADS, HEAD_SIZE), key_norm_gain), positions))
    values = low(value_projected.reshape(length, KEY_VALUE_HEADS, HEAD_SIZE))
    keys_all = jnp.repeat(keys, QUERY_HEADS // KEY_VALUE_HEADS, axis=1)
    values_all = jnp.repeat(values, QUERY_HEADS // KEY_VALUE_HEADS, axis=1)
    block = math.gcd(TREE_LEN, 1024)
    count = TREE_LEN // block

    def attend(items):
        query_block, seg_block, first_block, second_block, depth_block = items
        scores = jnp.einsum('qhd,khd->hqk', query_block, keys_all, precision=HIGH, preferred_element_type=jnp.float32)
        scores = reduced_gradient(scores * HEAD_SIZE ** (-0.5))
        visible = ((segment[None, :] == seg_block[:, None]) | (segment[None, :] == first_block[:, None]) | (segment[None, :] == second_block[:, None])) & (depth[None, :] <= depth_block[:, None])
        probs = jax.nn.softmax(jnp.where(visible[None], scores, NEGATIVE), axis=-1)
        return jnp.einsum('hqk,khd->qhd', low(probs), values_all, precision=HIGH, preferred_element_type=jnp.float32)
    mixed = lax.map(jax.checkpoint(attend), (queries.reshape(count, block, QUERY_HEADS, HEAD_SIZE), segment.reshape(count, block), first_up.reshape(count, block), second_up.reshape(count, block), depth.reshape(count, block)))
    attention_output = reduced_gradient(low(mixed.reshape(length, QUERY_HEADS * HEAD_SIZE)))
    branch_index = reduced_gradient(adapter_result(attention_output, output_matrix, output_adapter_inmaps, output_adapter_outmaps, select_adapter))
    middle_values = tokens + branch_index
    feedfwd_hidden_state = low(middle_values * norm_scale(middle_values) * feedfwd_norm_gain)
    gate_values = reduced_gradient(adapter_result(feedfwd_hidden_state, gate_matrix, gate_adapter_inmaps, gate_adapter_outmaps, select_adapter))
    upward_pass = reduced_gradient(adapter_result(feedfwd_hidden_state, up_matrix, up_adapter_inmaps, up_adapter_outmaps, select_adapter))
    swish_output = low(jax.nn.silu(gate_values) * upward_pass)
    return middle_values + reduced_gradient(adapter_result(swish_output, down_matrix, down_adapter_inmaps, down_adapter_outmaps, select_adapter))

def reference(tokens, cotangent, attention_norm_gain, feedfwd_norm_gain, query_norm_gain, key_norm_gain, query_matrix, key_matrix, value_matrix, output_matrix, gate_matrix, up_matrix, down_matrix, query_adapter_inmaps, query_adapter_outmaps, key_adapter_inmaps, key_adapter_outmaps, value_adapter_inmaps, value_adapter_outmaps, output_adapter_inmaps, output_adapter_outmaps, gate_adapter_inmaps, gate_adapter_outmaps, up_adapter_inmaps, up_adapter_outmaps, down_adapter_inmaps, down_adapter_outmaps, segment, depth, parent, adapter):
    weight_tuple = tuple((make_array.astype(jnp.float32) for make_array in (attention_norm_gain, feedfwd_norm_gain, query_norm_gain, key_norm_gain, query_matrix, key_matrix, value_matrix, output_matrix, gate_matrix, up_matrix, down_matrix)))
    adapter_apply = tuple((make_array.astype(jnp.float32) for make_array in (query_adapter_inmaps, query_adapter_outmaps, key_adapter_inmaps, key_adapter_outmaps, value_adapter_inmaps, value_adapter_outmaps, output_adapter_inmaps, output_adapter_outmaps, gate_adapter_inmaps, gate_adapter_outmaps, up_adapter_inmaps, up_adapter_outmaps, down_adapter_inmaps, down_adapter_outmaps)))

    def layer_forward(input_rows, adapters):

        def step(carry, items):
            tree_tokens, tree_segment, tree_depth, tree_parent, tree_adapter = items
            return (carry, jax.checkpoint(prefix_tree_layer)(tree_tokens, tree_segment, tree_depth, tree_parent, tree_adapter, weight_tuple, adapters))
        carry_zero = jnp.zeros((), jnp.float32)
        final, outputs = lax.scan(step, carry_zero, (input_rows.reshape(TREES, TREE_LEN, MODEL_WIDTH), segment.reshape(TREES, TREE_LEN), depth.reshape(TREES, TREE_LEN), parent, adapter))
        return outputs.reshape(TREES * TREE_LEN, MODEL_WIDTH)
    final_result, reverse_function = jax.vjp(layer_forward, tokens.astype(jnp.float32), adapter_apply)
    input_gradient, adapter_gradient = reverse_function(cotangent.astype(jnp.float32))
    return (final_result.astype(jnp.bfloat16), input_gradient, adapter_gradient[0], adapter_gradient[1], adapter_gradient[2], adapter_gradient[3], adapter_gradient[4], adapter_gradient[5], adapter_gradient[6], adapter_gradient[7], adapter_gradient[8], adapter_gradient[9], adapter_gradient[10], adapter_gradient[11], adapter_gradient[12], adapter_gradient[13])
```

```python
import functools
import math

import jax
import jax.numpy as jnp
from jax import lax
from jax.experimental import pallas as pl
from jax.experimental.pallas import tpu as pltpu
from jax.sharding import PartitionSpec as P

MODEL_WIDTH = 2048
QUERY_HEADS = 16
KEY_VALUE_HEADS = 8
HEAD_SIZE = 128
ADAPTER_RANK = 16
TREE_LEN = 5120
TRUNK = 2048
SEG_LEN = 256
FFN_CHUNKS = 3

EPSILON = 1e-06
THETA = 1000000.0
ADAPTER_FACTOR = 2.0
BF = jnp.bfloat16
F32 = jnp.float32
SCALE = HEAD_SIZE ** (-0.5)
SCALE_LOG2 = SCALE * math.log2(math.e)
PLANE = ("col", "row")
LANES = 128
VMEM_LIMIT = 60 * 1024 * 1024


def dot(left, right):
    return jnp.dot(left, right, preferred_element_type=F32)


def dot_nt(left, right):
    return lax.dot_general(left, right, (((1,), (1,)), ((), ())), preferred_element_type=F32)


def dot_tn(left, right):
    return lax.dot_general(left, right, (((0,), (0,)), ((), ())), preferred_element_type=F32)


def attention_forward_kernel(parent_ref, q_ref, k_ref, v_ref, o_ref, l_ref, acc_ref):
    index = pl.program_id(0)
    trunk_blocks = TRUNK // SEG_LEN
    query = q_ref[...]
    acc_ref[...] = jnp.zeros_like(acc_ref)

    def step(start, size, causal=False):
        rows = pl.ds(start, size)
        scores = dot_nt(query, k_ref[rows, :])
        probs = jnp.exp2(scores * SCALE_LOG2)
        if causal:
            ahead = lax.broadcasted_iota(jnp.int32, probs.shape, 0)
            behind = lax.broadcasted_iota(jnp.int32, probs.shape, 1)
            probs = jnp.where(behind <= ahead, probs, 0.0)
        acc_ref[...] += dot(probs.astype(BF), v_ref[rows, :])

    @pl.when(index < trunk_blocks)
    def _():
        @pl.loop(0, index)
        def _(block):
            step(pl.multiple_of(block * SEG_LEN, SEG_LEN), SEG_LEN)

    @pl.when(index >= trunk_blocks)
    def _():
        size = 512
        for part in range(TRUNK // size):
            step(part * size, size)

        above = parent_ref[index]

        @pl.when(above >= 0)
        def _():
            step(pl.multiple_of(above * SEG_LEN, SEG_LEN), SEG_LEN)

    step(pl.multiple_of(index * SEG_LEN, SEG_LEN), SEG_LEN, True)
    total = acc_ref[:, HEAD_SIZE : HEAD_SIZE + 1]
    o_ref[...] = acc_ref[:, :HEAD_SIZE] / total
    spread = jnp.broadcast_to(total, (SEG_LEN, LANES))
    l_ref[0] = jnp.transpose(spread)[:8, :]


def attention_forward(parent_block, query, key, value):
    length = query.shape[0]
    blocks = length // SEG_LEN
    ones = (jnp.arange(HEAD_SIZE) == 0).astype(BF)
    widened = jnp.concatenate([value, jnp.broadcast_to(ones, value.shape)], axis=1)
    whole = lambda i, p: (0, 0)
    return pl.pallas_call(
        attention_forward_kernel,
        grid_spec=pltpu.PrefetchScalarGridSpec(
            num_scalar_prefetch=1,
            grid=(blocks,),
            in_specs=[
                pl.BlockSpec((SEG_LEN, HEAD_SIZE), lambda i, p: (i, 0)),
                pl.BlockSpec((length, HEAD_SIZE), whole),
                pl.BlockSpec((length, 2 * HEAD_SIZE), whole),
            ],
            out_specs=[
                pl.BlockSpec((SEG_LEN, HEAD_SIZE), lambda i, p: (i, 0)),
                pl.BlockSpec((1, 8, SEG_LEN), lambda i, p: (i, 0, 0)),
            ],
            scratch_shapes=[pltpu.VMEM((SEG_LEN, 2 * HEAD_SIZE), F32)],
        ),
        out_shape=[
            jax.ShapeDtypeStruct((length, HEAD_SIZE), F32),
            jax.ShapeDtypeStruct((blocks, 8, SEG_LEN), F32),
        ],
        compiler_params=pltpu.CompilerParams(vmem_limit_bytes=VMEM_LIMIT),
        cost_estimate=pl.CostEstimate(
            flops=160 * SEG_LEN * SEG_LEN * HEAD_SIZE * 4,
            bytes_accessed=length * HEAD_SIZE * 12,
            transcendentals=160 * SEG_LEN * SEG_LEN,
        ),
        name="attention_forward",
    )(parent_block, query, key, widened)


def attention_backward_kernel(
    parent_ref, q_ref, g_ref, o_ref, l_ref, k_ref, v_ref, kt_ref, dq_ref, dk_ref, dv_ref, acc_ref
):
    index = pl.program_id(0)
    trunk_blocks = TRUNK // SEG_LEN

    @pl.when(index == 0)
    def _():
        dk_ref[...] = jnp.zeros_like(dk_ref)
        dv_ref[...] = jnp.zeros_like(dv_ref)

    query = q_ref[...]
    grad = g_ref[...]
    delta = jnp.sum(grad.astype(F32) * o_ref[...], axis=1, keepdims=True)
    delta = jnp.transpose(jnp.broadcast_to(delta, (SEG_LEN, LANES)))[:1, :]
    inverse = 1.0 / l_ref[0, :1, :]
    acc_ref[...] = jnp.zeros_like(acc_ref)

    def step(start, size, causal=False):
        rows = pl.ds(start, size)
        probs = jnp.exp2(dot_nt(k_ref[rows, :], query) * SCALE_LOG2) * inverse
        if causal:
            behind = lax.broadcasted_iota(jnp.int32, probs.shape, 0)
            ahead = lax.broadcasted_iota(jnp.int32, probs.shape, 1)
            probs = jnp.where(behind <= ahead, probs, 0.0)
        dprobs = dot_nt(v_ref[rows, :], grad)
        dscores = (probs * (dprobs - delta)).astype(BF)
        dv_ref[rows, :] += dot(probs.astype(BF), grad)
        dk_ref[rows, :] += dot(dscores, query)
        acc_ref[...] += dot(kt_ref[:, rows], dscores)

    @pl.when(index < trunk_blocks)
    def _():
        @pl.loop(0, index)
        def _(block):
            step(pl.multiple_of(block * SEG_LEN, SEG_LEN), SEG_LEN)

    @pl.when(index >= trunk_blocks)
    def _():
        size = 512
        for part in range(TRUNK // size):
            step(part * size, size)

        above = parent_ref[index]

        @pl.when(above >= 0)
        def _():
            step(pl.multiple_of(above * SEG_LEN, SEG_LEN), SEG_LEN)

    step(pl.multiple_of(index * SEG_LEN, SEG_LEN), SEG_LEN, True)
    dq_ref[...] = jnp.transpose(acc_ref[...]) * SCALE


def attention_backward(parent_block, query, grad, attended, totals, key, value):
    length = query.shape[0]
    blocks = length // SEG_LEN
    whole = lambda i, p: (0, 0)
    part = lambda i, p: (i, 0)
    return pl.pallas_call(
        attention_backward_kernel,
        grid_spec=pltpu.PrefetchScalarGridSpec(
            num_scalar_prefetch=1,
            grid=(blocks,),
            in_specs=[
                pl.BlockSpec((SEG_LEN, HEAD_SIZE), part),
                pl.BlockSpec((SEG_LEN, HEAD_SIZE), part),
                pl.BlockSpec((SEG_LEN, HEAD_SIZE), part),
                pl.BlockSpec((1, 8, SEG_LEN), lambda i, p: (i, 0, 0)),
                pl.BlockSpec((length, HEAD_SIZE), whole),
                pl.BlockSpec((length, HEAD_SIZE), whole),
                pl.BlockSpec((HEAD_SIZE, length), whole),
            ],
            out_specs=[
                pl.BlockSpec((SEG_LEN, HEAD_SIZE), part),
                pl.BlockSpec((length, HEAD_SIZE), whole),
                pl.BlockSpec((length, HEAD_SIZE), whole),
            ],
            scratch_shapes=[pltpu.VMEM((HEAD_SIZE, SEG_LEN), F32)],
        ),
        out_shape=[jax.ShapeDtypeStruct((length, HEAD_SIZE), F32)] * 3,
        compiler_params=pltpu.CompilerParams(vmem_limit_bytes=VMEM_LIMIT),
        cost_estimate=pl.CostEstimate(
            flops=160 * SEG_LEN * SEG_LEN * HEAD_SIZE * 10,
            bytes_accessed=length * HEAD_SIZE * 24,
            transcendentals=160 * SEG_LEN * SEG_LEN,
        ),
        name="attention_backward",
    )(parent_block, query, grad, attended, totals, key, value, jnp.transpose(key))


def feed_forward_kernel(
    first,
    h_ref,
    c_ref,
    mg_ref,
    mu_ref,
    nd_ref,
    mgt_ref,
    mut_ref,
    ndt_ref,
    w_ref,
    bg_ref,
    bu_ref,
    ad_ref,
    *refs,
):
    if first:
        previous = None
        outs = refs
    else:
        previous = refs[:5]
        outs = refs[5:]
    accs = outs[:5]
    pa_ref, pg_ref, pu_ref = outs[5:8]
    out_acc, gh_acc, md_acc, ig_acc, iu_acc = scratch = outs[8:13]
    sems = outs[13]
    index = pl.program_id(0)
    width = w_ref.shape[-1]
    row_blocks = w_ref.shape[1]
    depth = MODEL_WIDTH // row_blocks
    pieces = depth // width

    @pl.when(index == 0)
    def _():
        if first:
            for ref in scratch:
                ref[...] = jnp.zeros_like(ref)
        else:
            copies = [
                pltpu.make_async_copy(previous[i], scratch[i], sems.at[i]) for i in range(5)
            ]
            for copy in copies:
                copy.start()
            for copy in copies:
                copy.wait()

    gate = dot_nt(mg_ref[...], bg_ref[0])
    upward = dot_nt(mu_ref[...], bu_ref[0])
    grad_act = dot_nt(nd_ref[...], ad_ref[0])
    for row in range(row_blocks):
        block = h_ref[:, row * depth : (row + 1) * depth]
        gate += dot(block, w_ref[0, row, :depth, :])
        upward += dot(block, w_ref[0, row, depth : 2 * depth, :])
        for piece in range(pieces):
            at = row * depth + piece * width
            down = w_ref[0, row, 2 * depth + piece * width : 2 * depth + (piece + 1) * width, :]
            grad_act += dot_nt(c_ref[:, at : at + width], down)
    sigma = 1.0 / (1.0 + jnp.exp(-gate))
    swish = gate * sigma
    act = (swish * upward).astype(BF)
    grad_gate = (grad_act * upward * (sigma * (1.0 + gate * (1.0 - sigma)))).astype(BF)
    grad_up = (grad_act * swish).astype(BF)
    for row in range(row_blocks):
        gh_acc[:, row * depth : (row + 1) * depth] += dot_nt(
            grad_gate, w_ref[0, row, :depth, :]
        ) + dot_nt(grad_up, w_ref[0, row, depth : 2 * depth, :])
        for piece in range(pieces):
            at = row * depth + piece * width
            down = w_ref[0, row, 2 * depth + piece * width : 2 * depth + (piece + 1) * width, :]
            out_acc[:, at : at + width] += dot(act, down)
    md_acc[...] += dot(act, ad_ref[0])
    ig_acc[...] += dot(grad_gate, bg_ref[0])
    iu_acc[...] += dot(grad_up, bu_ref[0])
    pa_ref[0] = dot(ndt_ref[...], act)
    pg_ref[0] = dot(mgt_ref[...], grad_gate)
    pu_ref[0] = dot(mut_ref[...], grad_up)

    @pl.when(index == pl.num_programs(0) - 1)
    def _():
        copies = [pltpu.make_async_copy(scratch[i], accs[i], sems.at[i]) for i in range(5)]
        for copy in copies:
            copy.start()
        for copy in copies:
            copy.wait()


def feed_forward_chunk(hidden, cotangent, masks, weights, maps, previous):
    first = previous is None
    rows = hidden.shape[0]
    cols, row_blocks, tall, width = weights.shape
    whole = lambda i: (0, 0)
    step = lambda i: (i, 0, 0)
    mask_rows = masks[3].shape[0]
    acc_shapes = [(rows, MODEL_WIDTH)] * 2 + [(rows, LANES)] * 3
    in_specs = (
        [pl.BlockSpec((rows, MODEL_WIDTH), whole)] * 2
        + [pl.BlockSpec((rows, LANES), whole)] * 3
        + [pl.BlockSpec((mask_rows, rows), whole)] * 3
        + [pl.BlockSpec((1, row_blocks, tall, width), lambda i: (i, 0, 0, 0))]
        + [pl.BlockSpec((1, width, LANES), step)] * 3
    )
    operands = [hidden, cotangent, *masks, weights, *maps]
    aliases = {}
    if not first:
        aliases = {len(operands) + i: i for i in range(5)}
        in_specs = in_specs + [pl.BlockSpec(memory_space=pl.ANY)] * 5
        operands = operands + list(previous)
    outs = pl.pallas_call(
        functools.partial(feed_forward_kernel, first),
        grid=(cols,),
        in_specs=in_specs,
        out_specs=[pl.BlockSpec(memory_space=pl.ANY)] * 5
        + [pl.BlockSpec((1, mask_rows, width), step)] * 3,
        out_shape=[jax.ShapeDtypeStruct(s, F32) for s in acc_shapes]
        + [jax.ShapeDtypeStruct((cols, mask_rows, width), F32)] * 3,
        scratch_shapes=[pltpu.VMEM(s, F32) for s in acc_shapes]
        + [pltpu.SemaphoreType.DMA((5,))],
        input_output_aliases=aliases,
        compiler_params=pltpu.CompilerParams(vmem_limit_bytes=VMEM_LIMIT),
        cost_estimate=pl.CostEstimate(
            flops=12 * rows * MODEL_WIDTH * cols * width,
            bytes_accessed=cols * row_blocks * tall * width * 2,
            transcendentals=rows * cols * width,
        ),
        name="feed_forward",
    )(*operands)
    return outs[:5], outs[5:]


def rotate(values, positions):
    half = HEAD_SIZE // 2
    freqs = THETA ** (-2.0 * jnp.arange(half).astype(F32) / HEAD_SIZE)
    angle = positions[:, None, None] * freqs[None, None, :]
    cosine = jnp.cos(angle)
    sine = jnp.sin(angle)
    first = values[..., :half]
    second = values[..., half:]
    return jnp.concatenate(
        [first * cosine - second * sine, second * cosine + first * sine], axis=-1
    )


def head_shape(gain, positions):
    def shaped(lines):
        normed = lines * lax.rsqrt(jnp.mean(lines * lines, axis=-1, keepdims=True) + EPSILON) * gain
        return rotate(normed, positions)

    return shaped


def norm_back(values, scale, gain, gradient):
    weighted = gain * gradient
    inner_sum = jnp.sum(weighted * values, axis=1, keepdims=True)
    return scale * weighted - values * scale**3 * inner_sum / MODEL_WIDTH


def lane_pad(values):
    return jnp.pad(values, ((0, 0),) * (values.ndim - 1) + ((0, LANES - values.shape[-1]),))


def place(own, own_at, other, other_at, columns):
    index = jnp.arange(columns)[None, :] // ADAPTER_RANK
    copies = columns // ADAPTER_RANK
    return jnp.where(index == own_at, jnp.tile(own, (1, copies)), 0.0) + jnp.where(
        index == other_at, jnp.tile(other, (1, copies)), 0.0
    )


def on_device(
    tokens,
    cotangent,
    attention_norm_gain,
    feedfwd_norm_gain,
    query_norm_gain,
    key_norm_gain,
    query_matrix,
    key_matrix,
    value_matrix,
    output_matrix,
    gate_matrix,
    up_matrix,
    down_matrix,
    query_adapter_inmaps,
    query_adapter_outmaps,
    key_adapter_inmaps,
    key_adapter_outmaps,
    value_adapter_inmaps,
    value_adapter_outmaps,
    output_adapter_inmaps,
    output_adapter_outmaps,
    gate_adapter_inmaps,
    gate_adapter_outmaps,
    up_adapter_inmaps,
    up_adapter_outmaps,
    down_adapter_inmaps,
    down_adapter_outmaps,
    segment,
    depth,
    parent,
    adapter,
):
    rows = lax.axis_size("row")
    cols = lax.axis_size("col")
    devices = rows * cols
    repeat = devices // QUERY_HEADS
    plane = lax.axis_index("dp")
    row = lax.axis_index("row")
    col = lax.axis_index("col")
    length = segment.shape[0]
    own = tokens.shape[0] // rows
    columns = query_adapter_inmaps.shape[1]
    rank = ADAPTER_RANK
    swap = [(0, 1), (1, 0)]
    pairs = [(r, r ^ repeat) for r in range(rows)]

    own_adapter = adapter[0]
    other_adapter = lax.ppermute(adapter, "dp", swap)[0]

    def inmap(table, at):
        return lax.dynamic_slice_in_dim(table, at * rank, rank, 1)

    def outmap(table, at):
        return jnp.transpose(lax.dynamic_slice_in_dim(table, at * rank, rank, 0))

    both = (own_adapter, other_adapter)
    ffn_half = gate_matrix.shape[1] // 2
    half_start = plane * ffn_half

    def half_of(table):
        return lax.dynamic_slice_in_dim(table, half_start, ffn_half, 0)

    row_pack = jnp.concatenate(
        [
            inmap(query_adapter_inmaps, own_adapter),
            inmap(key_adapter_inmaps, own_adapter),
            inmap(value_adapter_inmaps, own_adapter),
            *[inmap(gate_adapter_inmaps, a) for a in both],
            *[inmap(up_adapter_inmaps, a) for a in both],
            *[outmap(down_adapter_outmaps, a) for a in both],
            outmap(output_adapter_outmaps, own_adapter),
        ],
        axis=1,
    )
    col_attn = jnp.concatenate(
        [
            inmap(output_adapter_inmaps, own_adapter),
            outmap(query_adapter_outmaps, own_adapter),
            jnp.concatenate(
                [
                    outmap(key_adapter_outmaps, own_adapter),
                    outmap(value_adapter_outmaps, own_adapter),
                ],
                axis=0,
            ),
        ],
        axis=1,
    )
    col_ffn = half_of(
        jnp.concatenate(
            [
                *[inmap(down_adapter_inmaps, a) for a in both],
                *[outmap(gate_adapter_outmaps, a) for a in both],
                *[outmap(up_adapter_outmaps, a) for a in both],
            ],
            axis=1,
        )
    )
    attn_rows = col_attn.shape[0]
    col_pack = jnp.concatenate(
        [jnp.pad(col_attn, ((0, 0), (0, col_ffn.shape[1] - col_attn.shape[1]))), col_ffn], axis=0
    )
    row_maps = lax.all_gather(row_pack, "row", axis=0, tiled=True)
    col_maps = lax.all_gather(col_pack, "col", axis=0, tiled=False)
    in_qkv = row_maps[:, : 3 * rank]
    in_gu = row_maps[:, 3 * rank : 7 * rank]
    out_down = row_maps[:, 7 * rank : 9 * rank]
    out_o = row_maps[:, 9 * rank : 10 * rank]
    col_attn = col_maps[:, :attn_rows]
    col_ffn = col_maps[:, attn_rows:]
    in_o = col_attn[:, :, :rank].reshape(-1, rank)
    out_q = col_attn[:, :, rank : 2 * rank].reshape(-1, rank)
    kv_local = key_matrix.shape[1]
    out_k = col_attn[:, :kv_local, 2 * rank : 3 * rank].reshape(-1, rank)
    out_v = col_attn[:, kv_local:, 2 * rank : 3 * rank].reshape(-1, rank)

    qkv_local = jnp.concatenate([query_matrix, key_matrix, value_matrix], axis=1)
    weights_qkv = lax.all_gather(qkv_local, PLANE, axis=0, tiled=True).reshape(
        cols, MODEL_WIDTH, -1
    )
    weights_o = lax.all_gather(output_matrix, ("row", "col"), axis=0, tiled=True).reshape(
        rows, QUERY_HEADS * HEAD_SIZE, -1
    )
    q_local = query_matrix.shape[1]
    width = ffn_half // FFN_CHUNKS
    depth_rows = gate_matrix.shape[0]
    ffn_weights = []
    for chunk in range(FFN_CHUNKS):
        start = half_start + chunk * width
        down = lax.dynamic_slice_in_dim(down_matrix, start, width, 0)
        pack = jnp.concatenate(
            [
                lax.dynamic_slice_in_dim(gate_matrix, start, width, 1),
                lax.dynamic_slice_in_dim(up_matrix, start, width, 1),
                *[
                    down[:, piece * width : (piece + 1) * width]
                    for piece in range(depth_rows // width)
                ],
            ],
            axis=0,
        )
        ffn_weights.append(
            lax.all_gather(pack, PLANE, axis=0, tiled=True).reshape(cols, rows, -1, width)
        )

    own_tokens = lax.all_to_all(tokens, "row", 0, 1, tiled=True)
    own_cotangent = lax.all_to_all(cotangent, "row", 0, 1, tiled=True)
    other_cotangent = lax.ppermute(own_cotangent, "dp", swap)
    gain_pair = lax.all_gather(
        jnp.stack([attention_norm_gain, feedfwd_norm_gain], axis=1), "row", axis=0, tiled=True
    )
    gain_one = gain_pair[:, 0]
    gain_two = gain_pair[:, 1]
    resid = own_tokens.astype(F32)
    scale_one = lax.rsqrt(jnp.mean(resid * resid, axis=1, keepdims=True) + EPSILON)
    hidden = (resid * scale_one * gain_one).astype(BF)

    masked_qkv = dot(hidden, in_qkv).astype(BF)
    projected = [dot(hidden, weights_qkv[c]) for c in range(cols)]
    query_pre = jnp.concatenate([p[:, :q_local] for p in projected], axis=1)
    key_pre = jnp.concatenate([p[:, q_local : q_local + kv_local] for p in projected], axis=1)
    value_pre = jnp.concatenate([p[:, q_local + kv_local :] for p in projected], axis=1)
    query_pre = query_pre + ADAPTER_FACTOR * dot_nt(masked_qkv[:, :rank], out_q)
    key_pre = key_pre + ADAPTER_FACTOR * dot_nt(masked_qkv[:, rank : 2 * rank], out_k)
    value_pre = value_pre + ADAPTER_FACTOR * dot_nt(masked_qkv[:, 2 * rank :], out_v)
    token_start = (col * rows + row) * own
    positions = lax.dynamic_slice_in_dim(depth, token_start, own, 0).astype(F32)
    query, query_back = jax.vjp(
        head_shape(query_norm_gain, positions), query_pre.reshape(own, QUERY_HEADS, HEAD_SIZE)
    )
    key, key_back = jax.vjp(
        head_shape(key_norm_gain, positions), key_pre.reshape(own, KEY_VALUE_HEADS, HEAD_SIZE)
    )
    value = value_pre.reshape(own, KEY_VALUE_HEADS, HEAD_SIZE)
    key_value = jnp.stack([key.astype(BF), value.astype(BF)], axis=2).reshape(
        own, QUERY_HEADS, HEAD_SIZE
    )

    def to_heads(lines):
        sent = jnp.transpose(lines, (1, 0, 2))
        if repeat > 1:
            sent = jnp.repeat(sent, repeat, axis=0)
        return lax.all_to_all(sent, PLANE, 0, 0, tiled=True).reshape(length, lines.shape[2])

    def to_tokens(lines):
        got = lax.all_to_all(
            lines.reshape(devices, own, lines.shape[1]), PLANE, 0, 0, tiled=True
        )
        if repeat > 1:
            got = got[::repeat]
        return jnp.transpose(got, (1, 0, 2))

    got = to_heads(jnp.concatenate([query.astype(BF), key_value], axis=2))
    head_query = got[:, :HEAD_SIZE]
    mine = got[:, HEAD_SIZE:]
    theirs = lax.ppermute(mine, "row", pairs)
    has_key = (row // repeat) % 2 == 0
    head_key = jnp.where(has_key, mine, theirs)
    head_value = jnp.where(has_key, theirs, mine)

    block_node = segment.reshape(-1, SEG_LEN)[:, 0]
    nodes = jnp.arange(parent.shape[1])
    node_parent = jnp.sum(jnp.where(block_node[:, None] == nodes, parent.reshape(1, -1), 0), axis=1)
    block_index = jnp.arange(block_node.shape[0])
    parent_block = jnp.max(
        jnp.where(node_parent[:, None] == block_node[None, :], block_index[None, :], 0), axis=1
    )
    parent_block = jnp.where(node_parent > 0, parent_block, -1).astype(jnp.int32)
    head_attended, totals = attention_forward(parent_block, head_query, head_key, head_value)
    attended = to_tokens(head_attended.astype(BF)).reshape(own, -1)

    masked_o = dot(attended, in_o).astype(BF)
    branch = jnp.concatenate([dot(attended, weights_o[r]) for r in range(rows)], axis=1)
    middle = resid + branch + ADAPTER_FACTOR * dot_nt(masked_o, out_o)
    scale_two = lax.rsqrt(jnp.mean(middle * middle, axis=1, keepdims=True) + EPSILON)
    hidden_ffn = (middle * scale_two * gain_two).astype(BF)

    other_ffn = lax.ppermute(hidden_ffn, "dp", swap)
    hidden_both = jnp.concatenate([hidden_ffn, other_ffn], axis=0)
    cot_both = jnp.concatenate([own_cotangent, other_cotangent], axis=0)
    tree_mask = (
        jnp.arange(2 * own)[:, None] // own == (jnp.arange(2 * rank)[None, :] // rank)
    ).astype(F32)
    masked_gu = dot(hidden_both, in_gu) * jnp.tile(tree_mask, (1, 2))
    masked_g = masked_gu[:, : 2 * rank].astype(BF)
    masked_u = masked_gu[:, 2 * rank :].astype(BF)
    inner_d = (ADAPTER_FACTOR * dot(cot_both, out_down) * tree_mask).astype(BF)
    masks = [
        lane_pad((ADAPTER_FACTOR * masked_g.astype(F32)).astype(BF)),
        lane_pad((ADAPTER_FACTOR * masked_u.astype(F32)).astype(BF)),
        lane_pad(inner_d),
        jnp.transpose(masked_g),
        jnp.transpose(masked_u),
        jnp.transpose(inner_d),
    ]
    accs = None
    parts = []
    for chunk in range(FFN_CHUNKS):
        maps = [
            lane_pad(
                col_ffn[
                    :, chunk * width : (chunk + 1) * width, 2 * rank * kind : 2 * rank * (kind + 1)
                ]
            )
            for kind in (1, 2, 0)
        ]
        accs, part = feed_forward_chunk(
            hidden_both, cot_both, masks, ffn_weights[chunk], maps, accs
        )
        parts.append(part)
    out_acc, gh_acc, md_acc, ig_acc, iu_acc = accs
    masked_down = (md_acc[:, : 2 * rank] * tree_mask).astype(BF)
    inner_gu = (
        ADAPTER_FACTOR
        * jnp.concatenate([ig_acc[:, : 2 * rank], iu_acc[:, : 2 * rank]], axis=1)
        * jnp.tile(tree_mask, (1, 2))
    ).astype(BF)
    gh_acc = gh_acc + dot_nt(inner_gu, in_gu)
    out_acc = out_acc + ADAPTER_FACTOR * dot_nt(masked_down, out_down)
    gh_other = lax.ppermute(gh_acc[own:].astype(BF), "dp", swap)
    out_other = lax.ppermute(out_acc[own:].astype(BF), "dp", swap)
    output = (middle + out_acc[:own] + out_other.astype(F32)).astype(BF)
    output = lax.all_to_all(output, "row", 1, 0, tiled=True)
    grad_hidden_ffn = gh_acc[:own] + gh_other.astype(F32)
    grad_middle = own_cotangent.astype(F32) + norm_back(middle, scale_two, gain_two, grad_hidden_ffn)
    grad_middle_low = grad_middle.astype(BF)

    inner_o = (ADAPTER_FACTOR * dot(grad_middle_low, out_o)).astype(BF)
    o_local = weights_o.shape[2]
    grad_attended = dot_nt(inner_o, in_o)
    for r in range(rows):
        grad_attended = grad_attended + dot_nt(
            grad_middle_low[:, r * o_local : (r + 1) * o_local], weights_o[r]
        )
    grad_low = grad_attended.astype(BF).reshape(own, QUERY_HEADS, HEAD_SIZE)
    head_grad = to_heads(grad_low)

    dq, dk, dv = attention_backward(
        parent_block, head_query, head_grad, head_attended, totals, head_key, head_value
    )
    dk = dk * SCALE
    kept = jnp.where(has_key, dk, dv)
    given = jnp.where(has_key, dv, dk)
    kept = kept + lax.ppermute(given, "row", pairs)
    returned = to_tokens(jnp.concatenate([dq.astype(BF), kept.astype(BF)], axis=1))
    grad_kv = returned[:, :, HEAD_SIZE:].reshape(own, KEY_VALUE_HEADS, 2, HEAD_SIZE)
    grad_q = query_back(returned[:, :, :HEAD_SIZE].astype(F32))[0].astype(BF).reshape(own, -1)
    grad_k = key_back(grad_kv[:, :, 0].astype(F32))[0].astype(BF).reshape(own, -1)
    grad_v = grad_kv[:, :, 1].reshape(own, -1)

    inner_qkv = (
        ADAPTER_FACTOR
        * jnp.concatenate([dot(grad_q, out_q), dot(grad_k, out_k), dot(grad_v, out_v)], axis=1)
    ).astype(BF)
    grad_hidden = dot_nt(inner_qkv, in_qkv)
    for c in range(cols):
        grad_c = jnp.concatenate(
            [
                grad_q[:, c * q_local : (c + 1) * q_local],
                grad_k[:, c * kv_local : (c + 1) * kv_local],
                grad_v[:, c * kv_local : (c + 1) * kv_local],
            ],
            axis=1,
        )
        grad_hidden = grad_hidden + dot_nt(grad_c, weights_qkv[c])
    input_gradient = grad_middle + norm_back(resid, scale_one, gain_one, grad_hidden)
    input_gradient = lax.all_to_all(input_gradient.astype(BF), "row", 1, 0, tiled=True).astype(F32)

    def over_rows(values):
        mine = lax.psum_scatter(values, "row", scatter_dimension=0, tiled=True)
        return lax.psum(mine, "col")

    def over_cols(values):
        mine = lax.psum_scatter(values, "col", scatter_dimension=0, tiled=True)
        return lax.psum(mine, "row")

    f = ADAPTER_FACTOR
    row_mid = over_rows(
        jnp.concatenate(
            [
                dot_tn(hidden_both, inner_gu),
                f * dot_tn(cot_both, masked_down),
                f * dot_tn(grad_middle_low, masked_o),
            ],
            axis=1,
        )
    )
    ffn_parts = jnp.concatenate(
        [jnp.concatenate([part[kind] for part in parts], axis=2) for kind in range(3)], axis=1
    )
    o_parts = dot_tn(attended, inner_o).reshape(cols, -1)
    col_mid = over_cols(
        jnp.concatenate([ffn_parts.reshape(cols, -1), o_parts], axis=1)
    ).reshape(-1)
    row_end = over_rows(dot_tn(hidden, inner_qkv))
    end_parts = [
        (f * dot_tn(grad, masked_qkv[:, i * rank : (i + 1) * rank])).reshape(cols, -1)
        for i, grad in enumerate((grad_q, grad_k, grad_v))
    ]
    col_end = over_cols(jnp.concatenate(end_parts, axis=1)).reshape(-1)
    row_all = jnp.concatenate([row_mid, row_end], axis=1)
    row_got = lax.ppermute(row_all, "dp", swap)
    col_all = jnp.concatenate([col_mid, col_end])
    col_got = lax.ppermute(col_all, "dp", swap)

    def placed(first, second):
        return place(first, own_adapter, second, other_adapter, columns)

    def row_sum(at):
        first = row_all[:, at : at + rank] + row_got[:, at + rank : at + 2 * rank]
        second = row_all[:, at + rank : at + 2 * rank] + row_got[:, at : at + rank]
        return placed(first, second)

    def row_own(at):
        return placed(row_all[:, at : at + rank], row_got[:, at : at + rank])

    grad_a_gate = row_sum(0)
    grad_a_up = row_sum(2 * rank)
    grad_b_down = row_sum(4 * rank).T
    grad_b_o = row_own(6 * rank).T
    grad_a_q, grad_a_k, grad_a_v = (row_own((7 + i) * rank) for i in range(3))

    block = 6 * rank * ffn_half
    here = col_all[:block].reshape(3, 2 * rank, ffn_half)
    there = col_got[:block].reshape(3, 2 * rank, ffn_half)
    there = jnp.concatenate([there[:, rank:], there[:, :rank]], axis=1)
    low_half = jnp.where(plane == 0, here, there)
    high_half = jnp.where(plane == 0, there, here)
    ffn_full = jnp.concatenate([low_half, high_half], axis=2)

    def ffn_placed(kind, factor):
        full = factor * ffn_full[kind]
        return placed(full[:rank].T, full[rank:].T)

    grad_a_down = ffn_placed(0, 1.0)
    grad_b_gate = ffn_placed(1, f).T
    grad_b_up = ffn_placed(2, f).T

    def col_own(at, count):
        first = col_all[at : at + count * rank].reshape(count, rank)
        second = col_got[at : at + count * rank].reshape(count, rank)
        return placed(first, second)

    o_rows = output_matrix.shape[0]
    grad_a_o = col_own(block, o_rows)
    block = block + o_rows * rank
    grad_b_q = col_own(block, q_local).T
    block = block + q_local * rank
    grad_b_k = col_own(block, kv_local).T
    block = block + kv_local * rank
    grad_b_v = col_own(block, kv_local).T

    return (
        output,
        input_gradient,
        grad_a_q,
        grad_b_q,
        grad_a_k,
        grad_b_k,
        grad_a_v,
        grad_b_v,
        grad_a_o,
        grad_b_o,
        grad_a_gate,
        grad_b_gate,
        grad_a_up,
        grad_b_up,
        grad_a_down,
        grad_b_down,
    )


def solution(mesh):
    return jax.shard_map(
        on_device,
        mesh=mesh,
        in_specs=(
            P(("dp", "col"), "row"),
            P(("dp", "col"), "row"),
            P("row"),
            P("row"),
            P(),
            P(),
            P("row", "col"),
            P("row", "col"),
            P("row", "col"),
            P("col", "row"),
            P("row", "col"),
            P("row", "col"),
            P("col", "row"),
            P("row", None),
            P(None, "col"),
            P("row", None),
            P(None, "col"),
            P("row", None),
            P(None, "col"),
            P("col", None),
            P(None, "row"),
            P("row", None),
            P(None, "col"),
            P("row", None),
            P(None, "col"),
            P("col", None),
            P(None, "row"),
            P("dp"),
            P("dp"),
            P("dp", None),
            P("dp"),
        ),
        out_specs=(
            P(("dp", "col"), "row"),
            P(("dp", "col"), "row"),
            P("row", None),
            P(None, "col"),
            P("row", None),
            P(None, "col"),
            P("row", None),
            P(None, "col"),
            P("col", None),
            P(None, "row"),
            P("row", None),
            P(None, "col"),
            P("row", None),
            P(None, "col"),
            P("col", None),
            P(None, "row"),
        ),
        check_vma=False,
    )
```

```python
import functools
import math

import jax
import jax.numpy as jnp
from jax import lax
from jax.experimental import pallas as pl
from jax.experimental.pallas import tpu as pltpu
from jax.sharding import PartitionSpec as P

MODEL_WIDTH = 2048
QUERY_HEADS = 16
KEY_VALUE_HEADS = 8
HEAD_SIZE = 128
ADAPTER_RANK = 16
TREE_LEN = 5120
TRUNK = 2048
SEG_LEN = 256

EPSILON = 1e-06
THETA = 1000000.0
ADAPTER_FACTOR = 2.0
BF = jnp.bfloat16
F32 = jnp.float32
SCALE = HEAD_SIZE ** (-0.5)
SCALE_LOG2 = SCALE * math.log2(math.e)
PLANE = ("col", "row")
LANES = 128
VMEM_LIMIT = 63 * 1024 * 1024


def dot(left, right):
    return jnp.dot(left, right, preferred_element_type=F32)


def dot_nt(left, right):
    return lax.dot_general(left, right, (((1,), (1,)), ((), ())), preferred_element_type=F32)


def dot_tn(left, right):
    return lax.dot_general(left, right, (((0,), (0,)), ((), ())), preferred_element_type=F32)


def attention_forward_kernel(
    parent_ref, flag_ref, q_ref, mine_ref, theirs_ref, o_ref, low_ref, l_ref, k_ref, v_ref, acc_ref
):
    index = pl.program_id(0)
    trunk_blocks = TRUNK // SEG_LEN

    @pl.when(index == 0)
    def _():
        lane = lax.broadcasted_iota(jnp.int32, (v_ref.shape[0], HEAD_SIZE), 1)
        v_ref[:, HEAD_SIZE:] = jnp.where(lane == 0, 1.0, 0.0).astype(BF)

        @pl.when(flag_ref[0] == 1)
        def _():
            k_ref[...] = mine_ref[...]
            v_ref[:, :HEAD_SIZE] = theirs_ref[...]

        @pl.when(flag_ref[0] != 1)
        def _():
            k_ref[...] = theirs_ref[...]
            v_ref[:, :HEAD_SIZE] = mine_ref[...]

    query = q_ref[...]
    acc_ref[...] = jnp.zeros_like(acc_ref)

    def step(start, size, causal=False):
        rows = pl.ds(start, size)
        scores = dot_nt(query, k_ref[rows, :])
        probs = jnp.exp2(scores * SCALE_LOG2)
        if causal:
            ahead = lax.broadcasted_iota(jnp.int32, probs.shape, 0)
            behind = lax.broadcasted_iota(jnp.int32, probs.shape, 1)
            probs = jnp.where(behind <= ahead, probs, 0.0)
        acc_ref[...] += dot(probs.astype(BF), v_ref[rows, :])

    @pl.when(index < trunk_blocks)
    def _():
        @pl.loop(0, index)
        def _(block):
            step(pl.multiple_of(block * SEG_LEN, SEG_LEN), SEG_LEN)

    @pl.when(index >= trunk_blocks)
    def _():
        size = 512
        for part in range(TRUNK // size):
            step(part * size, size)

        above = parent_ref[index]

        @pl.when(above >= 0)
        def _():
            step(pl.multiple_of(above * SEG_LEN, SEG_LEN), SEG_LEN)

    step(pl.multiple_of(index * SEG_LEN, SEG_LEN), SEG_LEN, True)
    total = acc_ref[:, HEAD_SIZE : HEAD_SIZE + 1]
    attended = acc_ref[:, :HEAD_SIZE] / total
    o_ref[...] = attended
    low_ref[...] = attended.astype(BF)
    spread = jnp.broadcast_to(total, (SEG_LEN, LANES))
    l_ref[0] = jnp.transpose(spread)[:8, :]


def attention_forward(parent_block, flag, got, theirs):
    length = theirs.shape[0]
    blocks = length // SEG_LEN
    whole = lambda i, p, f: (0, 0)
    part = lambda i, p, f: (i, 0)
    return pl.pallas_call(
        attention_forward_kernel,
        grid_spec=pltpu.PrefetchScalarGridSpec(
            num_scalar_prefetch=2,
            grid=(blocks,),
            in_specs=[
                pl.BlockSpec((SEG_LEN, HEAD_SIZE), part),
                pl.BlockSpec((length, HEAD_SIZE), lambda i, p, f: (0, 1)),
                pl.BlockSpec((length, HEAD_SIZE), whole),
            ],
            out_specs=[
                pl.BlockSpec((SEG_LEN, HEAD_SIZE), part),
                pl.BlockSpec((SEG_LEN, HEAD_SIZE), part),
                pl.BlockSpec((1, 8, SEG_LEN), lambda i, p, f: (i, 0, 0)),
            ],
            scratch_shapes=[
                pltpu.VMEM((length, HEAD_SIZE), BF),
                pltpu.VMEM((length, 2 * HEAD_SIZE), BF),
                pltpu.VMEM((SEG_LEN, 2 * HEAD_SIZE), F32),
            ],
        ),
        out_shape=[
            jax.ShapeDtypeStruct((length, HEAD_SIZE), F32),
            jax.ShapeDtypeStruct((length, HEAD_SIZE), BF),
            jax.ShapeDtypeStruct((blocks, 8, SEG_LEN), F32),
        ],
        compiler_params=pltpu.CompilerParams(vmem_limit_bytes=VMEM_LIMIT),
        cost_estimate=pl.CostEstimate(
            flops=160 * SEG_LEN * SEG_LEN * HEAD_SIZE * 4,
            bytes_accessed=length * HEAD_SIZE * 12,
            transcendentals=160 * SEG_LEN * SEG_LEN,
        ),
        name="attention_forward",
    )(parent_block, flag, got, got, theirs)


def attention_backward_kernel(
    parent_ref,
    flag_ref,
    q_ref,
    g_ref,
    o_ref,
    l_ref,
    mine_ref,
    theirs_ref,
    dq_ref,
    kept_ref,
    given_ref,
    k_ref,
    v_ref,
    kt_ref,
    dk_ref,
    dv_ref,
    acc_ref,
):
    index = pl.program_id(0)
    trunk_blocks = TRUNK // SEG_LEN

    @pl.when(index == 0)
    def _():
        dk_ref[...] = jnp.zeros_like(dk_ref)
        dv_ref[...] = jnp.zeros_like(dv_ref)

        @pl.when(flag_ref[0] == 1)
        def _():
            k_ref[...] = mine_ref[...]
            v_ref[...] = theirs_ref[...]

        @pl.when(flag_ref[0] != 1)
        def _():
            k_ref[...] = theirs_ref[...]
            v_ref[...] = mine_ref[...]

        @pl.loop(0, k_ref.shape[0] // SEG_LEN)
        def _(block):
            rows = pl.ds(pl.multiple_of(block * SEG_LEN, SEG_LEN), SEG_LEN)
            kt_ref[:, rows] = jnp.transpose(k_ref[rows, :])

    query = q_ref[...]
    grad = g_ref[...]
    delta = jnp.sum(grad.astype(F32) * o_ref[...], axis=1, keepdims=True)
    delta = jnp.transpose(jnp.broadcast_to(delta, (SEG_LEN, LANES)))[:1, :]
    inverse = 1.0 / l_ref[0, :1, :]
    acc_ref[...] = jnp.zeros_like(acc_ref)

    def step(start, size, causal=False):
        rows = pl.ds(start, size)
        probs = jnp.exp2(dot_nt(k_ref[rows, :], query) * SCALE_LOG2) * inverse
        if causal:
            behind = lax.broadcasted_iota(jnp.int32, probs.shape, 0)
            ahead = lax.broadcasted_iota(jnp.int32, probs.shape, 1)
            probs = jnp.where(behind <= ahead, probs, 0.0)
        dprobs = dot_nt(v_ref[rows, :], grad)
        dscores = (probs * (dprobs - delta)).astype(BF)
        dv_ref[rows, :] += dot(probs.astype(BF), grad)
        dk_ref[rows, :] += dot(dscores, query)
        acc_ref[...] += dot(kt_ref[:, rows], dscores)

    @pl.when(index < trunk_blocks)
    def _():
        @pl.loop(0, index)
        def _(block):
            step(pl.multiple_of(block * SEG_LEN, SEG_LEN), SEG_LEN)

    @pl.when(index >= trunk_blocks)
    def _():
        size = 512
        for part in range(TRUNK // size):
            step(part * size, size)

        above = parent_ref[index]

        @pl.when(above >= 0)
        def _():
            step(pl.multiple_of(above * SEG_LEN, SEG_LEN), SEG_LEN)

    step(pl.multiple_of(index * SEG_LEN, SEG_LEN), SEG_LEN, True)
    dq_ref[...] = (jnp.transpose(acc_ref[...]) * SCALE).astype(BF)

    @pl.when(index == pl.num_programs(0) - 1)
    def _():
        @pl.when(flag_ref[0] == 1)
        def _():
            kept_ref[...] = dk_ref[...] * SCALE
            given_ref[...] = dv_ref[...]

        @pl.when(flag_ref[0] != 1)
        def _():
            kept_ref[...] = dv_ref[...]
            given_ref[...] = dk_ref[...] * SCALE


def attention_backward(parent_block, flag, got, grad, attended, totals, theirs):
    length = theirs.shape[0]
    blocks = length // SEG_LEN
    whole = lambda i, p, f: (0, 0)
    part = lambda i, p, f: (i, 0)
    return pl.pallas_call(
        attention_backward_kernel,
        grid_spec=pltpu.PrefetchScalarGridSpec(
            num_scalar_prefetch=2,
            grid=(blocks,),
            in_specs=[
                pl.BlockSpec((SEG_LEN, HEAD_SIZE), part),
                pl.BlockSpec((SEG_LEN, HEAD_SIZE), part),
                pl.BlockSpec((SEG_LEN, HEAD_SIZE), part),
                pl.BlockSpec((1, 8, SEG_LEN), lambda i, p, f: (i, 0, 0)),
                pl.BlockSpec((length, HEAD_SIZE), lambda i, p, f: (0, 1)),
                pl.BlockSpec((length, HEAD_SIZE), whole),
            ],
            out_specs=[
                pl.BlockSpec((SEG_LEN, HEAD_SIZE), part),
                pl.BlockSpec((length, HEAD_SIZE), whole),
                pl.BlockSpec((length, HEAD_SIZE), whole),
            ],
            scratch_shapes=[
                pltpu.VMEM((length, HEAD_SIZE), BF),
                pltpu.VMEM((length, HEAD_SIZE), BF),
                pltpu.VMEM((HEAD_SIZE, length), BF),
                pltpu.VMEM((length, HEAD_SIZE), F32),
                pltpu.VMEM((length, HEAD_SIZE), F32),
                pltpu.VMEM((HEAD_SIZE, SEG_LEN), F32),
            ],
        ),
        out_shape=[
            jax.ShapeDtypeStruct((length, 2 * HEAD_SIZE), BF),
            jax.ShapeDtypeStruct((length, HEAD_SIZE), F32),
            jax.ShapeDtypeStruct((length, HEAD_SIZE), F32),
        ],
        compiler_params=pltpu.CompilerParams(vmem_limit_bytes=VMEM_LIMIT),
        cost_estimate=pl.CostEstimate(
            flops=160 * SEG_LEN * SEG_LEN * HEAD_SIZE * 10,
            bytes_accessed=length * HEAD_SIZE * 24,
            transcendentals=160 * SEG_LEN * SEG_LEN,
        ),
        name="attention_backward",
    )(parent_block, flag, got, grad, attended, totals, got, theirs)


def merge_kernel(lines_ref, kept_ref, got_ref, out_ref):
    out_ref[...] = (kept_ref[...] + got_ref[...]).astype(BF)


def merge(lines, kept, got):
    length = kept.shape[0]
    rows = 4 * SEG_LEN
    part = pl.BlockSpec((rows, HEAD_SIZE), lambda i: (i, 0))
    return pl.pallas_call(
        merge_kernel,
        grid=(length // rows,),
        in_specs=[pl.BlockSpec(memory_space=pl.ANY), part, part],
        out_specs=pl.BlockSpec((rows, HEAD_SIZE), lambda i: (i, 1)),
        out_shape=jax.ShapeDtypeStruct(lines.shape, lines.dtype),
        input_output_aliases={0: 0},
        cost_estimate=pl.CostEstimate(
            flops=length * HEAD_SIZE, bytes_accessed=length * HEAD_SIZE * 10, transcendentals=0
        ),
        name="merge",
    )(lines, kept, got)


def norm_scale(values):
    return lax.rsqrt(jnp.mean(values * values, axis=1, keepdims=True) + EPSILON)


def norm_back(values, scale, gain, gradient):
    weighted = gain * gradient
    inner_sum = jnp.sum(weighted * values, axis=1, keepdims=True)
    return scale * weighted - values * (scale**3 * (inner_sum * (1.0 / MODEL_WIDTH)))


def outmaps_of(w_ref, pieces, piece, used):
    at = pieces * piece
    return jnp.concatenate(
        [w_ref[0, 0, at + p * used : at + (p + 1) * used, :] for p in range(pieces)], axis=1
    )


def qkv_forward_kernel(
    x_ref,
    gain_ref,
    a_ref,
    cos_ref,
    sin_ref,
    hg_ref,
    w_ref,
    m_ref,
    pre_ref,
    sent_ref,
    hidden_ref,
):
    row_blocks = w_ref.shape[1]
    piece = w_ref.shape[3]
    pieces = w_ref.shape[2] // piece
    heads = sent_ref.shape[0]
    used = m_ref.shape[1]

    @pl.when(pl.program_id(0) == 0)
    def _():
        resid = x_ref[...].astype(F32)
        hidden_ref[...] = (resid * norm_scale(resid) * gain_ref[...]).astype(BF)
        m_ref[...] = dot(hidden_ref[...], a_ref[...]).astype(BF)

    hidden = hidden_ref[...]
    whole = jnp.concatenate(
        [
            dot(
                hidden,
                jnp.concatenate(
                    [w_ref[0, r, p * piece : (p + 1) * piece, :] for r in range(row_blocks)], axis=0
                ),
            )
            for p in range(pieces)
        ],
        axis=1,
    ) + ADAPTER_FACTOR * dot(m_ref[...], outmaps_of(w_ref, pieces, piece, used))
    pre_ref[0] = whole[:, : pre_ref.shape[2]]
    cosine = cos_ref[...]
    sine = sin_ref[...]

    def shaped(at, gain):
        lines = whole[:, at : at + HEAD_SIZE]
        normed = lines * norm_scale(lines) * gain
        return (normed * cosine + pltpu.roll(normed, HEAD_SIZE // 2, 1) * sine).astype(BF)

    for head in range(heads):
        sent_ref[head, :, :HEAD_SIZE] = shaped(head * HEAD_SIZE, hg_ref[0:1, :])
    key_at = heads * HEAD_SIZE
    value_at = key_at + heads // 2 * HEAD_SIZE
    for pair in range(heads // 2):
        at = pair * HEAD_SIZE
        sent_ref[2 * pair, :, HEAD_SIZE:] = shaped(key_at + at, hg_ref[1:2, :])
        sent_ref[2 * pair + 1, :, HEAD_SIZE:] = whole[
            :, value_at + at : value_at + at + HEAD_SIZE
        ].astype(BF)


def qkv_forward(x, gain, inmaps, cosine, sine, head_gains, weights):
    own = x.shape[0]
    cols, row_blocks, tall, piece = weights.shape
    wide = tall // piece * piece
    used = inmaps.shape[1]
    heads = QUERY_HEADS // cols
    whole = lambda c: (0, 0)
    step = lambda c: (c, 0, 0)
    return pl.pallas_call(
        qkv_forward_kernel,
        grid=(cols,),
        in_specs=[
            pl.BlockSpec(x.shape, whole),
            pl.BlockSpec(gain.shape, whole),
            pl.BlockSpec(inmaps.shape, whole),
            pl.BlockSpec(cosine.shape, whole),
            pl.BlockSpec(sine.shape, whole),
            pl.BlockSpec(head_gains.shape, whole),
            pl.BlockSpec((1, row_blocks, tall, piece), lambda c: (c, 0, 0, 0)),
        ],
        out_specs=[
            pl.BlockSpec((own, used), whole),
            pl.BlockSpec((1, own, wide * 3 // 4), step),
            pl.BlockSpec((heads, own, 2 * HEAD_SIZE), step),
        ],
        out_shape=[
            jax.ShapeDtypeStruct((own, used), BF),
            jax.ShapeDtypeStruct((cols, own, wide * 3 // 4), F32),
            jax.ShapeDtypeStruct((QUERY_HEADS, own, 2 * HEAD_SIZE), BF),
        ],
        scratch_shapes=[pltpu.VMEM((own, MODEL_WIDTH), BF)],
        compiler_params=pltpu.CompilerParams(vmem_limit_bytes=VMEM_LIMIT),
        cost_estimate=pl.CostEstimate(
            flops=2 * own * MODEL_WIDTH * cols * wide,
            bytes_accessed=cols * wide * MODEL_WIDTH * 2,
            transcendentals=own * cols * 8,
        ),
        name="qkv_forward",
    )(x, gain, inmaps, cosine, sine, head_gains, weights)


def qkv_unshape_kernel(
    ret_ref,
    pre_ref,
    m_ref,
    x_ref,
    gain_ref,
    cos_ref,
    sin_ref,
    hg_ref,
    w_ref,
    grads_ref,
    inner_ref,
    ga_ref,
    gb_ref,
    in_acc_ref,
):
    step = pl.program_id(0)
    row_blocks, used, piece = ga_ref.shape
    heads = ret_ref.shape[0]
    pieces = grads_ref.shape[2] // piece
    cosine = cos_ref[...]
    sine = sin_ref[...]

    @pl.when(step == 0)
    def _():
        in_acc_ref[...] = jnp.zeros_like(in_acc_ref)

    def unshaped(grad, at, gain):
        grad = grad.astype(F32)
        lines = pre_ref[0, :, at : at + HEAD_SIZE]
        turned = gain * (grad * cosine + pltpu.roll(grad * sine, HEAD_SIZE // 2, 1))
        scale = norm_scale(lines)
        inner_mean = jnp.mean(turned * lines, axis=1, keepdims=True)
        return (scale * turned - lines * (scale**3 * inner_mean)).astype(BF)

    parts = []
    for head in range(heads):
        parts.append(unshaped(ret_ref[head, :, :HEAD_SIZE], head * HEAD_SIZE, hg_ref[0:1, :]))
    for pair in range(heads // 2):
        at = (heads + pair) * HEAD_SIZE
        parts.append(unshaped(ret_ref[2 * pair, :, HEAD_SIZE:], at, hg_ref[1:2, :]))
    for pair in range(heads // 2):
        parts.append(ret_ref[2 * pair + 1, :, HEAD_SIZE:])
    grads = jnp.concatenate(parts, axis=1)
    grads_ref[0] = grads
    outmaps = jnp.concatenate(
        [w_ref[0, 0, p * used : (p + 1) * used, :] for p in range(pieces)], axis=1
    )
    in_acc_ref[...] += dot_nt(grads, outmaps)
    outer = ADAPTER_FACTOR * dot_tn(m_ref[...], grads)
    rank = ADAPTER_RANK
    edges = (0, heads * HEAD_SIZE, heads * HEAD_SIZE * 3 // 2, heads * HEAD_SIZE * 2)
    for i in range(3):
        gb_ref[0, :, edges[i] : edges[i + 1]] = outer[
            i * rank : (i + 1) * rank, edges[i] : edges[i + 1]
        ]

    @pl.when(step == pl.num_programs(0) - 1)
    def _():
        inner = (ADAPTER_FACTOR * in_acc_ref[...]).astype(BF)
        inner_ref[...] = inner
        resid = x_ref[...].astype(F32)
        hidden = (resid * norm_scale(resid) * gain_ref[...]).astype(BF)
        for r in range(row_blocks):
            ga_ref[r] = dot_tn(inner, hidden[:, r * piece : (r + 1) * piece])


def qkv_unshape(returned, pre, masked, x, gain, cosine, sine, head_gains, weights):
    own = x.shape[0]
    cols, row_blocks, tall, piece = weights.shape
    pieces = tall // piece
    wide = pieces * piece
    heads = QUERY_HEADS // cols
    used = 3 * ADAPTER_RANK
    map_rows = tall - wide
    at = wide // map_rows if wide % map_rows == 0 else None
    maps = weights[:, :1, wide:] if at is None else weights
    first = 0 if at is None else at
    whole = lambda c: (0, 0)
    step = lambda c: (c, 0, 0)
    return pl.pallas_call(
        qkv_unshape_kernel,
        grid=(cols,),
        in_specs=[
            pl.BlockSpec((heads, own, 2 * HEAD_SIZE), step),
            pl.BlockSpec((1, own, pre.shape[2]), step),
            pl.BlockSpec(masked.shape, whole),
            pl.BlockSpec(x.shape, whole),
            pl.BlockSpec(gain.shape, whole),
            pl.BlockSpec(cosine.shape, whole),
            pl.BlockSpec(sine.shape, whole),
            pl.BlockSpec(head_gains.shape, whole),
            pl.BlockSpec((1, 1, map_rows, piece), lambda c: (c, 0, first, 0)),
        ],
        out_specs=[
            pl.BlockSpec((1, own, wide), step),
            pl.BlockSpec((own, used), whole),
            pl.BlockSpec((row_blocks, used, piece), lambda c: (0, 0, 0)),
            pl.BlockSpec((1, ADAPTER_RANK, wide), step),
        ],
        out_shape=[
            jax.ShapeDtypeStruct((cols, own, wide), BF),
            jax.ShapeDtypeStruct((own, used), BF),
            jax.ShapeDtypeStruct((row_blocks, used, piece), F32),
            jax.ShapeDtypeStruct((cols, ADAPTER_RANK, wide), F32),
        ],
        scratch_shapes=[pltpu.VMEM((own, used), F32)],
        compiler_params=pltpu.CompilerParams(vmem_limit_bytes=VMEM_LIMIT),
        cost_estimate=pl.CostEstimate(
            flops=4 * own * 64 * cols * wide,
            bytes_accessed=cols * own * wide * 8,
            transcendentals=own * cols * 8,
        ),
        name="qkv_unshape",
    )(returned, pre, masked, x, gain, cosine, sine, head_gains, maps)


def qkv_backward_kernel(
    grads_ref, inner_ref, x_ref, gm_ref, gain_ref, a_ref, w_ref, grad_ref, acc_ref
):
    step = pl.program_id(0)
    row_blocks = w_ref.shape[1]
    piece = w_ref.shape[3]
    pieces = w_ref.shape[2] // piece

    @pl.when(step == 0)
    def _():
        acc_ref[...] = dot_nt(inner_ref[...], a_ref[...])

    for r in range(row_blocks):
        weights = jnp.concatenate(
            [w_ref[0, r, p * piece : (p + 1) * piece, :] for p in range(pieces)], axis=1
        )
        acc_ref[:, r * piece : (r + 1) * piece] += dot_nt(grads_ref[0], weights)

    @pl.when(step == pl.num_programs(0) - 1)
    def _():
        resid = x_ref[...].astype(F32)
        grad_ref[...] = (
            gm_ref[...] + norm_back(resid, norm_scale(resid), gain_ref[...], acc_ref[...])
        ).astype(BF)


def qkv_backward(grads, inner, x, grad_middle, gain, inmaps, weights):
    own = x.shape[0]
    cols, row_blocks, tall, piece = weights.shape
    wide = tall // piece * piece
    whole = lambda c: (0, 0)
    once = pl.Buffered(1)
    return pl.pallas_call(
        qkv_backward_kernel,
        grid=(cols,),
        in_specs=[
            pl.BlockSpec((1, own, wide), lambda c: (c, 0, 0)),
            pl.BlockSpec(inner.shape, whole),
            pl.BlockSpec(x.shape, whole, pipeline_mode=once),
            pl.BlockSpec(grad_middle.shape, whole, pipeline_mode=once),
            pl.BlockSpec(gain.shape, whole),
            pl.BlockSpec(inmaps.shape, whole),
            pl.BlockSpec((1, row_blocks, wide, piece), lambda c: (c, 0, 0, 0)),
        ],
        out_specs=pl.BlockSpec((own, MODEL_WIDTH), whole),
        out_shape=jax.ShapeDtypeStruct((own, MODEL_WIDTH), BF),
        scratch_shapes=[pltpu.VMEM((own, MODEL_WIDTH), F32)],
        compiler_params=pltpu.CompilerParams(vmem_limit_bytes=VMEM_LIMIT),
        cost_estimate=pl.CostEstimate(
            flops=2 * own * MODEL_WIDTH * cols * wide,
            bytes_accessed=cols * wide * MODEL_WIDTH * 2,
            transcendentals=own,
        ),
        name="qkv_backward",
    )(grads, inner, x, grad_middle, gain, inmaps, weights)


def joined(refs, tall):
    return jnp.concatenate(
        [ref[0, r, 0, :tall, :] for r in range(refs[0].shape[1]) for ref in refs], axis=1
    )


def output_specs(weights, first_unit, features):
    row_blocks, tall = weights.shape[1], weights.shape[3]

    def spec(unit):
        return pl.BlockSpec((1, row_blocks, 1, tall, LANES), lambda c: (c, 0, unit, 0, 0))

    return [spec(first_unit + j) for j in range(features // LANES)]


def output_forward_kernel(att_ref, x_ref, gain_ref, a_ref, b_ref, *refs):
    weight_refs = refs[:-5]
    middle_ref, hidden_ref, m_ref, acc_ref, m_acc_ref = refs[-5:]
    step = pl.program_id(0)
    heads = att_ref.shape[0]

    @pl.when(step == 0)
    def _():
        acc_ref[...] = x_ref[...].astype(F32)
        m_acc_ref[...] = jnp.zeros_like(m_acc_ref)

    attended = jnp.concatenate([att_ref[h] for h in range(heads)], axis=1)
    acc_ref[...] += dot(attended, joined(weight_refs, attended.shape[1]))
    m_acc_ref[...] += dot_nt(attended, a_ref[0])

    @pl.when(step == pl.num_programs(0) - 1)
    def _():
        masked = m_acc_ref[...].astype(BF)
        m_ref[...] = masked
        middle = acc_ref[...] + ADAPTER_FACTOR * dot_nt(masked, b_ref[...])
        middle_ref[...] = middle
        hidden_ref[...] = (middle * norm_scale(middle) * gain_ref[...]).astype(BF)


def output_forward(attended, x, gain, inmaps, outmaps, weights, first_unit):
    own = x.shape[0]
    cols, row_blocks = weights.shape[:2]
    features = MODEL_WIDTH // row_blocks
    heads = QUERY_HEADS // cols
    o_rows = heads * HEAD_SIZE
    specs = output_specs(weights, first_unit, features)
    whole = lambda c: (0, 0)
    step = lambda c: (c, 0, 0)
    return pl.pallas_call(
        output_forward_kernel,
        grid=(cols,),
        in_specs=[
            pl.BlockSpec((heads, own, HEAD_SIZE), step),
            pl.BlockSpec(x.shape, whole),
            pl.BlockSpec(gain.shape, whole),
            pl.BlockSpec((1, LANES, o_rows), step),
            pl.BlockSpec(outmaps.shape, whole),
            *specs,
        ],
        out_specs=[
            pl.BlockSpec((own, MODEL_WIDTH), whole),
            pl.BlockSpec((own, MODEL_WIDTH), whole),
            pl.BlockSpec((own, LANES), whole),
        ],
        out_shape=[
            jax.ShapeDtypeStruct((own, MODEL_WIDTH), F32),
            jax.ShapeDtypeStruct((own, MODEL_WIDTH), BF),
            jax.ShapeDtypeStruct((own, LANES), BF),
        ],
        scratch_shapes=[pltpu.VMEM((own, MODEL_WIDTH), F32), pltpu.VMEM((own, LANES), F32)],
        compiler_params=pltpu.CompilerParams(vmem_limit_bytes=VMEM_LIMIT),
        cost_estimate=pl.CostEstimate(
            flops=2 * own * MODEL_WIDTH * MODEL_WIDTH,
            bytes_accessed=2 * MODEL_WIDTH * MODEL_WIDTH,
            transcendentals=own,
        ),
        name="output_forward",
    )(attended, x, gain, inmaps, outmaps, *[weights] * len(specs))


def output_backward_kernel(
    gh_ref,
    got_ref,
    cot_ref,
    middle_ref,
    gain_ref,
    a_ref,
    b_ref,
    att_ref,
    m_ref,
    *refs,
):
    weight_refs = refs[:-6]
    gm_ref, sent_ref, gb_ref, ga_ref, low_ref, inner_ref = refs[-6:]
    heads = sent_ref.shape[0]
    row_blocks, rank, features = gb_ref.shape

    @pl.when(pl.program_id(0) == 0)
    def _():
        grad_hidden = gh_ref[...] + got_ref[...].astype(F32)
        middle = middle_ref[...]
        grad = cot_ref[...].astype(F32) + norm_back(
            middle, norm_scale(middle), gain_ref[...], grad_hidden
        )
        gm_ref[...] = grad
        low_ref[...] = grad.astype(BF)
        inner_ref[...] = (ADAPTER_FACTOR * dot(low_ref[...], b_ref[...])).astype(BF)
        outer = ADAPTER_FACTOR * dot_tn(m_ref[...], low_ref[...])
        for r in range(row_blocks):
            gb_ref[r] = outer[:rank, r * features : (r + 1) * features]

    attended = jnp.concatenate([att_ref[h] for h in range(heads)], axis=1)
    ga_ref[0] = dot_tn(inner_ref[...], attended)[:rank, :]
    weights = joined(weight_refs, heads * HEAD_SIZE)
    grad = (dot_nt(low_ref[...], weights) + dot(inner_ref[...], a_ref[0])).astype(BF)
    for head in range(heads):
        sent_ref[head] = grad[:, head * HEAD_SIZE : (head + 1) * HEAD_SIZE]


def output_backward(
    grad_hidden, got, cotangent, middle, gain, inmaps, outmaps, attended, masked, weights, first_unit
):
    own = middle.shape[0]
    cols, row_blocks = weights.shape[:2]
    features = MODEL_WIDTH // row_blocks
    heads = QUERY_HEADS // cols
    o_rows = heads * HEAD_SIZE
    specs = output_specs(weights, first_unit, features)
    whole = lambda c: (0, 0)
    step = lambda c: (c, 0, 0)
    once = pl.Buffered(1)
    return pl.pallas_call(
        output_backward_kernel,
        grid=(cols,),
        in_specs=[
            pl.BlockSpec((own, MODEL_WIDTH), whole, pipeline_mode=once),
            pl.BlockSpec((own, MODEL_WIDTH), whole, pipeline_mode=once),
            pl.BlockSpec((own, MODEL_WIDTH), whole, pipeline_mode=once),
            pl.BlockSpec((own, MODEL_WIDTH), whole, pipeline_mode=once),
            pl.BlockSpec(gain.shape, whole),
            pl.BlockSpec((1, LANES, o_rows), step),
            pl.BlockSpec(outmaps.shape, whole),
            pl.BlockSpec((heads, own, HEAD_SIZE), step),
            pl.BlockSpec(masked.shape, whole),
            *specs,
        ],
        out_specs=[
            pl.BlockSpec((own, MODEL_WIDTH), whole),
            pl.BlockSpec((heads, own, HEAD_SIZE), step),
            pl.BlockSpec((row_blocks, ADAPTER_RANK, features), lambda c: (0, 0, 0)),
            pl.BlockSpec((1, ADAPTER_RANK, o_rows), step),
        ],
        out_shape=[
            jax.ShapeDtypeStruct((own, MODEL_WIDTH), F32),
            jax.ShapeDtypeStruct((QUERY_HEADS, own, HEAD_SIZE), BF),
            jax.ShapeDtypeStruct((row_blocks, ADAPTER_RANK, features), F32),
            jax.ShapeDtypeStruct((cols, ADAPTER_RANK, o_rows), F32),
        ],
        scratch_shapes=[pltpu.VMEM((own, MODEL_WIDTH), BF), pltpu.VMEM((own, LANES), BF)],
        compiler_params=pltpu.CompilerParams(vmem_limit_bytes=VMEM_LIMIT),
        cost_estimate=pl.CostEstimate(
            flops=2 * own * MODEL_WIDTH * MODEL_WIDTH,
            bytes_accessed=2 * MODEL_WIDTH * MODEL_WIDTH,
            transcendentals=own,
        ),
        name="output_backward",
    )(
        grad_hidden,
        got,
        cotangent,
        middle,
        gain,
        inmaps,
        outmaps,
        attended,
        masked,
        *[weights] * len(specs),
    )


def feed_forward_kernel(
    first, last, h_ref, c_ref, mg_ref, mu_ref, nd_ref, mask_ref, ag_ref, au_ref, od_ref, *refs
):
    weight_refs, map_refs, refs = refs[:2], refs[2:4], refs[4:]
    if first:
        previous = None
    else:
        previous, refs = refs[:5], refs[5:]
    if last:
        (gh_ref, out_ref, rows_ref), refs = refs[:3], refs[3:]
    else:
        accs, refs = refs[:5], refs[5:]
    grads_refs, refs = refs[:2], refs[2:]
    gh_acc, out_acc, md_acc, ig_acc, iu_acc = scratch = refs[:5]
    sems = refs[5]
    step = pl.program_id(0)
    row_blocks = weight_refs[0].shape[1]
    deep = MODEL_WIDTH // row_blocks
    used = mg_ref.shape[1]

    @pl.when(step == 0)
    def _():
        if first:
            for ref in scratch:
                ref[...] = jnp.zeros_like(ref)
        else:
            copies = [
                pltpu.make_async_copy(previous[i], scratch[i], sems.at[i]) for i in range(5)
            ]
            for copy in copies:
                copy.start()
            for copy in copies:
                copy.wait()

    def side(kind, row):
        return jnp.concatenate([ref[0, row, kind] for ref in weight_refs], axis=1)

    def tall_side(kind):
        return jnp.concatenate([side(kind, row) for row in range(row_blocks)], axis=0)

    def down_side(row):
        return jnp.concatenate(
            [
                jnp.concatenate(
                    [ref[0, row, 2, at : at + LANES, :] for at in range(0, deep, LANES)], axis=1
                )
                for ref in weight_refs
            ],
            axis=0,
        )

    def maps(kind):
        return jnp.concatenate(
            [ref[0, kind * used : (kind + 1) * used, :] for ref in map_refs], axis=1
        )

    gate_map, up_map, down_map = maps(0), maps(1), maps(2)
    gate = dot(h_ref[...], tall_side(0)) + ADAPTER_FACTOR * dot(mg_ref[...], gate_map)
    upward = dot(h_ref[...], tall_side(1)) + ADAPTER_FACTOR * dot(mu_ref[...], up_map)
    down = jnp.concatenate([down_side(row) for row in range(row_blocks)], axis=1)
    grad_act = dot_nt(c_ref[...], down) + dot(nd_ref[...], down_map)
    sigma = 1.0 / (1.0 + jnp.exp(-gate))
    swish = gate * sigma
    act = (swish * upward).astype(BF)
    grad_gate = (grad_act * upward * (sigma * (1.0 + gate * (1.0 - sigma)))).astype(BF)
    grad_up = (grad_act * swish).astype(BF)
    both = jnp.concatenate([grad_gate, grad_up], axis=1)
    for row in range(row_blocks):
        at = slice(row * deep, (row + 1) * deep)
        gh_acc[:, at] += dot_nt(both, jnp.concatenate([side(0, row), side(1, row)], axis=1))
        out_acc[:, at] += dot(act, down_side(row))
    md_acc[...] += dot_nt(act, down_map)
    ig_acc[...] += dot_nt(grad_gate, gate_map)
    iu_acc[...] += dot_nt(grad_up, up_map)
    partial = (
        ADAPTER_FACTOR * dot_tn(mg_ref[...], grad_gate),
        ADAPTER_FACTOR * dot_tn(mu_ref[...], grad_up),
        dot_tn(nd_ref[...], act),
    )
    for kind in range(3):
        for i, ref in enumerate(grads_refs):
            ref[0, kind * used : (kind + 1) * used, :] = partial[kind][
                :, i * LANES : (i + 1) * LANES
            ]

    @pl.when(step == pl.num_programs(0) - 1)
    def _():
        if last:
            mask = mask_ref[...]
            inner_g = (ADAPTER_FACTOR * ig_acc[...] * mask).astype(BF)
            inner_u = (ADAPTER_FACTOR * iu_acc[...] * mask).astype(BF)
            masked = (md_acc[...] * mask).astype(BF)
            gh_ref[...] = (
                gh_acc[...] + dot_nt(inner_g, ag_ref[...]) + dot_nt(inner_u, au_ref[...])
            ).astype(gh_ref.dtype)
            out_ref[...] = (out_acc[...] + ADAPTER_FACTOR * dot_nt(masked, od_ref[...])).astype(
                out_ref.dtype
            )
            for row in range(row_blocks):
                at = slice(row * deep, (row + 1) * deep)
                rows_ref[row, :used, :] = dot_tn(inner_g, h_ref[:, at])
                rows_ref[row, used : 2 * used, :] = dot_tn(inner_u, h_ref[:, at])
                rows_ref[row, 2 * used :, :] = ADAPTER_FACTOR * dot_tn(masked, c_ref[:, at])
        else:
            copies = [pltpu.make_async_copy(scratch[i], accs[i], sems.at[i]) for i in range(5)]
            for copy in copies:
                copy.start()
            for copy in copies:
                copy.wait()


def feed_forward_chunk(hidden, cotangent, masks, tables, weights, maps, previous, last, dtype):
    first = previous is None
    cols, row_blocks, _, deep, _ = weights.shape
    slabs = maps.shape[0] // cols
    count, used = masks[0].shape
    whole = lambda i: (0, 0)
    once = pl.Buffered(1)
    steps = cols * slabs // 2
    acc_shapes = [(count, MODEL_WIDTH)] * 2 + [(count, used)] * 3

    def weight_spec(side):
        def at(i):
            return ((2 * i + side) // slabs, 0, (2 * i + side) % slabs, 0, 0)

        return pl.BlockSpec((1, row_blocks, 3, deep, LANES), at)

    def slab_spec(side):
        return pl.BlockSpec((1, 3 * used, LANES), lambda i: (2 * i + side, 0, 0))

    def half_spec(side):
        return pl.BlockSpec((1, 3 * used, LANES), lambda i: (i, 0, 0))

    in_specs = (
        [pl.BlockSpec((count, MODEL_WIDTH), whole, pipeline_mode=once)] * 2
        + [pl.BlockSpec((count, used), whole)] * 4
        + [pl.BlockSpec((MODEL_WIDTH, used), whole, pipeline_mode=once)] * 3
        + [weight_spec(0), weight_spec(1), slab_spec(0), slab_spec(1)]
    )
    operands = [hidden, cotangent, *masks, *tables, weights, weights, maps, maps]
    if not first:
        in_specs = in_specs + [pl.BlockSpec(memory_space=pl.ANY)] * 5
        operands = operands + list(previous)
    if last:
        out_specs = [pl.BlockSpec((count, MODEL_WIDTH), whole)] * 2 + [
            pl.BlockSpec((row_blocks, 3 * used, deep), lambda i: (0, 0, 0))
        ]
        out_shape = [jax.ShapeDtypeStruct(s, dtype) for s in acc_shapes[:2]] + [
            jax.ShapeDtypeStruct((row_blocks, 3 * used, deep), F32)
        ]
    else:
        out_specs = [pl.BlockSpec(memory_space=pl.ANY)] * 5
        out_shape = [jax.ShapeDtypeStruct(s, F32) for s in acc_shapes]
    outs = pl.pallas_call(
        functools.partial(feed_forward_kernel, first, last),
        grid=(steps,),
        in_specs=in_specs,
        out_specs=out_specs + [half_spec(0), half_spec(1)],
        out_shape=out_shape + [jax.ShapeDtypeStruct((steps, 3 * used, LANES), F32)] * 2,
        scratch_shapes=[pltpu.VMEM(s, F32) for s in acc_shapes]
        + [pltpu.SemaphoreType.DMA((5,))],
        compiler_params=pltpu.CompilerParams(vmem_limit_bytes=VMEM_LIMIT),
        cost_estimate=pl.CostEstimate(
            flops=24 * count * MODEL_WIDTH * steps * LANES,
            bytes_accessed=steps * row_blocks * 6 * deep * LANES * 2,
            transcendentals=count * steps * 2 * LANES,
        ),
        name="feed_forward",
    )(*operands)
    return outs[:-2], outs[-2:]


def place(first, first_at, second, second_at, columns):
    index = jnp.arange(columns)[:, None] // ADAPTER_RANK
    copies = columns // ADAPTER_RANK
    return jnp.where(index == first_at, jnp.tile(first, (copies, 1)), 0.0) + jnp.where(
        index == second_at, jnp.tile(second, (copies, 1)), 0.0
    )


def lane_pad(values):
    return jnp.pad(values, ((0, 0),) * (values.ndim - 1) + ((0, LANES - values.shape[-1]),))


def row_pad(values):
    return jnp.pad(
        values, ((0, 0),) * (values.ndim - 2) + ((0, LANES - values.shape[-2]), (0, 0))
    )


def thirds(values):
    parts = []
    for _ in range(3):
        part = lax.reduce_precision(values, 8, 7)
        parts.append(part.astype(BF)[:, None])
        values = values - part
    return parts


def summed(values, axis):
    size = lax.axis_size(axis)
    bit = 1
    while bit < size:
        pairs = [(i, i ^ bit) for i in range(size)]
        values = values + lax.ppermute(values, axis, pairs)
        bit = 2 * bit
    return values


def summed_block(blocks, axis):
    size = lax.axis_size(axis)
    at = lax.axis_index(axis)
    bit = size // 2
    while bit:
        pairs = [(i, i ^ bit) for i in range(size)]
        halves = blocks.reshape(2, bit, *blocks.shape[1:])
        upper = (at // bit) % 2
        kept = lax.dynamic_index_in_dim(halves, upper, 0, False)
        sent = lax.dynamic_index_in_dim(halves, 1 - upper, 0, False)
        blocks = kept + lax.ppermute(sent, axis, pairs)
        bit = bit // 2
    return blocks[0]


def on_device(
    tokens,
    cotangent,
    attention_norm_gain,
    feedfwd_norm_gain,
    query_norm_gain,
    key_norm_gain,
    query_matrix,
    key_matrix,
    value_matrix,
    output_matrix,
    gate_matrix,
    up_matrix,
    down_matrix,
    query_adapter_inmaps,
    query_adapter_outmaps,
    key_adapter_inmaps,
    key_adapter_outmaps,
    value_adapter_inmaps,
    value_adapter_outmaps,
    output_adapter_inmaps,
    output_adapter_outmaps,
    gate_adapter_inmaps,
    gate_adapter_outmaps,
    up_adapter_inmaps,
    up_adapter_outmaps,
    down_adapter_inmaps,
    down_adapter_outmaps,
    segment,
    depth,
    parent,
    adapter,
):
    rows = lax.axis_size("row")
    cols = lax.axis_size("col")
    devices = rows * cols
    repeat = devices // QUERY_HEADS
    plane = lax.axis_index("dp")
    row = lax.axis_index("row")
    col = lax.axis_index("col")
    length = segment.shape[0]
    own = tokens.shape[0] // rows
    columns = query_adapter_inmaps.shape[1]
    rank = ADAPTER_RANK
    swap = [(0, 1), (1, 0)]
    pairs = [(r, r ^ repeat) for r in range(rows)]
    q_local = query_matrix.shape[1]
    kv_local = key_matrix.shape[1]
    wide = q_local + 2 * kv_local
    features = gate_matrix.shape[0]

    own_adapter = adapter[0]
    other_adapter = lax.ppermute(adapter, "dp", swap)[0]
    both = (own_adapter, other_adapter)

    def inmap(table, at):
        return lax.dynamic_slice_in_dim(table, at * rank, rank, 1)

    def outmap(table, at):
        return lax.dynamic_slice_in_dim(table, at * rank, rank, 0)

    qkv_local = jnp.concatenate([query_matrix, key_matrix, value_matrix], axis=1)

    def block_of(table, before, after):
        return jnp.pad(outmap(table, own_adapter), ((0, 0), (before, after)))

    qkv_maps = jnp.concatenate(
        [
            block_of(query_adapter_outmaps, 0, 2 * kv_local),
            block_of(key_adapter_outmaps, q_local, kv_local),
            block_of(value_adapter_outmaps, q_local + kv_local, 0),
        ],
        axis=0,
    )
    attention_pack = jnp.concatenate(
        [
            table[:, at : at + features]
            for table in (qkv_local, qkv_maps)
            for at in range(0, wide, features)
        ],
        axis=0,
    )
    attention_weights = lax.all_gather(attention_pack, PLANE, axis=0, tiled=True).reshape(
        cols, rows, -1, features
    )
    o_rows = output_matrix.shape[0]
    ffn_half = gate_matrix.shape[1] // 2
    half_start = plane * ffn_half
    chunks = 2 if ffn_half % 256 == 0 else 3
    width = ffn_half // chunks
    slabs = width // LANES

    def plates(table):
        return [table[:, at : at + LANES] for at in range(0, table.shape[1], LANES)]

    def half_of(table):
        return lax.dynamic_slice_in_dim(table, half_start, ffn_half, 1)

    map_width = max(ffn_half, o_rows)

    def to_width(table):
        return jnp.pad(table, ((0, 0), (0, map_width - table.shape[1])))

    col_pack = jnp.concatenate(
        [
            *[to_width(half_of(outmap(gate_adapter_outmaps, a))) for a in both],
            *[to_width(half_of(outmap(up_adapter_outmaps, a))) for a in both],
            *[to_width(half_of(inmap(down_adapter_inmaps, a).T)) for a in both],
            to_width(inmap(output_adapter_inmaps, own_adapter).T),
            jnp.zeros((rank, map_width), BF),
        ],
        axis=0,
    )
    map_rows = col_pack.shape[0] // rows
    map_plates = plates(lax.dynamic_slice_in_dim(col_pack, row * map_rows, map_rows, 0))
    ffn_weights = []
    for chunk in range(chunks):
        pack = []
        for slab in range(slabs):
            start = half_start + (chunk * slabs + slab) * LANES
            pack.append(lax.dynamic_slice_in_dim(gate_matrix, start, LANES, 1))
            pack.append(lax.dynamic_slice_in_dim(up_matrix, start, LANES, 1))
            pack.extend(plates(lax.dynamic_slice_in_dim(down_matrix, start, LANES, 0)))
        if chunk == 0:
            spare = features - map_rows * len(map_plates)
            for plate in plates(output_matrix):
                pack.append(jnp.pad(plate, ((0, features - o_rows), (0, 0))))
            pack = pack + map_plates + [jnp.zeros((spare, LANES), BF)]
        pack = jnp.concatenate(pack, axis=0)
        ffn_weights.append(
            lax.all_gather(pack, PLANE, axis=0, tiled=True).reshape(
                cols, rows, -1, features, LANES
            )
        )
    o_unit = 3 * slabs
    col_maps = ffn_weights[0][:, :, -1, : map_rows * len(map_plates)].reshape(
        cols, rows, len(map_plates), map_rows, LANES
    )
    col_maps = jnp.transpose(col_maps, (0, 2, 1, 3, 4)).reshape(
        cols, len(map_plates), rows * map_rows, LANES
    )
    in_o = jnp.transpose(col_maps[:, : o_rows // LANES, 6 * rank : 7 * rank], (0, 2, 1, 3))
    in_o = row_pad(in_o.reshape(cols, rank, o_rows))

    row_pack = jnp.concatenate(
        [
            inmap(query_adapter_inmaps, own_adapter),
            inmap(key_adapter_inmaps, own_adapter),
            inmap(value_adapter_inmaps, own_adapter),
            *[inmap(gate_adapter_inmaps, a) for a in both],
            *[inmap(up_adapter_inmaps, a) for a in both],
            *[outmap(down_adapter_outmaps, a).T for a in both],
            outmap(output_adapter_outmaps, own_adapter).T,
            *thirds(attention_norm_gain),
            *thirds(feedfwd_norm_gain),
        ],
        axis=1,
    )

    row_maps = lax.all_gather(row_pack, "row", axis=0, tiled=True)
    in_qkv = row_maps[:, : 3 * rank]
    in_gate = row_maps[:, 3 * rank : 5 * rank]
    in_up = row_maps[:, 5 * rank : 7 * rank]
    out_down = row_maps[:, 7 * rank : 9 * rank]
    out_o = lane_pad(row_maps[:, 9 * rank : 10 * rank])
    gain_parts = row_maps[:, 10 * rank :].astype(F32)
    gain_one = (gain_parts[:, 0] + (gain_parts[:, 1] + gain_parts[:, 2])).reshape(1, -1)
    gain_two = (gain_parts[:, 3] + (gain_parts[:, 4] + gain_parts[:, 5])).reshape(1, -1)

    own_tokens = lax.all_to_all(tokens, "row", 0, 1, tiled=True)
    own_cotangent = lax.all_to_all(cotangent, "row", 0, 1, tiled=True)
    other_cotangent = lax.ppermute(own_cotangent, "dp", swap)
    head_gains = jnp.stack([query_norm_gain, key_norm_gain], axis=0)
    token_start = (col * rows + row) * own
    positions = lax.dynamic_slice_in_dim(depth, token_start, own, 0).astype(F32)
    half = HEAD_SIZE // 2
    freqs = THETA ** (-2.0 * jnp.arange(half).astype(F32) / HEAD_SIZE)
    angle = positions[:, None] * freqs[None, :]
    cosine = jnp.tile(jnp.cos(angle), (1, 2))
    sine = jnp.concatenate([-jnp.sin(angle), jnp.sin(angle)], axis=1)

    masked_qkv, pre, sent = qkv_forward(
        own_tokens, gain_one, in_qkv, cosine, sine, head_gains, attention_weights
    )

    def to_heads(sent):
        if repeat > 1:
            sent = jnp.repeat(sent, repeat, axis=0)
        return lax.all_to_all(sent, PLANE, 0, 0, tiled=True).reshape(length, sent.shape[2])

    def to_tokens(lines):
        got = lax.all_to_all(
            lines.reshape(devices, own, lines.shape[1]), PLANE, 0, 0, tiled=True
        )
        return got[::repeat] if repeat > 1 else got

    got = to_heads(sent)
    theirs = lax.ppermute(got[:, HEAD_SIZE:], "row", pairs)
    flag = (1 - (row // repeat) % 2).astype(jnp.int32).reshape(1)

    block_node = segment.reshape(-1, SEG_LEN)[:, 0]
    nodes = jnp.arange(parent.shape[1])
    node_parent = jnp.sum(jnp.where(block_node[:, None] == nodes, parent.reshape(1, -1), 0), axis=1)
    block_index = jnp.arange(block_node.shape[0])
    parent_block = jnp.max(
        jnp.where(node_parent[:, None] == block_node[None, :], block_index[None, :], 0), axis=1
    )
    parent_block = jnp.where(node_parent > 0, parent_block, -1).astype(jnp.int32)
    head_attended, head_low, totals = attention_forward(parent_block, flag, got, theirs)
    attended = to_tokens(head_low)

    middle, hidden_ffn, masked_o = output_forward(
        attended, own_tokens, gain_two, in_o, out_o, ffn_weights[0], o_unit
    )

    other_ffn = lax.ppermute(hidden_ffn, "dp", swap)
    tables = (in_gate, in_up, out_down)
    column_tree = jnp.arange(2 * rank)[None, :] // rank

    def masks_of(hidden, cot, tree):
        mask = jnp.broadcast_to((column_tree == tree).astype(F32), (own, 2 * rank))
        return (
            (dot(hidden, in_gate) * mask).astype(BF),
            (dot(hidden, in_up) * mask).astype(BF),
            (ADAPTER_FACTOR * dot(cot, out_down) * mask).astype(BF),
            mask,
        )

    parts = []

    def run(chunk, side, masks, accs):
        hidden, cot = side
        maps = col_maps[:, chunk * slabs : (chunk + 1) * slabs].reshape(cols * slabs, -1, LANES)
        last = chunk == chunks - 1
        return feed_forward_chunk(
            hidden,
            cot,
            masks,
            tables,
            ffn_weights[chunk],
            maps,
            accs,
            last,
            F32 if side is own_side else BF,
        )

    own_side = (hidden_ffn, own_cotangent)
    own_masks = masks_of(*own_side, 0)
    here, own_part = run(0, own_side, own_masks, None)
    other_ffn, here = lax.optimization_barrier((other_ffn, here))
    other_side = (other_ffn, other_cotangent)
    other_masks = masks_of(*other_side, 1)
    there, other_part = run(0, other_side, other_masks, None)
    parts = [(own_part, other_part)]
    for chunk in range(1, chunks):
        there, other_part = run(chunk, other_side, other_masks, there)
        here, own_part = run(chunk, own_side, own_masks, here)
        parts.append((own_part, other_part))

    def slab_order(part):
        even, odd = (part[0][i] + part[1][i] for i in range(2))
        part = jnp.stack([even, odd], axis=1).reshape(cols, slabs, 6 * rank, LANES)
        return jnp.transpose(part, (0, 2, 1, 3)).reshape(cols, 6 * rank, width)

    parts = [slab_order(part) for part in parts]
    gh_other = lax.ppermute(there[0], "dp", swap)

    grad_middle, sent, grad_o_rows, grad_o_cols = output_backward(
        here[0],
        gh_other,
        own_cotangent,
        middle,
        gain_two,
        in_o,
        out_o,
        attended,
        masked_o,
        ffn_weights[0],
        o_unit,
    )
    out_sent, sent = lax.optimization_barrier((there[1], sent))
    out_other = lax.ppermute(out_sent, "dp", swap)
    head_grad = to_heads(sent)

    row_mid = jnp.concatenate([here[2] + there[2], grad_o_rows], axis=1).reshape(-1, features)

    def to_map_width(table):
        return jnp.pad(table, ((0, 0), (0, 0), (0, map_width - table.shape[2])))

    col_mid = jnp.concatenate(
        [to_map_width(jnp.concatenate(parts, axis=2)), to_map_width(grad_o_cols)], axis=1
    ).reshape(-1, map_width)
    head_grad, row_mid, col_mid = lax.optimization_barrier((head_grad, row_mid, col_mid))
    row_mid = lax.psum_scatter(row_mid, "row", scatter_dimension=0, tiled=True)
    col_mid = lax.psum_scatter(col_mid, "col", scatter_dimension=0, tiled=True)

    lines, kept, given = attention_backward(
        parent_block, flag, got, head_grad, head_attended, totals, theirs
    )
    lines, kept, given, row_mid, col_mid, out_other = lax.optimization_barrier(
        (lines, kept, given, row_mid, col_mid, out_other)
    )
    returned = to_tokens(merge(lines, kept, lax.ppermute(given, "row", pairs)))
    output = (middle + here[1] + out_other.astype(F32)).astype(BF)
    row_mid = summed(row_mid, "col")
    col_mid = summed(col_mid, "row")
    row_got, col_got = lax.ppermute((row_mid, col_mid), "dp", swap)
    returned, row_mid, col_mid, row_got, col_got, output = lax.optimization_barrier(
        (returned, row_mid, col_mid, row_got, col_got, output)
    )
    output = lax.all_to_all(output, "row", 1, 0, tiled=True)

    grads_qkv, inner_qkv, row_end, col_end = qkv_unshape(
        returned,
        pre,
        masked_qkv,
        own_tokens,
        gain_one,
        cosine,
        sine,
        head_gains,
        attention_weights,
    )
    grad_low = qkv_backward(
        grads_qkv, inner_qkv, own_tokens, grad_middle, gain_one, in_qkv, attention_weights
    )
    grad_low, output = lax.optimization_barrier((grad_low, output))
    input_gradient = lax.all_to_all(grad_low, "row", 1, 0, tiled=True).astype(F32)
    row_end = summed(summed_block(row_end, "row"), "col")
    col_end = summed(summed_block(col_end, "col"), "row")
    row_end_got, col_end_got = lax.ppermute((row_end, col_end), "dp", swap)

    def placed(first, second):
        return place(first, own_adapter, second, other_adapter, columns)

    def row_sum(at):
        first = row_mid[at : at + rank] + row_got[at + rank : at + 2 * rank]
        second = row_mid[at + rank : at + 2 * rank] + row_got[at : at + rank]
        return placed(first, second)

    grad_a_gate = row_sum(0).T
    grad_a_up = row_sum(2 * rank).T
    grad_b_down = row_sum(4 * rank)
    grad_b_o = placed(row_mid[6 * rank :], row_got[6 * rank :])
    at = 6 * rank
    grad_a_o = placed(col_mid[at:, :o_rows], col_got[at:, :o_rows]).T

    def ffn_placed(kind):
        at = 2 * rank * kind
        mine = placed(col_mid[at : at + rank], col_mid[at + rank : at + 2 * rank])
        theirs = placed(col_got[at + rank : at + 2 * rank], col_got[at : at + rank])
        low = jnp.where(plane == 0, mine, theirs)
        high = jnp.where(plane == 0, theirs, mine)
        return jnp.concatenate([low[:, :ffn_half], high[:, :ffn_half]], axis=1)

    grad_b_gate = ffn_placed(0)
    grad_b_up = ffn_placed(1)
    grad_a_down = ffn_placed(2).T

    grad_a_q, grad_a_k, grad_a_v = (
        placed(row_end[i * rank : (i + 1) * rank], row_end_got[i * rank : (i + 1) * rank]).T
        for i in range(3)
    )
    grad_b = placed(col_end, col_end_got)
    grad_b_q = grad_b[:, :q_local]
    grad_b_k = grad_b[:, q_local : q_local + kv_local]
    grad_b_v = grad_b[:, q_local + kv_local :]

    return (
        output,
        input_gradient,
        grad_a_q,
        grad_b_q,
        grad_a_k,
        grad_b_k,
        grad_a_v,
        grad_b_v,
        grad_a_o,
        grad_b_o,
        grad_a_gate,
        grad_b_gate,
        grad_a_up,
        grad_b_up,
        grad_a_down,
        grad_b_down,
    )


def solution(mesh):
    return jax.shard_map(
        on_device,
        mesh=mesh,
        in_specs=(
            P(("dp", "col"), "row"),
            P(("dp", "col"), "row"),
            P("row"),
            P("row"),
            P(),
            P(),
            P("row", "col"),
            P("row", "col"),
            P("row", "col"),
            P("col", "row"),
            P("row", "col"),
            P("row", "col"),
            P("col", "row"),
            P("row", None),
            P(None, "col"),
            P("row", None),
            P(None, "col"),
            P("row", None),
            P(None, "col"),
            P("col", None),
            P(None, "row"),
            P("row", None),
            P(None, "col"),
            P("row", None),
            P(None, "col"),
            P("col", None),
            P(None, "row"),
            P("dp"),
            P("dp"),
            P("dp", None),
            P("dp"),
        ),
        out_specs=(
            P(("dp", "col"), "row"),
            P(("dp", "col"), "row"),
            P("row", None),
            P(None, "col"),
            P("row", None),
            P(None, "col"),
            P("row", None),
            P(None, "col"),
            P("col", None),
            P(None, "row"),
            P("row", None),
            P(None, "col"),
            P("row", None),
            P(None, "col"),
            P("col", None),
            P(None, "row"),
        ),
        check_vma=False,
    )
```

```python
import functools
import math

import jax
import jax.numpy as jnp
from jax import lax
from jax.experimental import pallas as pl
from jax.experimental.pallas import tpu as pltpu
from jax.sharding import PartitionSpec as P

MODEL_WIDTH = 2048
QUERY_HEADS = 16
KEY_VALUE_HEADS = 8
HEAD_SIZE = 128
ADAPTER_RANK = 16
TREE_LEN = 5120
TRUNK = 2048
SEG_LEN = 256
QUERY_BLOCK = 512
KEY_BLOCK = 1024

EPSILON = 1e-06
THETA = 1000000.0
ADAPTER_FACTOR = 2.0
BF = jnp.bfloat16
F32 = jnp.float32
SCALE = HEAD_SIZE ** (-0.5)
SCALE_LOG2 = SCALE * math.log2(math.e)
PLANE = ("col", "row")
LANES = 128
VMEM_LIMIT = 63 * 1024 * 1024


def dot(left, right):
    return jnp.dot(left, right, preferred_element_type=F32)


def dot_nt(left, right):
    return lax.dot_general(left, right, (((1,), (1,)), ((), ())), preferred_element_type=F32)


def dot_tn(left, right):
    return lax.dot_general(left, right, (((0,), (0,)), ((), ())), preferred_element_type=F32)


def walk_keys(index, parent_ref, step):
    trunk_blocks = TRUNK // QUERY_BLOCK

    @pl.when(index < trunk_blocks)
    def _():
        @pl.loop(0, index)
        def _(block):
            step(pl.multiple_of(block * QUERY_BLOCK, QUERY_BLOCK), QUERY_BLOCK)

        step(pl.multiple_of(index * QUERY_BLOCK, QUERY_BLOCK), QUERY_BLOCK, causal=True)

    @pl.when(index >= trunk_blocks)
    def _():
        for part in range(TRUNK // KEY_BLOCK):
            step(part * KEY_BLOCK, KEY_BLOCK)
        for side in range(QUERY_BLOCK // SEG_LEN):
            block = index * (QUERY_BLOCK // SEG_LEN) + side
            first = side * SEG_LEN
            start = pl.multiple_of(block * SEG_LEN, SEG_LEN)
            step(start, SEG_LEN, first, SEG_LEN, True)
            above = parent_ref[block]

            @pl.when(above >= 0)
            def _():
                step(pl.multiple_of(above * SEG_LEN, SEG_LEN), SEG_LEN, first, SEG_LEN)


def attention_forward_kernel(
    parent_ref, flag_ref, q_ref, mine_ref, theirs_ref, o_ref, low_ref, l_ref, k_ref, v_ref, acc_ref
):
    index = pl.program_id(0)

    @pl.when(index == 0)
    def _():
        lane = lax.broadcasted_iota(jnp.int32, (v_ref.shape[0], HEAD_SIZE), 1)
        v_ref[:, HEAD_SIZE:] = jnp.where(lane == 0, 1.0, 0.0).astype(BF)

        @pl.when(flag_ref[0] == 1)
        def _():
            k_ref[...] = mine_ref[...]
            v_ref[:, :HEAD_SIZE] = theirs_ref[...]

        @pl.when(flag_ref[0] != 1)
        def _():
            k_ref[...] = theirs_ref[...]
            v_ref[:, :HEAD_SIZE] = mine_ref[...]

    acc_ref[...] = jnp.zeros_like(acc_ref)

    def step(start, size, first=0, count=QUERY_BLOCK, causal=False):
        rows = pl.ds(start, size)
        at = pl.ds(first, count)
        scores = dot_nt(q_ref[at, :], k_ref[rows, :])
        probs = jnp.exp2(scores * SCALE_LOG2)
        if causal:
            ahead = lax.broadcasted_iota(jnp.int32, probs.shape, 0)
            behind = lax.broadcasted_iota(jnp.int32, probs.shape, 1)
            probs = jnp.where(behind <= ahead, probs, 0.0)
        acc_ref[at, :] += dot(probs.astype(BF), v_ref[rows, :])

    walk_keys(index, parent_ref, step)
    total = acc_ref[:, HEAD_SIZE : HEAD_SIZE + 1]
    attended = acc_ref[:, :HEAD_SIZE] / total
    o_ref[...] = attended
    low_ref[...] = attended.astype(BF)
    spread = jnp.broadcast_to(total, (QUERY_BLOCK, LANES))
    l_ref[0] = jnp.transpose(spread)[:8, :]


def attention_forward(parent_block, flag, got, theirs):
    length = theirs.shape[0]
    blocks = length // QUERY_BLOCK
    whole = lambda i, p, f: (0, 0)
    part = lambda i, p, f: (i, 0)
    return pl.pallas_call(
        attention_forward_kernel,
        grid_spec=pltpu.PrefetchScalarGridSpec(
            num_scalar_prefetch=2,
            grid=(blocks,),
            in_specs=[
                pl.BlockSpec((QUERY_BLOCK, HEAD_SIZE), part),
                pl.BlockSpec((length, HEAD_SIZE), lambda i, p, f: (0, 1)),
                pl.BlockSpec((length, HEAD_SIZE), whole),
            ],
            out_specs=[
                pl.BlockSpec((QUERY_BLOCK, HEAD_SIZE), part),
                pl.BlockSpec((QUERY_BLOCK, HEAD_SIZE), part),
                pl.BlockSpec((1, 8, QUERY_BLOCK), lambda i, p, f: (i, 0, 0)),
            ],
            scratch_shapes=[
                pltpu.VMEM((length, HEAD_SIZE), BF),
                pltpu.VMEM((length, 2 * HEAD_SIZE), BF),
                pltpu.VMEM((QUERY_BLOCK, 2 * HEAD_SIZE), F32),
            ],
        ),
        out_shape=[
            jax.ShapeDtypeStruct((length, HEAD_SIZE), F32),
            jax.ShapeDtypeStruct((length, HEAD_SIZE), BF),
            jax.ShapeDtypeStruct((blocks, 8, QUERY_BLOCK), F32),
        ],
        compiler_params=pltpu.CompilerParams(vmem_limit_bytes=VMEM_LIMIT),
        cost_estimate=pl.CostEstimate(
            flops=160 * SEG_LEN * SEG_LEN * HEAD_SIZE * 4,
            bytes_accessed=length * HEAD_SIZE * 12,
            transcendentals=160 * SEG_LEN * SEG_LEN,
        ),
        name="attention_forward",
    )(parent_block, flag, got, got, theirs)


def attention_backward_kernel(
    parent_ref,
    flag_ref,
    q_ref,
    g_ref,
    o_ref,
    l_ref,
    mine_ref,
    theirs_ref,
    dq_ref,
    kept_ref,
    given_ref,
    k_ref,
    v_ref,
    kt_ref,
    dk_ref,
    dv_ref,
    acc_ref,
    delta_ref,
    inverse_ref,
):
    index = pl.program_id(0)

    @pl.when(index == 0)
    def _():
        dk_ref[...] = jnp.zeros_like(dk_ref)
        dv_ref[...] = jnp.zeros_like(dv_ref)

        @pl.when(flag_ref[0] == 1)
        def _():
            k_ref[...] = mine_ref[...]
            v_ref[...] = theirs_ref[...]

        @pl.when(flag_ref[0] != 1)
        def _():
            k_ref[...] = theirs_ref[...]
            v_ref[...] = mine_ref[...]

        @pl.loop(0, k_ref.shape[0] // SEG_LEN)
        def _(block):
            rows = pl.ds(pl.multiple_of(block * SEG_LEN, SEG_LEN), SEG_LEN)
            kt_ref[:, rows] = jnp.transpose(k_ref[rows, :])

    delta = jnp.sum(g_ref[...].astype(F32) * o_ref[...], axis=1, keepdims=True)
    delta_ref[...] = jnp.transpose(jnp.broadcast_to(delta, (QUERY_BLOCK, LANES)))[:8, :]
    inverse_ref[...] = 1.0 / l_ref[0]
    acc_ref[...] = jnp.zeros_like(acc_ref)

    def step(start, size, first=0, count=QUERY_BLOCK, causal=False):
        rows = pl.ds(start, size)
        at = pl.ds(first, count)
        query = q_ref[at, :]
        grad = g_ref[at, :]
        probs = jnp.exp2(dot_nt(k_ref[rows, :], query) * SCALE_LOG2) * inverse_ref[:1, at]
        if causal:
            behind = lax.broadcasted_iota(jnp.int32, probs.shape, 0)
            ahead = lax.broadcasted_iota(jnp.int32, probs.shape, 1)
            probs = jnp.where(behind <= ahead, probs, 0.0)
        dprobs = dot_nt(v_ref[rows, :], grad)
        dscores = (probs * (dprobs - delta_ref[:1, at])).astype(BF)
        dv_ref[rows, :] += dot(probs.astype(BF), grad)
        dk_ref[rows, :] += dot(dscores, query)
        acc_ref[:, at] += dot(kt_ref[:, rows], dscores)

    walk_keys(index, parent_ref, step)
    dq_ref[...] = (jnp.transpose(acc_ref[...]) * SCALE).astype(BF)

    @pl.when(index == pl.num_programs(0) - 1)
    def _():
        @pl.when(flag_ref[0] == 1)
        def _():
            kept_ref[...] = dk_ref[...] * SCALE
            given_ref[...] = dv_ref[...].astype(BF)

        @pl.when(flag_ref[0] != 1)
        def _():
            kept_ref[...] = dv_ref[...]
            given_ref[...] = (dk_ref[...] * SCALE).astype(BF)


def attention_backward(parent_block, flag, got, grad, attended, totals, theirs):
    length = theirs.shape[0]
    blocks = length // QUERY_BLOCK
    whole = lambda i, p, f: (0, 0)
    part = lambda i, p, f: (i, 0)
    return pl.pallas_call(
        attention_backward_kernel,
        grid_spec=pltpu.PrefetchScalarGridSpec(
            num_scalar_prefetch=2,
            grid=(blocks,),
            in_specs=[
                pl.BlockSpec((QUERY_BLOCK, HEAD_SIZE), part),
                pl.BlockSpec((QUERY_BLOCK, HEAD_SIZE), part),
                pl.BlockSpec((QUERY_BLOCK, HEAD_SIZE), part),
                pl.BlockSpec((1, 8, QUERY_BLOCK), lambda i, p, f: (i, 0, 0)),
                pl.BlockSpec((length, HEAD_SIZE), lambda i, p, f: (0, 1)),
                pl.BlockSpec((length, HEAD_SIZE), whole),
            ],
            out_specs=[
                pl.BlockSpec((QUERY_BLOCK, HEAD_SIZE), part),
                pl.BlockSpec((length, HEAD_SIZE), whole),
                pl.BlockSpec((length, HEAD_SIZE), whole),
            ],
            scratch_shapes=[
                pltpu.VMEM((length, HEAD_SIZE), BF),
                pltpu.VMEM((length, HEAD_SIZE), BF),
                pltpu.VMEM((HEAD_SIZE, length), BF),
                pltpu.VMEM((length, HEAD_SIZE), F32),
                pltpu.VMEM((length, HEAD_SIZE), F32),
                pltpu.VMEM((HEAD_SIZE, QUERY_BLOCK), F32),
                pltpu.VMEM((8, QUERY_BLOCK), F32),
                pltpu.VMEM((8, QUERY_BLOCK), F32),
            ],
        ),
        out_shape=[
            jax.ShapeDtypeStruct((length, 2 * HEAD_SIZE), BF),
            jax.ShapeDtypeStruct((length, HEAD_SIZE), F32),
            jax.ShapeDtypeStruct((length, HEAD_SIZE), BF),
        ],
        compiler_params=pltpu.CompilerParams(vmem_limit_bytes=VMEM_LIMIT),
        cost_estimate=pl.CostEstimate(
            flops=160 * SEG_LEN * SEG_LEN * HEAD_SIZE * 10,
            bytes_accessed=length * HEAD_SIZE * 24,
            transcendentals=160 * SEG_LEN * SEG_LEN,
        ),
        name="attention_backward",
    )(parent_block, flag, got, grad, attended, totals, got, theirs)


def merge_kernel(lines_ref, kept_ref, got_ref, out_ref):
    out_ref[...] = (kept_ref[...] + got_ref[...].astype(F32)).astype(BF)


def merge(lines, kept, got):
    length = kept.shape[0]
    rows = 4 * SEG_LEN
    part = pl.BlockSpec((rows, HEAD_SIZE), lambda i: (i, 0))
    return pl.pallas_call(
        merge_kernel,
        grid=(length // rows,),
        in_specs=[pl.BlockSpec(memory_space=pl.ANY), part, part],
        out_specs=pl.BlockSpec((rows, HEAD_SIZE), lambda i: (i, 1)),
        out_shape=jax.ShapeDtypeStruct(lines.shape, lines.dtype),
        input_output_aliases={0: 0},
        cost_estimate=pl.CostEstimate(
            flops=length * HEAD_SIZE, bytes_accessed=length * HEAD_SIZE * 10, transcendentals=0
        ),
        name="merge",
    )(lines, kept, got)


def norm_scale(values):
    return lax.rsqrt(jnp.mean(values * values, axis=1, keepdims=True) + EPSILON)


def norm_back(values, scale, gain, gradient):
    weighted = gain * gradient
    inner_sum = jnp.sum(weighted * values, axis=1, keepdims=True)
    return scale * weighted - values * (scale**3 * (inner_sum * (1.0 / MODEL_WIDTH)))


def outmaps_of(w_ref, pieces, piece, used):
    at = pieces * piece
    return jnp.concatenate(
        [w_ref[0, 0, at + p * used : at + (p + 1) * used, :] for p in range(pieces)], axis=1
    )


def qkv_forward_kernel(
    x_ref,
    gain_ref,
    a_ref,
    cos_ref,
    sin_ref,
    hg_ref,
    w_ref,
    m_ref,
    pre_ref,
    sent_ref,
    hidden_ref,
):
    row_blocks = w_ref.shape[1]
    piece = w_ref.shape[3]
    pieces = w_ref.shape[2] // piece
    heads = sent_ref.shape[0]
    used = m_ref.shape[1]

    @pl.when(pl.program_id(0) == 0)
    def _():
        resid = x_ref[...].astype(F32)
        hidden_ref[...] = (resid * norm_scale(resid) * gain_ref[...]).astype(BF)
        m_ref[...] = dot(hidden_ref[...], a_ref[...]).astype(BF)

    hidden = hidden_ref[...]
    whole = jnp.concatenate(
        [
            dot(
                hidden,
                jnp.concatenate(
                    [w_ref[0, r, p * piece : (p + 1) * piece, :] for r in range(row_blocks)], axis=0
                ),
            )
            for p in range(pieces)
        ],
        axis=1,
    ) + ADAPTER_FACTOR * dot(m_ref[...], outmaps_of(w_ref, pieces, piece, used))
    pre_ref[0] = whole[:, : pre_ref.shape[2]]
    cosine = cos_ref[...]
    sine = sin_ref[...]

    def shaped(at, gain):
        lines = whole[:, at : at + HEAD_SIZE]
        normed = lines * norm_scale(lines) * gain
        return (normed * cosine + pltpu.roll(normed, HEAD_SIZE // 2, 1) * sine).astype(BF)

    for head in range(heads):
        sent_ref[head, :, :HEAD_SIZE] = shaped(head * HEAD_SIZE, hg_ref[0:1, :])
    key_at = heads * HEAD_SIZE
    value_at = key_at + heads // 2 * HEAD_SIZE
    for pair in range(heads // 2):
        at = pair * HEAD_SIZE
        sent_ref[2 * pair, :, HEAD_SIZE:] = shaped(key_at + at, hg_ref[1:2, :])
        sent_ref[2 * pair + 1, :, HEAD_SIZE:] = whole[
            :, value_at + at : value_at + at + HEAD_SIZE
        ].astype(BF)


def qkv_forward(x, gain, inmaps, cosine, sine, head_gains, weights):
    own = x.shape[0]
    cols, row_blocks, tall, piece = weights.shape
    wide = tall // piece * piece
    used = inmaps.shape[1]
    heads = QUERY_HEADS // cols
    whole = lambda c: (0, 0)
    step = lambda c: (c, 0, 0)
    return pl.pallas_call(
        qkv_forward_kernel,
        grid=(cols,),
        in_specs=[
            pl.BlockSpec(x.shape, whole),
            pl.BlockSpec(gain.shape, whole),
            pl.BlockSpec(inmaps.shape, whole),
            pl.BlockSpec(cosine.shape, whole),
            pl.BlockSpec(sine.shape, whole),
            pl.BlockSpec(head_gains.shape, whole),
            pl.BlockSpec((1, row_blocks, tall, piece), lambda c: (c, 0, 0, 0)),
        ],
        out_specs=[
            pl.BlockSpec((own, used), whole),
            pl.BlockSpec((1, own, wide * 3 // 4), step),
            pl.BlockSpec((heads, own, 2 * HEAD_SIZE), step),
        ],
        out_shape=[
            jax.ShapeDtypeStruct((own, used), BF),
            jax.ShapeDtypeStruct((cols, own, wide * 3 // 4), F32),
            jax.ShapeDtypeStruct((QUERY_HEADS, own, 2 * HEAD_SIZE), BF),
        ],
        scratch_shapes=[pltpu.VMEM((own, MODEL_WIDTH), BF)],
        compiler_params=pltpu.CompilerParams(vmem_limit_bytes=VMEM_LIMIT),
        cost_estimate=pl.CostEstimate(
            flops=2 * own * MODEL_WIDTH * cols * wide,
            bytes_accessed=cols * wide * MODEL_WIDTH * 2,
            transcendentals=own * cols * 8,
        ),
        name="qkv_forward",
    )(x, gain, inmaps, cosine, sine, head_gains, weights)


def qkv_unshape_kernel(
    ret_ref,
    pre_ref,
    m_ref,
    x_ref,
    gain_ref,
    cos_ref,
    sin_ref,
    hg_ref,
    w_ref,
    grads_ref,
    inner_ref,
    ga_ref,
    gb_ref,
    in_acc_ref,
):
    step = pl.program_id(0)
    row_blocks, used, piece = ga_ref.shape
    heads = ret_ref.shape[0]
    pieces = grads_ref.shape[2] // piece
    cosine = cos_ref[...]
    sine = sin_ref[...]

    @pl.when(step == 0)
    def _():
        in_acc_ref[...] = jnp.zeros_like(in_acc_ref)

    def unshaped(grad, at, gain):
        grad = grad.astype(F32)
        lines = pre_ref[0, :, at : at + HEAD_SIZE]
        turned = gain * (grad * cosine + pltpu.roll(grad * sine, HEAD_SIZE // 2, 1))
        scale = norm_scale(lines)
        inner_mean = jnp.mean(turned * lines, axis=1, keepdims=True)
        return (scale * turned - lines * (scale**3 * inner_mean)).astype(BF)

    parts = []
    for head in range(heads):
        parts.append(unshaped(ret_ref[head, :, :HEAD_SIZE], head * HEAD_SIZE, hg_ref[0:1, :]))
    for pair in range(heads // 2):
        at = (heads + pair) * HEAD_SIZE
        parts.append(unshaped(ret_ref[2 * pair, :, HEAD_SIZE:], at, hg_ref[1:2, :]))
    for pair in range(heads // 2):
        parts.append(ret_ref[2 * pair + 1, :, HEAD_SIZE:])
    grads = jnp.concatenate(parts, axis=1)
    grads_ref[0] = grads
    outmaps = jnp.concatenate(
        [w_ref[0, 0, p * used : (p + 1) * used, :] for p in range(pieces)], axis=1
    )
    in_acc_ref[...] += dot_nt(grads, outmaps)
    outer = ADAPTER_FACTOR * dot_tn(m_ref[...], grads)
    rank = ADAPTER_RANK
    edges = (0, heads * HEAD_SIZE, heads * HEAD_SIZE * 3 // 2, heads * HEAD_SIZE * 2)
    for i in range(3):
        gb_ref[0, :, edges[i] : edges[i + 1]] = outer[
            i * rank : (i + 1) * rank, edges[i] : edges[i + 1]
        ]

    @pl.when(step == pl.num_programs(0) - 1)
    def _():
        inner = (ADAPTER_FACTOR * in_acc_ref[...]).astype(BF)
        inner_ref[...] = inner
        resid = x_ref[...].astype(F32)
        hidden = (resid * norm_scale(resid) * gain_ref[...]).astype(BF)
        for r in range(row_blocks):
            ga_ref[r] = dot_tn(inner, hidden[:, r * piece : (r + 1) * piece])


def qkv_unshape(returned, pre, masked, x, gain, cosine, sine, head_gains, weights):
    own = x.shape[0]
    cols, row_blocks, tall, piece = weights.shape
    pieces = tall // piece
    wide = pieces * piece
    heads = QUERY_HEADS // cols
    used = 3 * ADAPTER_RANK
    map_rows = tall - wide
    at = wide // map_rows if wide % map_rows == 0 else None
    maps = weights[:, :1, wide:] if at is None else weights
    first = 0 if at is None else at
    whole = lambda c: (0, 0)
    step = lambda c: (c, 0, 0)
    return pl.pallas_call(
        qkv_unshape_kernel,
        grid=(cols,),
        in_specs=[
            pl.BlockSpec((heads, own, 2 * HEAD_SIZE), step),
            pl.BlockSpec((1, own, pre.shape[2]), step),
            pl.BlockSpec(masked.shape, whole),
            pl.BlockSpec(x.shape, whole),
            pl.BlockSpec(gain.shape, whole),
            pl.BlockSpec(cosine.shape, whole),
            pl.BlockSpec(sine.shape, whole),
            pl.BlockSpec(head_gains.shape, whole),
            pl.BlockSpec((1, 1, map_rows, piece), lambda c: (c, 0, first, 0)),
        ],
        out_specs=[
            pl.BlockSpec((1, own, wide), step),
            pl.BlockSpec((own, used), whole),
            pl.BlockSpec((row_blocks, used, piece), lambda c: (0, 0, 0)),
            pl.BlockSpec((1, ADAPTER_RANK, wide), step),
        ],
        out_shape=[
            jax.ShapeDtypeStruct((cols, own, wide), BF),
            jax.ShapeDtypeStruct((own, used), BF),
            jax.ShapeDtypeStruct((row_blocks, used, piece), F32),
            jax.ShapeDtypeStruct((cols, ADAPTER_RANK, wide), F32),
        ],
        scratch_shapes=[pltpu.VMEM((own, used), F32)],
        compiler_params=pltpu.CompilerParams(vmem_limit_bytes=VMEM_LIMIT),
        cost_estimate=pl.CostEstimate(
            flops=4 * own * 64 * cols * wide,
            bytes_accessed=cols * own * wide * 8,
            transcendentals=own * cols * 8,
        ),
        name="qkv_unshape",
    )(returned, pre, masked, x, gain, cosine, sine, head_gains, maps)


def qkv_backward_kernel(
    grads_ref, inner_ref, x_ref, gm_ref, gain_ref, a_ref, w_ref, grad_ref, acc_ref
):
    step = pl.program_id(0)
    row_blocks = w_ref.shape[1]
    piece = w_ref.shape[3]
    pieces = w_ref.shape[2] // piece

    @pl.when(step == 0)
    def _():
        acc_ref[...] = dot_nt(inner_ref[...], a_ref[...])

    for r in range(row_blocks):
        weights = jnp.concatenate(
            [w_ref[0, r, p * piece : (p + 1) * piece, :] for p in range(pieces)], axis=1
        )
        acc_ref[:, r * piece : (r + 1) * piece] += dot_nt(grads_ref[0], weights)

    @pl.when(step == pl.num_programs(0) - 1)
    def _():
        resid = x_ref[...].astype(F32)
        grad_ref[...] = (
            gm_ref[...] + norm_back(resid, norm_scale(resid), gain_ref[...], acc_ref[...])
        ).astype(BF)


def qkv_backward(grads, inner, x, grad_middle, gain, inmaps, weights):
    own = x.shape[0]
    cols, row_blocks, tall, piece = weights.shape
    wide = tall // piece * piece
    whole = lambda c: (0, 0)
    once = pl.Buffered(1)
    return pl.pallas_call(
        qkv_backward_kernel,
        grid=(cols,),
        in_specs=[
            pl.BlockSpec((1, own, wide), lambda c: (c, 0, 0)),
            pl.BlockSpec(inner.shape, whole),
            pl.BlockSpec(x.shape, whole, pipeline_mode=once),
            pl.BlockSpec(grad_middle.shape, whole, pipeline_mode=once),
            pl.BlockSpec(gain.shape, whole),
            pl.BlockSpec(inmaps.shape, whole),
            pl.BlockSpec((1, row_blocks, wide, piece), lambda c: (c, 0, 0, 0)),
        ],
        out_specs=pl.BlockSpec((own, MODEL_WIDTH), whole),
        out_shape=jax.ShapeDtypeStruct((own, MODEL_WIDTH), BF),
        scratch_shapes=[pltpu.VMEM((own, MODEL_WIDTH), F32)],
        compiler_params=pltpu.CompilerParams(vmem_limit_bytes=VMEM_LIMIT),
        cost_estimate=pl.CostEstimate(
            flops=2 * own * MODEL_WIDTH * cols * wide,
            bytes_accessed=cols * wide * MODEL_WIDTH * 2,
            transcendentals=own,
        ),
        name="qkv_backward",
    )(grads, inner, x, grad_middle, gain, inmaps, weights)


def whole_output_weights(flag_ref, own_ref, other_ref):
    own, other = (
        jnp.concatenate([ref[0, r] for r in range(ref.shape[1])], axis=1)
        for ref in (own_ref, other_ref)
    )
    first = flag_ref[0] == 0
    return jnp.concatenate(
        [jnp.where(first, own, other), jnp.where(first, other, own)], axis=0
    )


def output_forward_kernel(
    flag_ref,
    att_ref,
    x_ref,
    gain_ref,
    a_ref,
    b_ref,
    own_ref,
    other_ref,
    middle_ref,
    hidden_ref,
    m_ref,
    acc_ref,
    m_acc_ref,
):
    step = pl.program_id(0)
    heads = att_ref.shape[0]

    @pl.when(step == 0)
    def _():
        acc_ref[...] = x_ref[...].astype(F32)
        m_acc_ref[...] = jnp.zeros_like(m_acc_ref)

    attended = jnp.concatenate([att_ref[h] for h in range(heads)], axis=1)
    acc_ref[...] += dot(attended, whole_output_weights(flag_ref, own_ref, other_ref))
    m_acc_ref[...] += dot_nt(attended, a_ref[0])

    @pl.when(step == pl.num_programs(0) - 1)
    def _():
        masked = m_acc_ref[...].astype(BF)
        m_ref[...] = masked
        middle = acc_ref[...] + ADAPTER_FACTOR * dot_nt(masked, b_ref[...])
        middle_ref[...] = middle
        hidden_ref[...] = (middle * norm_scale(middle) * gain_ref[...]).astype(BF)


def output_forward(flag, attended, x, gain, inmaps, outmaps, weights):
    own = x.shape[0]
    cols = weights[0].shape[0]
    heads = QUERY_HEADS // cols
    o_rows = heads * HEAD_SIZE
    half = pl.BlockSpec((1, *weights[0].shape[1:]), lambda c: (c, 0, 0, 0))
    whole = lambda c: (0, 0)
    step = lambda c: (c, 0, 0)
    return pl.pallas_call(
        output_forward_kernel,
        grid=(cols,),
        in_specs=[
            pl.BlockSpec(memory_space=pltpu.SMEM),
            pl.BlockSpec((heads, own, HEAD_SIZE), step),
            pl.BlockSpec(x.shape, whole),
            pl.BlockSpec(gain.shape, whole),
            pl.BlockSpec((1, LANES, o_rows), step),
            pl.BlockSpec(outmaps.shape, whole),
            half,
            half,
        ],
        out_specs=[
            pl.BlockSpec((own, MODEL_WIDTH), whole),
            pl.BlockSpec((own, MODEL_WIDTH), whole),
            pl.BlockSpec((own, LANES), whole),
        ],
        out_shape=[
            jax.ShapeDtypeStruct((own, MODEL_WIDTH), F32),
            jax.ShapeDtypeStruct((own, MODEL_WIDTH), BF),
            jax.ShapeDtypeStruct((own, LANES), BF),
        ],
        scratch_shapes=[pltpu.VMEM((own, MODEL_WIDTH), F32), pltpu.VMEM((own, LANES), F32)],
        compiler_params=pltpu.CompilerParams(vmem_limit_bytes=VMEM_LIMIT),
        cost_estimate=pl.CostEstimate(
            flops=2 * own * MODEL_WIDTH * MODEL_WIDTH,
            bytes_accessed=2 * MODEL_WIDTH * MODEL_WIDTH,
            transcendentals=own,
        ),
        name="output_forward",
    )(flag, attended, x, gain, inmaps, outmaps, *weights)


def output_backward_kernel(
    flag_ref,
    gh_ref,
    got_ref,
    cot_ref,
    middle_ref,
    gain_ref,
    a_ref,
    b_ref,
    att_ref,
    m_ref,
    own_ref,
    other_ref,
    gm_ref,
    sent_ref,
    gb_ref,
    ga_ref,
    low_ref,
    inner_ref,
):
    heads = sent_ref.shape[0]
    row_blocks, rank, features = gb_ref.shape

    @pl.when(pl.program_id(0) == 0)
    def _():
        grad_hidden = gh_ref[...] + got_ref[...].astype(F32)
        middle = middle_ref[...]
        grad = cot_ref[...].astype(F32) + norm_back(
            middle, norm_scale(middle), gain_ref[...], grad_hidden
        )
        gm_ref[...] = grad
        low_ref[...] = grad.astype(BF)
        inner_ref[...] = (ADAPTER_FACTOR * dot(low_ref[...], b_ref[...])).astype(BF)
        outer = ADAPTER_FACTOR * dot_tn(m_ref[...], low_ref[...])
        for r in range(row_blocks):
            gb_ref[r] = outer[:rank, r * features : (r + 1) * features]

    attended = jnp.concatenate([att_ref[h] for h in range(heads)], axis=1)
    ga_ref[0] = dot_tn(inner_ref[...], attended)[:rank, :]
    weights = whole_output_weights(flag_ref, own_ref, other_ref)
    grad = (dot_nt(low_ref[...], weights) + dot(inner_ref[...], a_ref[0])).astype(BF)
    for head in range(heads):
        sent_ref[head] = grad[:, head * HEAD_SIZE : (head + 1) * HEAD_SIZE]


def output_backward(
    flag, grad_hidden, got, cotangent, middle, gain, inmaps, outmaps, attended, masked, weights
):
    own = middle.shape[0]
    cols, row_blocks = weights[0].shape[:2]
    features = MODEL_WIDTH // row_blocks
    heads = QUERY_HEADS // cols
    o_rows = heads * HEAD_SIZE
    half = pl.BlockSpec((1, *weights[0].shape[1:]), lambda c: (c, 0, 0, 0))
    whole = lambda c: (0, 0)
    step = lambda c: (c, 0, 0)
    once = pl.Buffered(1)
    return pl.pallas_call(
        output_backward_kernel,
        grid=(cols,),
        in_specs=[
            pl.BlockSpec(memory_space=pltpu.SMEM),
            pl.BlockSpec((own, MODEL_WIDTH), whole, pipeline_mode=once),
            pl.BlockSpec((own, MODEL_WIDTH), whole, pipeline_mode=once),
            pl.BlockSpec((own, MODEL_WIDTH), whole, pipeline_mode=once),
            pl.BlockSpec((own, MODEL_WIDTH), whole, pipeline_mode=once),
            pl.BlockSpec(gain.shape, whole),
            pl.BlockSpec((1, LANES, o_rows), step),
            pl.BlockSpec(outmaps.shape, whole),
            pl.BlockSpec((heads, own, HEAD_SIZE), step),
            pl.BlockSpec(masked.shape, whole),
            half,
            half,
        ],
        out_specs=[
            pl.BlockSpec((own, MODEL_WIDTH), whole),
            pl.BlockSpec((heads, own, HEAD_SIZE), step),
            pl.BlockSpec((row_blocks, ADAPTER_RANK, features), lambda c: (0, 0, 0)),
            pl.BlockSpec((1, ADAPTER_RANK, o_rows), step),
        ],
        out_shape=[
            jax.ShapeDtypeStruct((own, MODEL_WIDTH), F32),
            jax.ShapeDtypeStruct((QUERY_HEADS, own, HEAD_SIZE), BF),
            jax.ShapeDtypeStruct((row_blocks, ADAPTER_RANK, features), F32),
            jax.ShapeDtypeStruct((cols, ADAPTER_RANK, o_rows), F32),
        ],
        scratch_shapes=[pltpu.VMEM((own, MODEL_WIDTH), BF), pltpu.VMEM((own, LANES), BF)],
        compiler_params=pltpu.CompilerParams(vmem_limit_bytes=VMEM_LIMIT),
        cost_estimate=pl.CostEstimate(
            flops=2 * own * MODEL_WIDTH * MODEL_WIDTH,
            bytes_accessed=2 * MODEL_WIDTH * MODEL_WIDTH,
            transcendentals=own,
        ),
        name="output_backward",
    )(
        flag,
        grad_hidden,
        got,
        cotangent,
        middle,
        gain,
        inmaps,
        outmaps,
        attended,
        masked,
        *weights,
    )


def feed_forward_kernel(
    first, last, h_ref, c_ref, mg_ref, mu_ref, nd_ref, mask_ref, ag_ref, au_ref, od_ref, *refs
):
    weight_refs, map_refs, refs = refs[:2], refs[2:4], refs[4:]
    if first:
        previous = None
    else:
        previous, refs = refs[:5], refs[5:]
    if last:
        (gh_ref, out_ref, rows_ref), refs = refs[:3], refs[3:]
    else:
        accs, refs = refs[:5], refs[5:]
    grads_refs, refs = refs[:2], refs[2:]
    gh_acc, out_acc, md_acc, ig_acc, iu_acc = scratch = refs[:5]
    sems = refs[5]
    step = pl.program_id(0)
    row_blocks = weight_refs[0].shape[1]
    deep = MODEL_WIDTH // row_blocks
    used = mg_ref.shape[1]

    @pl.when(step == 0)
    def _():
        if first:
            for ref in scratch:
                ref[...] = jnp.zeros_like(ref)
        else:
            for i in range(5):
                pltpu.make_async_copy(previous[i], scratch[i], sems.at[i]).start()

    def side(kind, row):
        return jnp.concatenate([ref[0, row, kind] for ref in weight_refs], axis=1)

    def tall_side(kind):
        return jnp.concatenate([side(kind, row) for row in range(row_blocks)], axis=0)

    def down_side(row):
        return jnp.concatenate(
            [
                jnp.concatenate(
                    [ref[0, row, 2, at : at + LANES, :] for at in range(0, deep, LANES)], axis=1
                )
                for ref in weight_refs
            ],
            axis=0,
        )

    def maps(kind):
        return jnp.concatenate(
            [ref[0, kind * used : (kind + 1) * used, :] for ref in map_refs], axis=1
        )

    gate_map, up_map, down_map = maps(0), maps(1), maps(2)
    gate = dot(h_ref[...], tall_side(0)) + ADAPTER_FACTOR * dot(mg_ref[...], gate_map)
    upward = dot(h_ref[...], tall_side(1)) + ADAPTER_FACTOR * dot(mu_ref[...], up_map)
    down = jnp.concatenate([down_side(row) for row in range(row_blocks)], axis=1)
    grad_act = dot_nt(c_ref[...], down) + dot(nd_ref[...], down_map)
    sigma = 1.0 / (1.0 + jnp.exp(-gate))
    swish = gate * sigma
    act = (swish * upward).astype(BF)
    grad_gate = (grad_act * upward * (sigma * (1.0 + gate * (1.0 - sigma)))).astype(BF)
    grad_up = (grad_act * swish).astype(BF)
    both = jnp.concatenate([grad_gate, grad_up], axis=1)
    if not first:

        @pl.when(step == 0)
        def _():
            for i in range(5):
                pltpu.make_async_copy(previous[i], scratch[i], sems.at[i]).wait()

    for row in range(row_blocks):
        at = slice(row * deep, (row + 1) * deep)
        gh_acc[:, at] += dot_nt(both, jnp.concatenate([side(0, row), side(1, row)], axis=1))
        out_acc[:, at] += dot(act, down_side(row))
    md_acc[...] += dot_nt(act, down_map)
    ig_acc[...] += dot_nt(grad_gate, gate_map)
    iu_acc[...] += dot_nt(grad_up, up_map)
    partial = (
        ADAPTER_FACTOR * dot_tn(mg_ref[...], grad_gate),
        ADAPTER_FACTOR * dot_tn(mu_ref[...], grad_up),
        dot_tn(nd_ref[...], act),
    )
    for kind in range(3):
        for i, ref in enumerate(grads_refs):
            ref[0, kind * used : (kind + 1) * used, :] = partial[kind][
                :, i * LANES : (i + 1) * LANES
            ]

    @pl.when(step == pl.num_programs(0) - 1)
    def _():
        if last:
            mask = mask_ref[...]
            inner_g = (ADAPTER_FACTOR * ig_acc[...] * mask).astype(BF)
            inner_u = (ADAPTER_FACTOR * iu_acc[...] * mask).astype(BF)
            masked = (md_acc[...] * mask).astype(BF)
            gh_ref[...] = (
                gh_acc[...] + dot_nt(inner_g, ag_ref[...]) + dot_nt(inner_u, au_ref[...])
            ).astype(gh_ref.dtype)
            out_ref[...] = (out_acc[...] + ADAPTER_FACTOR * dot_nt(masked, od_ref[...])).astype(
                out_ref.dtype
            )
            for row in range(row_blocks):
                at = slice(row * deep, (row + 1) * deep)
                rows_ref[row, :used, :] = dot_tn(inner_g, h_ref[:, at])
                rows_ref[row, used : 2 * used, :] = dot_tn(inner_u, h_ref[:, at])
                rows_ref[row, 2 * used :, :] = ADAPTER_FACTOR * dot_tn(masked, c_ref[:, at])
        else:
            copies = [pltpu.make_async_copy(scratch[i], accs[i], sems.at[i]) for i in range(5)]
            for copy in copies:
                copy.start()
            for copy in copies:
                copy.wait()


def feed_forward_chunk(hidden, cotangent, masks, tables, weights, maps, previous, last, dtype):
    first = previous is None
    cols, row_blocks, _, deep, _ = weights.shape
    slabs = maps.shape[0] // cols
    count, used = masks[0].shape
    whole = lambda i: (0, 0)
    once = pl.Buffered(1)
    steps = cols * slabs // 2
    acc_shapes = [(count, MODEL_WIDTH)] * 2 + [(count, used)] * 3

    def weight_spec(side):
        def at(i):
            return ((2 * i + side) // slabs, 0, (2 * i + side) % slabs, 0, 0)

        return pl.BlockSpec((1, row_blocks, 3, deep, LANES), at)

    def slab_spec(side):
        return pl.BlockSpec((1, 3 * used, LANES), lambda i: (2 * i + side, 0, 0))

    def half_spec(side):
        return pl.BlockSpec((1, 3 * used, LANES), lambda i: (i, 0, 0))

    in_specs = (
        [pl.BlockSpec((count, MODEL_WIDTH), whole, pipeline_mode=once)] * 2
        + [pl.BlockSpec((count, used), whole)] * 4
        + [pl.BlockSpec((MODEL_WIDTH, used), whole, pipeline_mode=once)] * 3
        + [weight_spec(0), weight_spec(1), slab_spec(0), slab_spec(1)]
    )
    operands = [hidden, cotangent, *masks, *tables, weights, weights, maps, maps]
    if not first:
        in_specs = in_specs + [pl.BlockSpec(memory_space=pl.ANY)] * 5
        operands = operands + list(previous)
    if last:
        out_specs = [pl.BlockSpec((count, MODEL_WIDTH), whole)] * 2 + [
            pl.BlockSpec((row_blocks, 3 * used, deep), lambda i: (0, 0, 0))
        ]
        out_shape = [jax.ShapeDtypeStruct(s, dtype) for s in acc_shapes[:2]] + [
            jax.ShapeDtypeStruct((row_blocks, 3 * used, deep), F32)
        ]
    else:
        out_specs = [pl.BlockSpec(memory_space=pl.ANY)] * 5
        out_shape = [jax.ShapeDtypeStruct(s, F32) for s in acc_shapes]
    outs = pl.pallas_call(
        functools.partial(feed_forward_kernel, first, last),
        grid=(steps,),
        in_specs=in_specs,
        out_specs=out_specs + [half_spec(0), half_spec(1)],
        out_shape=out_shape + [jax.ShapeDtypeStruct((steps, 3 * used, LANES), F32)] * 2,
        scratch_shapes=[pltpu.VMEM(s, F32) for s in acc_shapes]
        + [pltpu.SemaphoreType.DMA((5,))],
        compiler_params=pltpu.CompilerParams(vmem_limit_bytes=VMEM_LIMIT),
        cost_estimate=pl.CostEstimate(
            flops=24 * count * MODEL_WIDTH * steps * LANES,
            bytes_accessed=steps * row_blocks * 6 * deep * LANES * 2,
            transcendentals=count * steps * 2 * LANES,
        ),
        name="feed_forward",
    )(*operands)
    return outs[:-2], outs[-2:]


def place(first, first_at, second, second_at, columns):
    index = jnp.arange(columns)[:, None] // ADAPTER_RANK
    copies = columns // ADAPTER_RANK
    return jnp.where(index == first_at, jnp.tile(first, (copies, 1)), 0.0) + jnp.where(
        index == second_at, jnp.tile(second, (copies, 1)), 0.0
    )


def lane_pad(values):
    return jnp.pad(values, ((0, 0),) * (values.ndim - 1) + ((0, LANES - values.shape[-1]),))


def row_pad(values):
    return jnp.pad(
        values, ((0, 0),) * (values.ndim - 2) + ((0, LANES - values.shape[-2]), (0, 0))
    )


def thirds(values):
    parts = []
    for _ in range(3):
        part = lax.reduce_precision(values, 8, 7)
        parts.append(part.astype(BF)[:, None])
        values = values - part
    return parts


def on_device(
    tokens,
    cotangent,
    attention_norm_gain,
    feedfwd_norm_gain,
    query_norm_gain,
    key_norm_gain,
    query_matrix,
    key_matrix,
    value_matrix,
    output_matrix,
    gate_matrix,
    up_matrix,
    down_matrix,
    query_adapter_inmaps,
    query_adapter_outmaps,
    key_adapter_inmaps,
    key_adapter_outmaps,
    value_adapter_inmaps,
    value_adapter_outmaps,
    output_adapter_inmaps,
    output_adapter_outmaps,
    gate_adapter_inmaps,
    gate_adapter_outmaps,
    up_adapter_inmaps,
    up_adapter_outmaps,
    down_adapter_inmaps,
    down_adapter_outmaps,
    segment,
    depth,
    parent,
    adapter,
):
    rows = lax.axis_size("row")
    cols = lax.axis_size("col")
    devices = rows * cols
    repeat = devices // QUERY_HEADS
    plane = lax.axis_index("dp")
    row = lax.axis_index("row")
    col = lax.axis_index("col")
    length = segment.shape[0]
    own = tokens.shape[0] // rows
    columns = query_adapter_inmaps.shape[1]
    rank = ADAPTER_RANK
    swap = [(0, 1), (1, 0)]
    pairs = [(r, r ^ repeat) for r in range(rows)]
    q_local = query_matrix.shape[1]
    kv_local = key_matrix.shape[1]
    wide = q_local + 2 * kv_local
    features = gate_matrix.shape[0]

    own_adapter = adapter[0]
    other_adapter = lax.ppermute(adapter, "dp", swap)[0]
    both = (own_adapter, other_adapter)

    def inmap(table, at):
        return lax.dynamic_slice_in_dim(table, at * rank, rank, 1)

    def outmap(table, at):
        return lax.dynamic_slice_in_dim(table, at * rank, rank, 0)

    qkv_local = jnp.concatenate([query_matrix, key_matrix, value_matrix], axis=1)

    def block_of(table, before, after):
        return jnp.pad(outmap(table, own_adapter), ((0, 0), (before, after)))

    qkv_maps = jnp.concatenate(
        [
            block_of(query_adapter_outmaps, 0, 2 * kv_local),
            block_of(key_adapter_outmaps, q_local, kv_local),
            block_of(value_adapter_outmaps, q_local + kv_local, 0),
        ],
        axis=0,
    )
    attention_pack = jnp.concatenate(
        [
            table[:, at : at + features]
            for table in (qkv_local, qkv_maps)
            for at in range(0, wide, features)
        ]
        + [
            lax.dynamic_slice_in_dim(
                output_matrix, plane * (output_matrix.shape[0] // 2), output_matrix.shape[0] // 2, 0
            )
        ],
        axis=0,
    )
    attention_weights = lax.all_gather(attention_pack, PLANE, axis=0, tiled=True).reshape(
        cols, rows, -1, features
    )
    o_rows = output_matrix.shape[0]
    own_output_weights = attention_weights[:, :, -(o_rows // 2) :]
    plane_flag = plane.astype(jnp.int32).reshape(1)
    ffn_half = gate_matrix.shape[1] // 2
    half_start = plane * ffn_half
    chunks = 2 if ffn_half % 256 == 0 else 3
    width = ffn_half // chunks
    slabs = width // LANES

    def plates(table):
        return [table[:, at : at + LANES] for at in range(0, table.shape[1], LANES)]

    def half_of(table):
        return lax.dynamic_slice_in_dim(table, half_start, ffn_half, 1)

    map_width = max(ffn_half, o_rows)

    def to_width(table):
        return jnp.pad(table, ((0, 0), (0, map_width - table.shape[1])))

    col_pack = jnp.concatenate(
        [
            *[to_width(half_of(outmap(gate_adapter_outmaps, a))) for a in both],
            *[to_width(half_of(outmap(up_adapter_outmaps, a))) for a in both],
            *[to_width(half_of(inmap(down_adapter_inmaps, a).T)) for a in both],
            to_width(inmap(output_adapter_inmaps, own_adapter).T),
            jnp.zeros((rank, map_width), BF),
        ],
        axis=0,
    )
    map_rows = col_pack.shape[0] // rows
    map_plates = plates(lax.dynamic_slice_in_dim(col_pack, row * map_rows, map_rows, 0))
    ffn_weights = []
    for chunk in range(chunks):
        pack = []
        for slab in range(slabs):
            start = half_start + (chunk * slabs + slab) * LANES
            pack.append(lax.dynamic_slice_in_dim(gate_matrix, start, LANES, 1))
            pack.append(lax.dynamic_slice_in_dim(up_matrix, start, LANES, 1))
            pack.extend(plates(lax.dynamic_slice_in_dim(down_matrix, start, LANES, 0)))
        if chunk == 0:
            spare = features - map_rows * len(map_plates)
            pack = pack + map_plates + [jnp.zeros((spare, LANES), BF)]
        pack = jnp.concatenate(pack, axis=0)
        ffn_weights.append(
            lax.all_gather(pack, PLANE, axis=0, tiled=True).reshape(
                cols, rows, -1, features, LANES
            )
        )
    col_maps = ffn_weights[0][:, :, -1, : map_rows * len(map_plates)].reshape(
        cols, rows, len(map_plates), map_rows, LANES
    )
    col_maps = jnp.transpose(col_maps, (0, 2, 1, 3, 4)).reshape(
        cols, len(map_plates), rows * map_rows, LANES
    )
    in_o = jnp.transpose(col_maps[:, : o_rows // LANES, 6 * rank : 7 * rank], (0, 2, 1, 3))
    in_o = row_pad(in_o.reshape(cols, rank, o_rows))

    row_pack = jnp.concatenate(
        [
            inmap(query_adapter_inmaps, own_adapter),
            inmap(key_adapter_inmaps, own_adapter),
            inmap(value_adapter_inmaps, own_adapter),
            *[inmap(gate_adapter_inmaps, a) for a in both],
            *[inmap(up_adapter_inmaps, a) for a in both],
            *[outmap(down_adapter_outmaps, a).T for a in both],
            outmap(output_adapter_outmaps, own_adapter).T,
            *thirds(attention_norm_gain),
            *thirds(feedfwd_norm_gain),
        ],
        axis=1,
    )

    row_maps = lax.all_gather(row_pack, "row", axis=0, tiled=True)
    in_qkv = row_maps[:, : 3 * rank]
    in_gate = row_maps[:, 3 * rank : 5 * rank]
    in_up = row_maps[:, 5 * rank : 7 * rank]
    out_down = row_maps[:, 7 * rank : 9 * rank]
    out_o = lane_pad(row_maps[:, 9 * rank : 10 * rank])
    gain_parts = row_maps[:, 10 * rank :].astype(F32)
    gain_one = (gain_parts[:, 0] + (gain_parts[:, 1] + gain_parts[:, 2])).reshape(1, -1)
    gain_two = (gain_parts[:, 3] + (gain_parts[:, 4] + gain_parts[:, 5])).reshape(1, -1)

    own_tokens = lax.all_to_all(tokens, "row", 0, 1, tiled=True)
    own_cotangent = lax.all_to_all(cotangent, "row", 0, 1, tiled=True)
    other_cotangent = lax.ppermute(own_cotangent, "dp", swap)
    own_tokens, other_cotangent, own_output_weights = lax.optimization_barrier(
        (own_tokens, other_cotangent, own_output_weights)
    )
    other_output_weights = lax.ppermute(own_output_weights, "dp", swap)
    head_gains = jnp.stack([query_norm_gain, key_norm_gain], axis=0)
    token_start = (col * rows + row) * own
    positions = lax.dynamic_slice_in_dim(depth, token_start, own, 0).astype(F32)
    half = HEAD_SIZE // 2
    freqs = THETA ** (-2.0 * jnp.arange(half).astype(F32) / HEAD_SIZE)
    angle = positions[:, None] * freqs[None, :]
    cosine = jnp.tile(jnp.cos(angle), (1, 2))
    sine = jnp.concatenate([-jnp.sin(angle), jnp.sin(angle)], axis=1)

    masked_qkv, pre, sent = qkv_forward(
        own_tokens, gain_one, in_qkv, cosine, sine, head_gains, attention_weights
    )

    def to_heads(sent):
        if repeat > 1:
            sent = jnp.repeat(sent, repeat, axis=0)
        return lax.all_to_all(sent, PLANE, 0, 0, tiled=True).reshape(length, sent.shape[2])

    def to_tokens(lines):
        got = lax.all_to_all(
            lines.reshape(devices, own, lines.shape[1]), PLANE, 0, 0, tiled=True
        )
        return got[::repeat] if repeat > 1 else got

    got, other_output_weights = lax.optimization_barrier((to_heads(sent), other_output_weights))
    output_weights = (own_output_weights, other_output_weights)
    theirs = lax.ppermute(got[:, HEAD_SIZE:], "row", pairs)
    flag = (1 - (row // repeat) % 2).astype(jnp.int32).reshape(1)

    block_node = segment.reshape(-1, SEG_LEN)[:, 0]
    nodes = jnp.arange(parent.shape[1])
    node_parent = jnp.sum(jnp.where(block_node[:, None] == nodes, parent.reshape(1, -1), 0), axis=1)
    block_index = jnp.arange(block_node.shape[0])
    parent_block = jnp.max(
        jnp.where(node_parent[:, None] == block_node[None, :], block_index[None, :], 0), axis=1
    )
    parent_block = jnp.where(node_parent > 0, parent_block, -1).astype(jnp.int32)
    head_attended, head_low, totals = attention_forward(parent_block, flag, got, theirs)
    attended = to_tokens(head_low)

    middle, hidden_ffn, masked_o = output_forward(
        plane_flag, attended, own_tokens, gain_two, in_o, out_o, output_weights
    )

    other_ffn = lax.ppermute(hidden_ffn, "dp", swap)
    tables = (in_gate, in_up, out_down)
    column_tree = jnp.arange(2 * rank)[None, :] // rank

    def masks_of(hidden, cot, tree):
        mask = jnp.broadcast_to((column_tree == tree).astype(F32), (own, 2 * rank))
        return (
            (dot(hidden, in_gate) * mask).astype(BF),
            (dot(hidden, in_up) * mask).astype(BF),
            (ADAPTER_FACTOR * dot(cot, out_down) * mask).astype(BF),
            mask,
        )

    parts = []

    def run(chunk, side, masks, accs):
        hidden, cot = side
        maps = col_maps[:, chunk * slabs : (chunk + 1) * slabs].reshape(cols * slabs, -1, LANES)
        last = chunk == chunks - 1
        return feed_forward_chunk(
            hidden,
            cot,
            masks,
            tables,
            ffn_weights[chunk],
            maps,
            accs,
            last,
            F32 if side is own_side else BF,
        )

    own_side = (hidden_ffn, own_cotangent)
    own_masks = masks_of(*own_side, 0)
    here, own_part = run(0, own_side, own_masks, None)
    other_ffn, here = lax.optimization_barrier((other_ffn, here))
    other_side = (other_ffn, other_cotangent)
    other_masks = masks_of(*other_side, 1)
    there, other_part = run(0, other_side, other_masks, None)
    parts = [(own_part, other_part)]
    for chunk in range(1, chunks):
        there, other_part = run(chunk, other_side, other_masks, there)
        here, own_part = run(chunk, own_side, own_masks, here)
        parts.append((own_part, other_part))

    def slab_order(part):
        even, odd = (part[0][i] + part[1][i] for i in range(2))
        part = jnp.stack([even, odd], axis=1).reshape(cols, slabs, 6 * rank, LANES)
        return jnp.transpose(part, (0, 2, 1, 3)).reshape(cols, 6 * rank, width)

    parts = [slab_order(part) for part in parts]
    gh_other = lax.ppermute(there[0], "dp", swap)

    grad_middle, sent, grad_o_rows, grad_o_cols = output_backward(
        plane_flag,
        here[0],
        gh_other,
        own_cotangent,
        middle,
        gain_two,
        in_o,
        out_o,
        attended,
        masked_o,
        output_weights,
    )
    out_sent, sent = lax.optimization_barrier((there[1], sent))
    out_other = lax.ppermute(out_sent, "dp", swap)
    head_grad = to_heads(sent)

    def pieces_of(row_table, col_table):
        row_table = jnp.swapaxes(row_table.astype(BF).reshape(rows, cols, -1, LANES), 0, 1)
        col_table = col_table.astype(BF).reshape(cols, rows, -1, LANES)
        return jnp.concatenate([row_table, col_table], axis=2).reshape(devices, -1, LANES)

    def gathered(values, axis, at):
        size = lax.axis_size(axis)
        whole = jnp.zeros((2, size, *values.shape[1:]), values.dtype)
        for k in range(size):
            block = values
            if k:
                block = lax.ppermute(values, axis, [(i, i ^ k) for i in range(size)])
            whole = lax.dynamic_update_index_in_dim(whole, block, at ^ k, 1)
        return whole

    def summed(pieces):
        mine = jnp.sum(pieces.astype(F32), axis=0).astype(BF)
        return jnp.stack([mine, lax.ppermute(mine, "dp", swap)], axis=0)

    def gathered_tables(both_trees, row_high):
        row_part = row_high * features // (cols * LANES)
        row_table = gathered(both_trees[:, :row_part], "col", col)
        col_table = gathered(both_trees[:, row_part:], "row", row)
        return row_table, col_table

    def tables_of(tables, row_high, col_high):
        row_table, col_table = tables
        row_table = row_table.reshape(2, row_high, features).astype(F32)
        col_table = col_table.reshape(2, col_high, -1).astype(F32)
        return row_table[0], col_table[0], row_table[1], col_table[1]

    def to_own_features(lines):
        blocks = lines.reshape(own, rows, features)
        whole = jnp.zeros((rows, own, features), lines.dtype)
        for k in range(rows):
            block = lax.dynamic_index_in_dim(blocks, row ^ k, 1, False)
            if k:
                block = lax.ppermute(block, "row", [(r, r ^ k) for r in range(rows)])
            whole = lax.dynamic_update_index_in_dim(whole, block, row ^ k, 0)
        return whole.reshape(rows * own, features)

    def to_map_width(table):
        return jnp.pad(table, ((0, 0), (0, 0), (0, map_width - table.shape[2])))

    mid_pieces = pieces_of(
        jnp.concatenate([here[2] + there[2], grad_o_rows], axis=1),
        jnp.concatenate(
            [to_map_width(jnp.concatenate(parts, axis=2)), to_map_width(grad_o_cols)], axis=1
        ),
    )
    head_grad, mid_pieces = lax.optimization_barrier((head_grad, mid_pieces))
    mid_pieces = lax.all_to_all(mid_pieces, PLANE, 0, 0, tiled=True)

    lines, kept, given = attention_backward(
        parent_block, flag, got, head_grad, head_attended, totals, theirs
    )
    lines, kept, given, mid_pieces, out_other = lax.optimization_barrier(
        (lines, kept, given, mid_pieces, out_other)
    )
    returned = to_tokens(merge(lines, kept, lax.ppermute(given, "row", pairs)))
    output = (middle + here[1] + out_other.astype(F32)).astype(BF)
    output = to_own_features(output)
    returned, output, mid_pieces = lax.optimization_barrier(
        (returned, output, summed(mid_pieces))
    )
    mid_tables = gathered_tables(mid_pieces, 7 * rank)

    grads_qkv, inner_qkv, row_end, col_end = qkv_unshape(
        returned,
        pre,
        masked_qkv,
        own_tokens,
        gain_one,
        cosine,
        sine,
        head_gains,
        attention_weights,
    )
    end_pieces = lax.all_to_all(pieces_of(row_end, col_end), PLANE, 0, 0, tiled=True)
    grad_low = qkv_backward(
        grads_qkv, inner_qkv, own_tokens, grad_middle, gain_one, in_qkv, attention_weights
    )
    grad_low, end_pieces, mid_tables = lax.optimization_barrier((grad_low, end_pieces, mid_tables))
    input_gradient = lax.all_to_all(grad_low, "row", 1, 0, tiled=True).astype(F32)
    end_tables = gathered_tables(summed(end_pieces), 3 * rank)
    row_mid, col_mid, row_got, col_got = tables_of(mid_tables, 7 * rank, 7 * rank)

    def placed(first, second):
        return place(first, own_adapter, second, other_adapter, columns)

    def row_sum(at):
        first = row_mid[at : at + rank] + row_got[at + rank : at + 2 * rank]
        second = row_mid[at + rank : at + 2 * rank] + row_got[at : at + rank]
        return placed(first, second)

    grad_a_gate = row_sum(0).T
    grad_a_up = row_sum(2 * rank).T
    grad_b_down = row_sum(4 * rank)
    grad_b_o = placed(row_mid[6 * rank :], row_got[6 * rank :])
    at = 6 * rank
    grad_a_o = placed(col_mid[at:, :o_rows], col_got[at:, :o_rows]).T

    def ffn_placed(kind):
        at = 2 * rank * kind
        mine = placed(col_mid[at : at + rank], col_mid[at + rank : at + 2 * rank])
        theirs = placed(col_got[at + rank : at + 2 * rank], col_got[at : at + rank])
        low = jnp.where(plane == 0, mine, theirs)
        high = jnp.where(plane == 0, theirs, mine)
        return jnp.concatenate([low[:, :ffn_half], high[:, :ffn_half]], axis=1)

    grad_b_gate = ffn_placed(0)
    grad_b_up = ffn_placed(1)
    grad_a_down = ffn_placed(2).T

    row_end, col_end, row_end_got, col_end_got = tables_of(end_tables, 3 * rank, rank)
    grad_a_q, grad_a_k, grad_a_v = (
        placed(row_end[i * rank : (i + 1) * rank], row_end_got[i * rank : (i + 1) * rank]).T
        for i in range(3)
    )
    grad_b = placed(col_end, col_end_got)
    grad_b_q = grad_b[:, :q_local]
    grad_b_k = grad_b[:, q_local : q_local + kv_local]
    grad_b_v = grad_b[:, q_local + kv_local :]

    return (
        output,
        input_gradient,
        grad_a_q,
        grad_b_q,
        grad_a_k,
        grad_b_k,
        grad_a_v,
        grad_b_v,
        grad_a_o,
        grad_b_o,
        grad_a_gate,
        grad_b_gate,
        grad_a_up,
        grad_b_up,
        grad_a_down,
        grad_b_down,
    )


def solution(mesh):
    return jax.shard_map(
        on_device,
        mesh=mesh,
        in_specs=(
            P(("dp", "col"), "row"),
            P(("dp", "col"), "row"),
            P("row"),
            P("row"),
            P(),
            P(),
            P("row", "col"),
            P("row", "col"),
            P("row", "col"),
            P("col", "row"),
            P("row", "col"),
            P("row", "col"),
            P("col", "row"),
            P("row", None),
            P(None, "col"),
            P("row", None),
            P(None, "col"),
            P("row", None),
            P(None, "col"),
            P("col", None),
            P(None, "row"),
            P("row", None),
            P(None, "col"),
            P("row", None),
            P(None, "col"),
            P("col", None),
            P(None, "row"),
            P("dp"),
            P("dp"),
            P("dp", None),
            P("dp"),
        ),
        out_specs=(
            P(("dp", "col"), "row"),
            P(("dp", "col"), "row"),
            P("row", None),
            P(None, "col"),
            P("row", None),
            P(None, "col"),
            P("row", None),
            P(None, "col"),
            P("col", None),
            P(None, "row"),
            P("row", None),
            P(None, "col"),
            P("row", None),
            P(None, "col"),
            P("col", None),
            P(None, "row"),
        ),
        check_vma=False,
    )
```

```python
import functools
import math

import jax
import jax.numpy as jnp
from jax import lax
from jax.experimental import pallas as pl
from jax.experimental.pallas import tpu as pltpu
from jax.sharding import PartitionSpec as P

MODEL_WIDTH = 2048
QUERY_HEADS = 16
KEY_VALUE_HEADS = 8
HEAD_SIZE = 128
ADAPTER_RANK = 16
TREE_LEN = 5120
TRUNK = 2048
SEG_LEN = 256
QUERY_BLOCK = 512
KEY_BLOCK = 1024

EPSILON = 1e-06
THETA = 1000000.0
ADAPTER_FACTOR = 2.0
BF = jnp.bfloat16
F32 = jnp.float32
SCALE = HEAD_SIZE ** (-0.5)
SCALE_LOG2 = SCALE * math.log2(math.e)
PLANE = ("col", "row")
LANES = 128
VMEM_LIMIT = 63 * 1024 * 1024


def dot(left, right):
    return jnp.dot(left, right, preferred_element_type=F32)


def dot_nt(left, right):
    return lax.dot_general(left, right, (((1,), (1,)), ((), ())), preferred_element_type=F32)


def dot_tn(left, right):
    return lax.dot_general(left, right, (((0,), (0,)), ((), ())), preferred_element_type=F32)


def walk_keys(index, parent_ref, step):
    trunk_blocks = TRUNK // QUERY_BLOCK

    @pl.when(index < trunk_blocks)
    def _():
        @pl.loop(0, index)
        def _(block):
            step(pl.multiple_of(block * QUERY_BLOCK, QUERY_BLOCK), QUERY_BLOCK)

        step(pl.multiple_of(index * QUERY_BLOCK, QUERY_BLOCK), QUERY_BLOCK, causal=True)

    @pl.when(index >= trunk_blocks)
    def _():
        @pl.loop(0, TRUNK // KEY_BLOCK)
        def _(part):
            step(pl.multiple_of(part * KEY_BLOCK, KEY_BLOCK), KEY_BLOCK)

        @pl.loop(0, QUERY_BLOCK // SEG_LEN)
        def _(side):
            block = index * (QUERY_BLOCK // SEG_LEN) + side
            first = pl.multiple_of(side * SEG_LEN, SEG_LEN)
            step(pl.multiple_of(block * SEG_LEN, SEG_LEN), SEG_LEN, first, SEG_LEN, True)
            above = parent_ref[block]

            @pl.when(above >= 0)
            def _():
                step(pl.multiple_of(above * SEG_LEN, SEG_LEN), SEG_LEN, first, SEG_LEN)


def attention_forward_kernel(
    parent_ref, flag_ref, q_ref, mine_ref, theirs_ref, o_ref, low_ref, l_ref, k_ref, v_ref, acc_ref
):
    index = pl.program_id(0)

    @pl.when(index == 0)
    def _():
        lane = lax.broadcasted_iota(jnp.int32, (v_ref.shape[0], HEAD_SIZE), 1)
        v_ref[:, HEAD_SIZE:] = jnp.where(lane == 0, 1.0, 0.0).astype(BF)

        @pl.when(flag_ref[0] == 1)
        def _():
            k_ref[...] = mine_ref[...]
            v_ref[:, :HEAD_SIZE] = theirs_ref[...]

        @pl.when(flag_ref[0] != 1)
        def _():
            k_ref[...] = theirs_ref[...]
            v_ref[:, :HEAD_SIZE] = mine_ref[...]

    acc_ref[...] = jnp.zeros_like(acc_ref)

    def step(start, size, first=0, count=QUERY_BLOCK, causal=False):
        rows = pl.ds(start, size)
        at = pl.ds(first, count)
        scores = dot_nt(q_ref[at, :], k_ref[rows, :])
        probs = jnp.exp2(scores * SCALE_LOG2)
        if causal:
            ahead = lax.broadcasted_iota(jnp.int32, probs.shape, 0)
            behind = lax.broadcasted_iota(jnp.int32, probs.shape, 1)
            probs = jnp.where(behind <= ahead, probs, 0.0)
        acc_ref[at, :] += dot(probs.astype(BF), v_ref[rows, :])

    walk_keys(index, parent_ref, step)
    total = acc_ref[:, HEAD_SIZE : HEAD_SIZE + 1]
    attended = acc_ref[:, :HEAD_SIZE] / total
    o_ref[...] = attended
    low_ref[...] = attended.astype(BF)
    spread = jnp.broadcast_to(total, (QUERY_BLOCK, LANES))
    l_ref[0] = jnp.transpose(spread)[:8, :]


def attention_forward(parent_block, flag, got, theirs):
    length = theirs.shape[0]
    blocks = length // QUERY_BLOCK
    whole = lambda i, p, f: (0, 0)
    part = lambda i, p, f: (i, 0)
    return pl.pallas_call(
        attention_forward_kernel,
        grid_spec=pltpu.PrefetchScalarGridSpec(
            num_scalar_prefetch=2,
            grid=(blocks,),
            in_specs=[
                pl.BlockSpec((QUERY_BLOCK, HEAD_SIZE), part),
                pl.BlockSpec((length, HEAD_SIZE), lambda i, p, f: (0, 1)),
                pl.BlockSpec((length, HEAD_SIZE), whole),
            ],
            out_specs=[
                pl.BlockSpec((QUERY_BLOCK, HEAD_SIZE), part),
                pl.BlockSpec((QUERY_BLOCK, HEAD_SIZE), part),
                pl.BlockSpec((1, 8, QUERY_BLOCK), lambda i, p, f: (i, 0, 0)),
            ],
            scratch_shapes=[
                pltpu.VMEM((length, HEAD_SIZE), BF),
                pltpu.VMEM((length, 2 * HEAD_SIZE), BF),
                pltpu.VMEM((QUERY_BLOCK, 2 * HEAD_SIZE), F32),
            ],
        ),
        out_shape=[
            jax.ShapeDtypeStruct((length, HEAD_SIZE), F32),
            jax.ShapeDtypeStruct((length, HEAD_SIZE), BF),
            jax.ShapeDtypeStruct((blocks, 8, QUERY_BLOCK), F32),
        ],
        compiler_params=pltpu.CompilerParams(vmem_limit_bytes=VMEM_LIMIT),
        cost_estimate=pl.CostEstimate(
            flops=160 * SEG_LEN * SEG_LEN * HEAD_SIZE * 4,
            bytes_accessed=length * HEAD_SIZE * 12,
            transcendentals=160 * SEG_LEN * SEG_LEN,
        ),
        name="attention_forward",
    )(parent_block, flag, got, got, theirs)


def attention_backward_kernel(
    parent_ref,
    flag_ref,
    q_ref,
    g_ref,
    o_ref,
    l_ref,
    mine_ref,
    theirs_ref,
    dq_ref,
    kept_ref,
    given_ref,
    k_ref,
    v_ref,
    kt_ref,
    dk_ref,
    dv_ref,
    acc_ref,
    delta_ref,
    inverse_ref,
):
    index = pl.program_id(0)

    @pl.when(index == 0)
    def _():
        dk_ref[...] = jnp.zeros_like(dk_ref)
        dv_ref[...] = jnp.zeros_like(dv_ref)

        @pl.when(flag_ref[0] == 1)
        def _():
            k_ref[...] = mine_ref[...]
            v_ref[...] = theirs_ref[...]

        @pl.when(flag_ref[0] != 1)
        def _():
            k_ref[...] = theirs_ref[...]
            v_ref[...] = mine_ref[...]

        @pl.loop(0, k_ref.shape[0] // SEG_LEN)
        def _(block):
            rows = pl.ds(pl.multiple_of(block * SEG_LEN, SEG_LEN), SEG_LEN)
            kt_ref[:, rows] = jnp.transpose(k_ref[rows, :])

    delta = jnp.sum(g_ref[...].astype(F32) * o_ref[...], axis=1, keepdims=True)
    delta_ref[...] = jnp.transpose(jnp.broadcast_to(delta, (QUERY_BLOCK, LANES)))[:8, :]
    inverse_ref[...] = 1.0 / l_ref[0]
    acc_ref[...] = jnp.zeros_like(acc_ref)

    def step(start, size, first=0, count=QUERY_BLOCK, causal=False):
        rows = pl.ds(start, size)
        at = pl.ds(first, count)
        query = q_ref[at, :]
        grad = g_ref[at, :]
        probs = jnp.exp2(dot_nt(k_ref[rows, :], query) * SCALE_LOG2) * inverse_ref[:1, at]
        if causal:
            behind = lax.broadcasted_iota(jnp.int32, probs.shape, 0)
            ahead = lax.broadcasted_iota(jnp.int32, probs.shape, 1)
            probs = jnp.where(behind <= ahead, probs, 0.0)
        dprobs = dot_nt(v_ref[rows, :], grad)
        dscores = (probs * (dprobs - delta_ref[:1, at])).astype(BF)
        dv_ref[rows, :] += dot(probs.astype(BF), grad)
        dk_ref[rows, :] += dot(dscores, query)
        acc_ref[:, at] += dot(kt_ref[:, rows], dscores)

    walk_keys(index, parent_ref, step)
    dq_ref[...] = (jnp.transpose(acc_ref[...]) * SCALE).astype(BF)

    @pl.when(index == pl.num_programs(0) - 1)
    def _():
        @pl.when(flag_ref[0] == 1)
        def _():
            kept_ref[...] = dk_ref[...] * SCALE
            given_ref[...] = dv_ref[...].astype(BF)

        @pl.when(flag_ref[0] != 1)
        def _():
            kept_ref[...] = dv_ref[...]
            given_ref[...] = (dk_ref[...] * SCALE).astype(BF)


def attention_backward(parent_block, flag, got, grad, attended, totals, theirs):
    length = theirs.shape[0]
    blocks = length // QUERY_BLOCK
    whole = lambda i, p, f: (0, 0)
    part = lambda i, p, f: (i, 0)
    return pl.pallas_call(
        attention_backward_kernel,
        grid_spec=pltpu.PrefetchScalarGridSpec(
            num_scalar_prefetch=2,
            grid=(blocks,),
            in_specs=[
                pl.BlockSpec((QUERY_BLOCK, HEAD_SIZE), part),
                pl.BlockSpec((QUERY_BLOCK, HEAD_SIZE), part),
                pl.BlockSpec((QUERY_BLOCK, HEAD_SIZE), part),
                pl.BlockSpec((1, 8, QUERY_BLOCK), lambda i, p, f: (i, 0, 0)),
                pl.BlockSpec((length, HEAD_SIZE), lambda i, p, f: (0, 1)),
                pl.BlockSpec((length, HEAD_SIZE), whole),
            ],
            out_specs=[
                pl.BlockSpec((QUERY_BLOCK, HEAD_SIZE), part),
                pl.BlockSpec((length, HEAD_SIZE), whole),
                pl.BlockSpec((length, HEAD_SIZE), whole),
            ],
            scratch_shapes=[
                pltpu.VMEM((length, HEAD_SIZE), BF),
                pltpu.VMEM((length, HEAD_SIZE), BF),
                pltpu.VMEM((HEAD_SIZE, length), BF),
                pltpu.VMEM((length, HEAD_SIZE), F32),
                pltpu.VMEM((length, HEAD_SIZE), F32),
                pltpu.VMEM((HEAD_SIZE, QUERY_BLOCK), F32),
                pltpu.VMEM((8, QUERY_BLOCK), F32),
                pltpu.VMEM((8, QUERY_BLOCK), F32),
            ],
        ),
        out_shape=[
            jax.ShapeDtypeStruct((length, 2 * HEAD_SIZE), BF),
            jax.ShapeDtypeStruct((length, HEAD_SIZE), F32),
            jax.ShapeDtypeStruct((length, HEAD_SIZE), BF),
        ],
        compiler_params=pltpu.CompilerParams(vmem_limit_bytes=VMEM_LIMIT),
        cost_estimate=pl.CostEstimate(
            flops=160 * SEG_LEN * SEG_LEN * HEAD_SIZE * 10,
            bytes_accessed=length * HEAD_SIZE * 24,
            transcendentals=160 * SEG_LEN * SEG_LEN,
        ),
        name="attention_backward",
    )(parent_block, flag, got, grad, attended, totals, got, theirs)


def merge_kernel(lines_ref, kept_ref, got_ref, out_ref):
    out_ref[...] = (kept_ref[...] + got_ref[...].astype(F32)).astype(BF)


def merge(lines, kept, got):
    length = kept.shape[0]
    rows = 4 * SEG_LEN
    part = pl.BlockSpec((rows, HEAD_SIZE), lambda i: (i, 0))
    return pl.pallas_call(
        merge_kernel,
        grid=(length // rows,),
        in_specs=[pl.BlockSpec(memory_space=pl.ANY), part, part],
        out_specs=pl.BlockSpec((rows, HEAD_SIZE), lambda i: (i, 1)),
        out_shape=jax.ShapeDtypeStruct(lines.shape, lines.dtype),
        input_output_aliases={0: 0},
        cost_estimate=pl.CostEstimate(
            flops=length * HEAD_SIZE, bytes_accessed=length * HEAD_SIZE * 10, transcendentals=0
        ),
        name="merge",
    )(lines, kept, got)


def norm_scale(values):
    return lax.rsqrt(jnp.mean(values * values, axis=1, keepdims=True) + EPSILON)


def norm_back(values, scale, gain, gradient):
    weighted = gain * gradient
    inner_sum = jnp.sum(weighted * values, axis=1, keepdims=True)
    return scale * weighted - values * (scale**3 * (inner_sum * (1.0 / MODEL_WIDTH)))


def outmaps_of(w_ref, pieces, piece, used):
    at = pieces * piece
    return jnp.concatenate(
        [w_ref[0, 0, at + p * used : at + (p + 1) * used, :] for p in range(pieces)], axis=1
    )


def qkv_forward_kernel(
    x_ref,
    gain_ref,
    a_ref,
    cos_ref,
    sin_ref,
    hg_ref,
    w_ref,
    m_ref,
    pre_ref,
    sent_ref,
    hidden_ref,
):
    row_blocks = w_ref.shape[1]
    piece = w_ref.shape[3]
    pieces = w_ref.shape[2] // piece
    heads = sent_ref.shape[0]
    used = m_ref.shape[1]

    @pl.when(pl.program_id(0) == 0)
    def _():
        resid = x_ref[...].astype(F32)
        hidden_ref[...] = (resid * norm_scale(resid) * gain_ref[...]).astype(BF)
        m_ref[...] = dot(hidden_ref[...], a_ref[...]).astype(BF)

    hidden = hidden_ref[...]
    whole = jnp.concatenate(
        [
            dot(
                hidden,
                jnp.concatenate(
                    [w_ref[0, r, p * piece : (p + 1) * piece, :] for r in range(row_blocks)], axis=0
                ),
            )
            for p in range(pieces)
        ],
        axis=1,
    ) + ADAPTER_FACTOR * dot(m_ref[...], outmaps_of(w_ref, pieces, piece, used))
    pre_ref[0] = whole[:, : pre_ref.shape[2]]
    cosine = cos_ref[...]
    sine = sin_ref[...]

    def shaped(at, gain):
        lines = whole[:, at : at + HEAD_SIZE]
        normed = lines * norm_scale(lines) * gain
        return (normed * cosine + pltpu.roll(normed, HEAD_SIZE // 2, 1) * sine).astype(BF)

    for head in range(heads):
        sent_ref[head, :, :HEAD_SIZE] = shaped(head * HEAD_SIZE, hg_ref[0:1, :])
    key_at = heads * HEAD_SIZE
    value_at = key_at + heads // 2 * HEAD_SIZE
    for pair in range(heads // 2):
        at = pair * HEAD_SIZE
        sent_ref[2 * pair, :, HEAD_SIZE:] = shaped(key_at + at, hg_ref[1:2, :])
        sent_ref[2 * pair + 1, :, HEAD_SIZE:] = whole[
            :, value_at + at : value_at + at + HEAD_SIZE
        ].astype(BF)


def qkv_forward(x, gain, inmaps, cosine, sine, head_gains, weights):
    own = x.shape[0]
    cols, row_blocks, tall, piece = weights.shape
    wide = tall // piece * piece
    used = inmaps.shape[1]
    heads = QUERY_HEADS // cols
    whole = lambda c: (0, 0)
    step = lambda c: (c, 0, 0)
    return pl.pallas_call(
        qkv_forward_kernel,
        grid=(cols,),
        in_specs=[
            pl.BlockSpec(x.shape, whole),
            pl.BlockSpec(gain.shape, whole),
            pl.BlockSpec(inmaps.shape, whole),
            pl.BlockSpec(cosine.shape, whole),
            pl.BlockSpec(sine.shape, whole),
            pl.BlockSpec(head_gains.shape, whole),
            pl.BlockSpec((1, row_blocks, tall, piece), lambda c: (c, 0, 0, 0)),
        ],
        out_specs=[
            pl.BlockSpec((own, used), whole),
            pl.BlockSpec((1, own, wide * 3 // 4), step),
            pl.BlockSpec((heads, own, 2 * HEAD_SIZE), step),
        ],
        out_shape=[
            jax.ShapeDtypeStruct((own, used), BF),
            jax.ShapeDtypeStruct((cols, own, wide * 3 // 4), F32),
            jax.ShapeDtypeStruct((QUERY_HEADS, own, 2 * HEAD_SIZE), BF),
        ],
        scratch_shapes=[pltpu.VMEM((own, MODEL_WIDTH), BF)],
        compiler_params=pltpu.CompilerParams(vmem_limit_bytes=VMEM_LIMIT),
        cost_estimate=pl.CostEstimate(
            flops=2 * own * MODEL_WIDTH * cols * wide,
            bytes_accessed=cols * wide * MODEL_WIDTH * 2,
            transcendentals=own * cols * 8,
        ),
        name="qkv_forward",
    )(x, gain, inmaps, cosine, sine, head_gains, weights)


def qkv_unshape_kernel(
    ret_ref,
    pre_ref,
    m_ref,
    x_ref,
    gain_ref,
    cos_ref,
    sin_ref,
    hg_ref,
    w_ref,
    grads_ref,
    inner_ref,
    ga_ref,
    gb_ref,
    in_acc_ref,
):
    step = pl.program_id(0)
    row_blocks, used, piece = ga_ref.shape
    heads = ret_ref.shape[0]
    pieces = grads_ref.shape[2] // piece
    cosine = cos_ref[...]
    sine = sin_ref[...]

    @pl.when(step == 0)
    def _():
        in_acc_ref[...] = jnp.zeros_like(in_acc_ref)

    def unshaped(grad, at, gain):
        grad = grad.astype(F32)
        lines = pre_ref[0, :, at : at + HEAD_SIZE]
        turned = gain * (grad * cosine + pltpu.roll(grad * sine, HEAD_SIZE // 2, 1))
        scale = norm_scale(lines)
        inner_mean = jnp.mean(turned * lines, axis=1, keepdims=True)
        return (scale * turned - lines * (scale**3 * inner_mean)).astype(BF)

    parts = []
    for head in range(heads):
        parts.append(unshaped(ret_ref[head, :, :HEAD_SIZE], head * HEAD_SIZE, hg_ref[0:1, :]))
    for pair in range(heads // 2):
        at = (heads + pair) * HEAD_SIZE
        parts.append(unshaped(ret_ref[2 * pair, :, HEAD_SIZE:], at, hg_ref[1:2, :]))
    for pair in range(heads // 2):
        parts.append(ret_ref[2 * pair + 1, :, HEAD_SIZE:])
    grads = jnp.concatenate(parts, axis=1)
    grads_ref[0] = grads
    outmaps = jnp.concatenate(
        [w_ref[0, 0, p * used : (p + 1) * used, :] for p in range(pieces)], axis=1
    )
    in_acc_ref[...] += dot_nt(grads, outmaps)
    outer = ADAPTER_FACTOR * dot_tn(m_ref[...], grads)
    rank = ADAPTER_RANK
    edges = (0, heads * HEAD_SIZE, heads * HEAD_SIZE * 3 // 2, heads * HEAD_SIZE * 2)
    for i in range(3):
        gb_ref[0, :, edges[i] : edges[i + 1]] = outer[
            i * rank : (i + 1) * rank, edges[i] : edges[i + 1]
        ]

    @pl.when(step == pl.num_programs(0) - 1)
    def _():
        inner = (ADAPTER_FACTOR * in_acc_ref[...]).astype(BF)
        inner_ref[...] = inner
        resid = x_ref[...].astype(F32)
        hidden = (resid * norm_scale(resid) * gain_ref[...]).astype(BF)
        for r in range(row_blocks):
            ga_ref[r] = dot_tn(inner, hidden[:, r * piece : (r + 1) * piece])


def qkv_unshape(returned, pre, masked, x, gain, cosine, sine, head_gains, weights):
    own = x.shape[0]
    cols, row_blocks, tall, piece = weights.shape
    pieces = tall // piece
    wide = pieces * piece
    heads = QUERY_HEADS // cols
    used = 3 * ADAPTER_RANK
    map_rows = tall - wide
    at = wide // map_rows if wide % map_rows == 0 else None
    maps = weights[:, :1, wide:] if at is None else weights
    first = 0 if at is None else at
    whole = lambda c: (0, 0)
    step = lambda c: (c, 0, 0)
    return pl.pallas_call(
        qkv_unshape_kernel,
        grid=(cols,),
        in_specs=[
            pl.BlockSpec((heads, own, 2 * HEAD_SIZE), step),
            pl.BlockSpec((1, own, pre.shape[2]), step),
            pl.BlockSpec(masked.shape, whole),
            pl.BlockSpec(x.shape, whole),
            pl.BlockSpec(gain.shape, whole),
            pl.BlockSpec(cosine.shape, whole),
            pl.BlockSpec(sine.shape, whole),
            pl.BlockSpec(head_gains.shape, whole),
            pl.BlockSpec((1, 1, map_rows, piece), lambda c: (c, 0, first, 0)),
        ],
        out_specs=[
            pl.BlockSpec((1, own, wide), step),
            pl.BlockSpec((own, used), whole),
            pl.BlockSpec((row_blocks, used, piece), lambda c: (0, 0, 0)),
            pl.BlockSpec((1, ADAPTER_RANK, wide), step),
        ],
        out_shape=[
            jax.ShapeDtypeStruct((cols, own, wide), BF),
            jax.ShapeDtypeStruct((own, used), BF),
            jax.ShapeDtypeStruct((row_blocks, used, piece), F32),
            jax.ShapeDtypeStruct((cols, ADAPTER_RANK, wide), F32),
        ],
        scratch_shapes=[pltpu.VMEM((own, used), F32)],
        compiler_params=pltpu.CompilerParams(vmem_limit_bytes=VMEM_LIMIT),
        cost_estimate=pl.CostEstimate(
            flops=4 * own * 64 * cols * wide,
            bytes_accessed=cols * own * wide * 8,
            transcendentals=own * cols * 8,
        ),
        name="qkv_unshape",
    )(returned, pre, masked, x, gain, cosine, sine, head_gains, maps)


def qkv_backward_kernel(
    grads_ref, inner_ref, x_ref, gm_ref, gain_ref, a_ref, w_ref, grad_ref, acc_ref
):
    step = pl.program_id(0)
    row_blocks = w_ref.shape[1]
    piece = w_ref.shape[3]
    pieces = w_ref.shape[2] // piece

    @pl.when(step == 0)
    def _():
        acc_ref[...] = dot_nt(inner_ref[...], a_ref[...])

    for r in range(row_blocks):
        weights = jnp.concatenate(
            [w_ref[0, r, p * piece : (p + 1) * piece, :] for p in range(pieces)], axis=1
        )
        acc_ref[:, r * piece : (r + 1) * piece] += dot_nt(grads_ref[0], weights)

    @pl.when(step == pl.num_programs(0) - 1)
    def _():
        resid = x_ref[...].astype(F32)
        grad_ref[...] = (
            gm_ref[...] + norm_back(resid, norm_scale(resid), gain_ref[...], acc_ref[...])
        ).astype(BF)


def qkv_backward(grads, inner, x, grad_middle, gain, inmaps, weights):
    own = x.shape[0]
    cols, row_blocks, tall, piece = weights.shape
    wide = tall // piece * piece
    whole = lambda c: (0, 0)
    once = pl.Buffered(1)
    return pl.pallas_call(
        qkv_backward_kernel,
        grid=(cols,),
        in_specs=[
            pl.BlockSpec((1, own, wide), lambda c: (c, 0, 0)),
            pl.BlockSpec(inner.shape, whole),
            pl.BlockSpec(x.shape, whole, pipeline_mode=once),
            pl.BlockSpec(grad_middle.shape, whole, pipeline_mode=once),
            pl.BlockSpec(gain.shape, whole),
            pl.BlockSpec(inmaps.shape, whole),
            pl.BlockSpec((1, row_blocks, wide, piece), lambda c: (c, 0, 0, 0)),
        ],
        out_specs=pl.BlockSpec((own, MODEL_WIDTH), whole),
        out_shape=jax.ShapeDtypeStruct((own, MODEL_WIDTH), BF),
        scratch_shapes=[pltpu.VMEM((own, MODEL_WIDTH), F32)],
        compiler_params=pltpu.CompilerParams(vmem_limit_bytes=VMEM_LIMIT),
        cost_estimate=pl.CostEstimate(
            flops=2 * own * MODEL_WIDTH * cols * wide,
            bytes_accessed=cols * wide * MODEL_WIDTH * 2,
            transcendentals=own,
        ),
        name="qkv_backward",
    )(grads, inner, x, grad_middle, gain, inmaps, weights)


def whole_output_weights(flag_ref, own_ref, other_ref):
    own, other = (
        jnp.concatenate([ref[0, r] for r in range(ref.shape[1])], axis=1)
        for ref in (own_ref, other_ref)
    )
    first = flag_ref[0] == 0
    return jnp.concatenate(
        [jnp.where(first, own, other), jnp.where(first, other, own)], axis=0
    )


def output_forward_kernel(
    flag_ref,
    att_ref,
    x_ref,
    gain_ref,
    a_ref,
    b_ref,
    own_ref,
    other_ref,
    middle_ref,
    hidden_ref,
    m_ref,
    acc_ref,
    m_acc_ref,
):
    step = pl.program_id(0)
    heads = att_ref.shape[0]

    @pl.when(step == 0)
    def _():
        acc_ref[...] = x_ref[...].astype(F32)
        m_acc_ref[...] = jnp.zeros_like(m_acc_ref)

    attended = jnp.concatenate([att_ref[h] for h in range(heads)], axis=1)
    acc_ref[...] += dot(attended, whole_output_weights(flag_ref, own_ref, other_ref))
    m_acc_ref[...] += dot_nt(attended, a_ref[0])

    @pl.when(step == pl.num_programs(0) - 1)
    def _():
        masked = m_acc_ref[...].astype(BF)
        m_ref[...] = masked
        middle = acc_ref[...] + ADAPTER_FACTOR * dot_nt(masked, b_ref[...])
        middle_ref[...] = middle
        hidden_ref[...] = (middle * norm_scale(middle) * gain_ref[...]).astype(BF)


def output_forward(flag, attended, x, gain, inmaps, outmaps, weights):
    own = x.shape[0]
    cols = weights[0].shape[0]
    heads = QUERY_HEADS // cols
    o_rows = heads * HEAD_SIZE
    half = pl.BlockSpec((1, *weights[0].shape[1:]), lambda c: (c, 0, 0, 0))
    whole = lambda c: (0, 0)
    step = lambda c: (c, 0, 0)
    return pl.pallas_call(
        output_forward_kernel,
        grid=(cols,),
        in_specs=[
            pl.BlockSpec(memory_space=pltpu.SMEM),
            pl.BlockSpec((heads, own, HEAD_SIZE), step),
            pl.BlockSpec(x.shape, whole),
            pl.BlockSpec(gain.shape, whole),
            pl.BlockSpec((1, LANES, o_rows), step),
            pl.BlockSpec(outmaps.shape, whole),
            half,
            half,
        ],
        out_specs=[
            pl.BlockSpec((own, MODEL_WIDTH), whole),
            pl.BlockSpec((own, MODEL_WIDTH), whole),
            pl.BlockSpec((own, LANES), whole),
        ],
        out_shape=[
            jax.ShapeDtypeStruct((own, MODEL_WIDTH), F32),
            jax.ShapeDtypeStruct((own, MODEL_WIDTH), BF),
            jax.ShapeDtypeStruct((own, LANES), BF),
        ],
        scratch_shapes=[pltpu.VMEM((own, MODEL_WIDTH), F32), pltpu.VMEM((own, LANES), F32)],
        compiler_params=pltpu.CompilerParams(vmem_limit_bytes=VMEM_LIMIT),
        cost_estimate=pl.CostEstimate(
            flops=2 * own * MODEL_WIDTH * MODEL_WIDTH,
            bytes_accessed=2 * MODEL_WIDTH * MODEL_WIDTH,
            transcendentals=own,
        ),
        name="output_forward",
    )(flag, attended, x, gain, inmaps, outmaps, *weights)


def output_backward_kernel(
    flag_ref,
    gh_ref,
    got_ref,
    cot_ref,
    middle_ref,
    gain_ref,
    a_ref,
    b_ref,
    att_ref,
    m_ref,
    own_ref,
    other_ref,
    gm_ref,
    sent_ref,
    gb_ref,
    ga_ref,
    low_ref,
    inner_ref,
):
    heads = sent_ref.shape[0]
    row_blocks, rank, features = gb_ref.shape

    @pl.when(pl.program_id(0) == 0)
    def _():
        grad_hidden = gh_ref[...] + got_ref[...].astype(F32)
        middle = middle_ref[...]
        grad = cot_ref[...].astype(F32) + norm_back(
            middle, norm_scale(middle), gain_ref[...], grad_hidden
        )
        gm_ref[...] = grad
        low_ref[...] = grad.astype(BF)
        inner_ref[...] = (ADAPTER_FACTOR * dot(low_ref[...], b_ref[...])).astype(BF)
        outer = ADAPTER_FACTOR * dot_tn(m_ref[...], low_ref[...])
        for r in range(row_blocks):
            gb_ref[r] = outer[:rank, r * features : (r + 1) * features]

    attended = jnp.concatenate([att_ref[h] for h in range(heads)], axis=1)
    ga_ref[0] = dot_tn(inner_ref[...], attended)[:rank, :]
    weights = whole_output_weights(flag_ref, own_ref, other_ref)
    grad = (dot_nt(low_ref[...], weights) + dot(inner_ref[...], a_ref[0])).astype(BF)
    for head in range(heads):
        sent_ref[head] = grad[:, head * HEAD_SIZE : (head + 1) * HEAD_SIZE]


def output_backward(
    flag, grad_hidden, got, cotangent, middle, gain, inmaps, outmaps, attended, masked, weights
):
    own = middle.shape[0]
    cols, row_blocks = weights[0].shape[:2]
    features = MODEL_WIDTH // row_blocks
    heads = QUERY_HEADS // cols
    o_rows = heads * HEAD_SIZE
    half = pl.BlockSpec((1, *weights[0].shape[1:]), lambda c: (c, 0, 0, 0))
    whole = lambda c: (0, 0)
    step = lambda c: (c, 0, 0)
    once = pl.Buffered(1)
    return pl.pallas_call(
        output_backward_kernel,
        grid=(cols,),
        in_specs=[
            pl.BlockSpec(memory_space=pltpu.SMEM),
            pl.BlockSpec((own, MODEL_WIDTH), whole, pipeline_mode=once),
            pl.BlockSpec((own, MODEL_WIDTH), whole, pipeline_mode=once),
            pl.BlockSpec((own, MODEL_WIDTH), whole, pipeline_mode=once),
            pl.BlockSpec((own, MODEL_WIDTH), whole, pipeline_mode=once),
            pl.BlockSpec(gain.shape, whole),
            pl.BlockSpec((1, LANES, o_rows), step),
            pl.BlockSpec(outmaps.shape, whole),
            pl.BlockSpec((heads, own, HEAD_SIZE), step),
            pl.BlockSpec(masked.shape, whole),
            half,
            half,
        ],
        out_specs=[
            pl.BlockSpec((own, MODEL_WIDTH), whole),
            pl.BlockSpec((heads, own, HEAD_SIZE), step),
            pl.BlockSpec((row_blocks, ADAPTER_RANK, features), lambda c: (0, 0, 0)),
            pl.BlockSpec((1, ADAPTER_RANK, o_rows), step),
        ],
        out_shape=[
            jax.ShapeDtypeStruct((own, MODEL_WIDTH), F32),
            jax.ShapeDtypeStruct((QUERY_HEADS, own, HEAD_SIZE), BF),
            jax.ShapeDtypeStruct((row_blocks, ADAPTER_RANK, features), F32),
            jax.ShapeDtypeStruct((cols, ADAPTER_RANK, o_rows), F32),
        ],
        scratch_shapes=[pltpu.VMEM((own, MODEL_WIDTH), BF), pltpu.VMEM((own, LANES), BF)],
        compiler_params=pltpu.CompilerParams(vmem_limit_bytes=VMEM_LIMIT),
        cost_estimate=pl.CostEstimate(
            flops=2 * own * MODEL_WIDTH * MODEL_WIDTH,
            bytes_accessed=2 * MODEL_WIDTH * MODEL_WIDTH,
            transcendentals=own,
        ),
        name="output_backward",
    )(
        flag,
        grad_hidden,
        got,
        cotangent,
        middle,
        gain,
        inmaps,
        outmaps,
        attended,
        masked,
        *weights,
    )


def feed_forward_kernel(
    first, last, group, h_ref, c_ref, mg_ref, mu_ref, nd_ref, mask_ref, ag_ref, au_ref, od_ref, *refs
):
    weight_refs, map_refs, refs = refs[:group], refs[group : 2 * group], refs[2 * group :]
    if first:
        previous = None
    else:
        previous, refs = refs[:5], refs[5:]
    if last:
        (gh_ref, out_ref, rows_ref), refs = refs[:3], refs[3:]
    else:
        accs, refs = refs[:5], refs[5:]
    grads_refs, refs = refs[:group], refs[group:]
    gh_acc, out_acc, md_acc, ig_acc, iu_acc = scratch = refs[:5]
    sems = refs[5]
    step = pl.program_id(0)
    row_blocks = weight_refs[0].shape[1]
    deep = MODEL_WIDTH // row_blocks
    used = mg_ref.shape[1]

    @pl.when(step == 0)
    def _():
        if first:
            for ref in scratch:
                ref[...] = jnp.zeros_like(ref)
        else:
            for i in range(5):
                pltpu.make_async_copy(previous[i], scratch[i], sems.at[i]).start()

    def side(kind, row):
        return jnp.concatenate([ref[0, row, kind] for ref in weight_refs], axis=1)

    def tall_side(kind):
        return jnp.concatenate([side(kind, row) for row in range(row_blocks)], axis=0)

    def down_side(row):
        return jnp.concatenate(
            [
                jnp.concatenate(
                    [ref[0, row, 2, at : at + LANES, :] for at in range(0, deep, LANES)], axis=1
                )
                for ref in weight_refs
            ],
            axis=0,
        )

    def maps(kind):
        return jnp.concatenate(
            [ref[0, kind * used : (kind + 1) * used, :] for ref in map_refs], axis=1
        )

    gate_map, up_map, down_map = maps(0), maps(1), maps(2)
    units = group * LANES
    gate_up = dot(h_ref[...], jnp.concatenate([tall_side(0), tall_side(1)], axis=1))
    gate = gate_up[:, :units] + ADAPTER_FACTOR * dot(mg_ref[...], gate_map)
    upward = gate_up[:, units:] + ADAPTER_FACTOR * dot(mu_ref[...], up_map)
    down = jnp.concatenate([down_side(row) for row in range(row_blocks)], axis=1)
    grad_act = dot_nt(c_ref[...], down) + dot(nd_ref[...], down_map)
    sigma = 1.0 / (1.0 + jnp.exp(-gate))
    swish = gate * sigma
    act = (swish * upward).astype(BF)
    grad_gate = (grad_act * upward * (sigma * (1.0 + gate * (1.0 - sigma)))).astype(BF)
    grad_up = (grad_act * swish).astype(BF)
    both = jnp.concatenate([grad_gate, grad_up], axis=1)
    if not first:

        @pl.when(step == 0)
        def _():
            for i in range(5):
                pltpu.make_async_copy(previous[i], scratch[i], sems.at[i]).wait()

    for row in range(row_blocks):
        at = slice(row * deep, (row + 1) * deep)
        gh_acc[:, at] += dot_nt(both, jnp.concatenate([side(0, row), side(1, row)], axis=1))
        out_acc[:, at] += dot(act, down_side(row))
    md_acc[...] += dot_nt(act, down_map)
    ig_acc[...] += dot_nt(grad_gate, gate_map)
    iu_acc[...] += dot_nt(grad_up, up_map)
    partial = (
        ADAPTER_FACTOR * dot_tn(mg_ref[...], grad_gate),
        ADAPTER_FACTOR * dot_tn(mu_ref[...], grad_up),
        dot_tn(nd_ref[...], act),
    )
    for kind in range(3):
        for i, ref in enumerate(grads_refs):
            ref[0, kind * used : (kind + 1) * used, :] = partial[kind][
                :, i * LANES : (i + 1) * LANES
            ]

    @pl.when(step == pl.num_programs(0) - 1)
    def _():
        if last:
            mask = mask_ref[...]
            inner_g = (ADAPTER_FACTOR * ig_acc[...] * mask).astype(BF)
            inner_u = (ADAPTER_FACTOR * iu_acc[...] * mask).astype(BF)
            masked = (md_acc[...] * mask).astype(BF)
            gh_ref[...] = (
                gh_acc[...] + dot_nt(inner_g, ag_ref[...]) + dot_nt(inner_u, au_ref[...])
            ).astype(gh_ref.dtype)
            out_ref[...] = (out_acc[...] + ADAPTER_FACTOR * dot_nt(masked, od_ref[...])).astype(
                out_ref.dtype
            )
            for row in range(row_blocks):
                at = slice(row * deep, (row + 1) * deep)
                rows_ref[row, :used, :] = dot_tn(inner_g, h_ref[:, at])
                rows_ref[row, used : 2 * used, :] = dot_tn(inner_u, h_ref[:, at])
                rows_ref[row, 2 * used :, :] = ADAPTER_FACTOR * dot_tn(masked, c_ref[:, at])
        else:
            copies = [pltpu.make_async_copy(scratch[i], accs[i], sems.at[i]) for i in range(5)]
            for copy in copies:
                copy.start()
            for copy in copies:
                copy.wait()


def slab_group(count):
    return 4 if count % 4 == 0 else 2


def feed_forward_chunk(hidden, cotangent, masks, tables, weights, maps, previous, last, dtype):
    first = previous is None
    cols, row_blocks, _, deep, _ = weights.shape
    slabs = maps.shape[0] // cols
    count, used = masks[0].shape
    whole = lambda i: (0, 0)
    once = pl.Buffered(1)
    group = slab_group(cols * slabs)
    steps = cols * slabs // group
    acc_shapes = [(count, MODEL_WIDTH)] * 2 + [(count, used)] * 3

    def weight_spec(side):
        def at(i):
            return ((group * i + side) // slabs, 0, (group * i + side) % slabs, 0, 0)

        return pl.BlockSpec((1, row_blocks, 3, deep, LANES), at)

    def slab_spec(side):
        return pl.BlockSpec((1, 3 * used, LANES), lambda i: (group * i + side, 0, 0))

    step_spec = pl.BlockSpec((1, 3 * used, LANES), lambda i: (i, 0, 0))
    in_specs = (
        [pl.BlockSpec((count, MODEL_WIDTH), whole, pipeline_mode=once)] * 2
        + [pl.BlockSpec((count, used), whole)] * 4
        + [pl.BlockSpec((MODEL_WIDTH, used), whole, pipeline_mode=once)] * 3
        + [weight_spec(side) for side in range(group)]
        + [slab_spec(side) for side in range(group)]
    )
    operands = [hidden, cotangent, *masks, *tables] + [weights] * group + [maps] * group
    if not first:
        in_specs = in_specs + [pl.BlockSpec(memory_space=pl.ANY)] * 5
        operands = operands + list(previous)
    if last:
        out_specs = [pl.BlockSpec((count, MODEL_WIDTH), whole)] * 2 + [
            pl.BlockSpec((row_blocks, 3 * used, deep), lambda i: (0, 0, 0))
        ]
        out_shape = [jax.ShapeDtypeStruct(s, dtype) for s in acc_shapes[:2]] + [
            jax.ShapeDtypeStruct((row_blocks, 3 * used, deep), F32)
        ]
    else:
        out_specs = [pl.BlockSpec(memory_space=pl.ANY)] * 5
        out_shape = [jax.ShapeDtypeStruct(s, F32) for s in acc_shapes]
    outs = pl.pallas_call(
        functools.partial(feed_forward_kernel, first, last, group),
        grid=(steps,),
        in_specs=in_specs,
        out_specs=out_specs + [step_spec] * group,
        out_shape=out_shape + [jax.ShapeDtypeStruct((steps, 3 * used, LANES), F32)] * group,
        scratch_shapes=[pltpu.VMEM(s, F32) for s in acc_shapes]
        + [pltpu.SemaphoreType.DMA((5,))],
        compiler_params=pltpu.CompilerParams(vmem_limit_bytes=VMEM_LIMIT),
        cost_estimate=pl.CostEstimate(
            flops=12 * count * MODEL_WIDTH * cols * slabs * LANES,
            bytes_accessed=cols * slabs * row_blocks * 3 * deep * LANES * 2,
            transcendentals=count * cols * slabs * LANES,
        ),
        name="feed_forward",
    )(*operands)
    return outs[:-group], outs[-group:]


def placed(ids_ref, first, second, count):
    zero = jnp.zeros_like(first)
    blocks = []
    for slot in range(count):
        blocks.append(
            jnp.where(ids_ref[0] == slot, first, zero)
            + jnp.where(ids_ref[1] == slot, second, zero)
        )
    return jnp.concatenate(blocks, axis=0)


def finish_middle_kernel(
    ids_ref, row_ref, col_ref, a_o, b_o, a_gate, b_gate, a_up, b_up, a_down, b_down
):
    rank = ADAPTER_RANK
    count = b_o.shape[0] // rank
    half = b_gate.shape[1] // 2

    def part(ref, tree, at):
        return ref[tree, at * rank : (at + 1) * rank, :].astype(F32)

    def both_planes(at):
        first = part(row_ref, 0, at) + part(row_ref, 1, at + 1)
        second = part(row_ref, 0, at + 1) + part(row_ref, 1, at)
        return placed(ids_ref, first, second, count)

    a_gate[...] = jnp.transpose(both_planes(0))
    a_up[...] = jnp.transpose(both_planes(2))
    b_down[...] = both_planes(4)
    b_o[...] = placed(ids_ref, part(row_ref, 0, 6), part(row_ref, 1, 6), count)
    o_rows = a_o.shape[0]
    a_o[...] = jnp.transpose(
        placed(ids_ref, part(col_ref, 0, 6)[:, :o_rows], part(col_ref, 1, 6)[:, :o_rows], count)
    )
    low_plane = ids_ref[2] == 0

    def halves(at):
        mine = placed(ids_ref, part(col_ref, 0, at), part(col_ref, 0, at + 1), count)[:, :half]
        theirs = placed(ids_ref, part(col_ref, 1, at + 1), part(col_ref, 1, at), count)[:, :half]
        return jnp.where(low_plane, mine, theirs), jnp.where(low_plane, theirs, mine)

    for at, out in ((0, b_gate), (2, b_up)):
        low, high = halves(at)
        out[:, :half] = low
        out[:, half:] = high
    low, high = halves(4)
    a_down[:half, :] = jnp.transpose(low)
    a_down[half:, :] = jnp.transpose(high)


def finish_end_kernel(ids_ref, row_ref, col_ref, a_q, b_q, a_k, b_k, a_v, b_v):
    rank = ADAPTER_RANK
    count = b_q.shape[0] // rank
    for at, out in enumerate((a_q, a_k, a_v)):
        rows = slice(at * rank, (at + 1) * rank)
        out[...] = jnp.transpose(
            placed(ids_ref, row_ref[0, rows, :].astype(F32), row_ref[1, rows, :].astype(F32), count)
        )
    start = 0
    for out in (b_q, b_k, b_v):
        lanes = slice(start, start + out.shape[1])
        out[...] = placed(
            ids_ref, col_ref[0, :, lanes].astype(F32), col_ref[1, :, lanes].astype(F32), count
        )
        start = start + out.shape[1]


def finish(kernel, ids, row_table, col_table, shapes, name):
    size = sum(shape[0] * shape[1] for shape in shapes)
    return pl.pallas_call(
        kernel,
        in_specs=[
            pl.BlockSpec(memory_space=pltpu.SMEM),
            pl.BlockSpec(memory_space=pltpu.VMEM),
            pl.BlockSpec(memory_space=pltpu.VMEM),
        ],
        out_specs=[pl.BlockSpec(memory_space=pltpu.VMEM)] * len(shapes),
        out_shape=[jax.ShapeDtypeStruct(shape, F32) for shape in shapes],
        cost_estimate=pl.CostEstimate(flops=size, bytes_accessed=8 * size, transcendentals=0),
        name=name,
    )(ids, row_table, col_table)


def lane_pad(values):
    return jnp.pad(values, ((0, 0),) * (values.ndim - 1) + ((0, LANES - values.shape[-1]),))


def row_pad(values):
    return jnp.pad(
        values, ((0, 0),) * (values.ndim - 2) + ((0, LANES - values.shape[-2]), (0, 0))
    )


def thirds(values):
    parts = []
    for _ in range(3):
        part = lax.reduce_precision(values, 8, 7)
        parts.append(part.astype(BF)[:, None])
        values = values - part
    return parts


def on_device(
    tokens,
    cotangent,
    attention_norm_gain,
    feedfwd_norm_gain,
    query_norm_gain,
    key_norm_gain,
    query_matrix,
    key_matrix,
    value_matrix,
    output_matrix,
    gate_matrix,
    up_matrix,
    down_matrix,
    query_adapter_inmaps,
    query_adapter_outmaps,
    key_adapter_inmaps,
    key_adapter_outmaps,
    value_adapter_inmaps,
    value_adapter_outmaps,
    output_adapter_inmaps,
    output_adapter_outmaps,
    gate_adapter_inmaps,
    gate_adapter_outmaps,
    up_adapter_inmaps,
    up_adapter_outmaps,
    down_adapter_inmaps,
    down_adapter_outmaps,
    segment,
    depth,
    parent,
    adapter,
):
    rows = lax.axis_size("row")
    cols = lax.axis_size("col")
    devices = rows * cols
    repeat = devices // QUERY_HEADS
    plane = lax.axis_index("dp")
    row = lax.axis_index("row")
    col = lax.axis_index("col")
    length = segment.shape[0]
    own = tokens.shape[0] // rows
    columns = query_adapter_inmaps.shape[1]
    rank = ADAPTER_RANK
    swap = [(0, 1), (1, 0)]
    pairs = [(r, r ^ repeat) for r in range(rows)]
    q_local = query_matrix.shape[1]
    kv_local = key_matrix.shape[1]
    wide = q_local + 2 * kv_local
    features = gate_matrix.shape[0]

    own_adapter = adapter[0]
    other_adapter = lax.ppermute(adapter, "dp", swap)[0]
    both = (own_adapter, other_adapter)

    def inmap(table, at):
        return lax.dynamic_slice_in_dim(table, at * rank, rank, 1)

    def outmap(table, at):
        return lax.dynamic_slice_in_dim(table, at * rank, rank, 0)

    qkv_local = jnp.concatenate([query_matrix, key_matrix, value_matrix], axis=1)

    def block_of(table, before, after):
        return jnp.pad(outmap(table, own_adapter), ((0, 0), (before, after)))

    qkv_maps = jnp.concatenate(
        [
            block_of(query_adapter_outmaps, 0, 2 * kv_local),
            block_of(key_adapter_outmaps, q_local, kv_local),
            block_of(value_adapter_outmaps, q_local + kv_local, 0),
        ],
        axis=0,
    )
    attention_pack = jnp.concatenate(
        [
            table[:, at : at + features]
            for table in (qkv_local, qkv_maps)
            for at in range(0, wide, features)
        ]
        + [
            lax.dynamic_slice_in_dim(
                output_matrix, plane * (output_matrix.shape[0] // 2), output_matrix.shape[0] // 2, 0
            )
        ],
        axis=0,
    )
    attention_weights = lax.all_gather(attention_pack, PLANE, axis=0, tiled=True).reshape(
        cols, rows, -1, features
    )
    o_rows = output_matrix.shape[0]
    own_output_weights = attention_weights[:, :, -(o_rows // 2) :]
    plane_flag = plane.astype(jnp.int32).reshape(1)
    ffn_half = gate_matrix.shape[1] // 2
    half_start = plane * ffn_half
    chunks = 2 if ffn_half % 256 == 0 else 3
    width = ffn_half // chunks
    slabs = width // LANES

    def plates(table):
        return [table[:, at : at + LANES] for at in range(0, table.shape[1], LANES)]

    def half_of(table):
        return lax.dynamic_slice_in_dim(table, half_start, ffn_half, 1)

    map_width = max(ffn_half, o_rows)

    def to_width(table):
        return jnp.pad(table, ((0, 0), (0, map_width - table.shape[1])))

    col_pack = jnp.concatenate(
        [
            *[to_width(half_of(outmap(gate_adapter_outmaps, a))) for a in both],
            *[to_width(half_of(outmap(up_adapter_outmaps, a))) for a in both],
            *[to_width(half_of(inmap(down_adapter_inmaps, a).T)) for a in both],
            to_width(inmap(output_adapter_inmaps, own_adapter).T),
            jnp.zeros((rank, map_width), BF),
        ],
        axis=0,
    )
    map_rows = col_pack.shape[0] // rows
    map_plates = plates(lax.dynamic_slice_in_dim(col_pack, row * map_rows, map_rows, 0))
    ffn_weights = []
    for chunk in range(chunks):
        pack = []
        for slab in range(slabs):
            start = half_start + (chunk * slabs + slab) * LANES
            pack.append(lax.dynamic_slice_in_dim(gate_matrix, start, LANES, 1))
            pack.append(lax.dynamic_slice_in_dim(up_matrix, start, LANES, 1))
            pack.extend(plates(lax.dynamic_slice_in_dim(down_matrix, start, LANES, 0)))
        if chunk == 0:
            spare = features - map_rows * len(map_plates)
            pack = pack + map_plates + [jnp.zeros((spare, LANES), BF)]
        pack = jnp.concatenate(pack, axis=0)
        ffn_weights.append(
            lax.all_gather(pack, PLANE, axis=0, tiled=True).reshape(
                cols, rows, -1, features, LANES
            )
        )
    col_maps = ffn_weights[0][:, :, -1, : map_rows * len(map_plates)].reshape(
        cols, rows, len(map_plates), map_rows, LANES
    )
    col_maps = jnp.transpose(col_maps, (0, 2, 1, 3, 4)).reshape(
        cols, len(map_plates), rows * map_rows, LANES
    )
    in_o = jnp.transpose(col_maps[:, : o_rows // LANES, 6 * rank : 7 * rank], (0, 2, 1, 3))
    in_o = row_pad(in_o.reshape(cols, rank, o_rows))

    row_pack = jnp.concatenate(
        [
            inmap(query_adapter_inmaps, own_adapter),
            inmap(key_adapter_inmaps, own_adapter),
            inmap(value_adapter_inmaps, own_adapter),
            *[inmap(gate_adapter_inmaps, a) for a in both],
            *[inmap(up_adapter_inmaps, a) for a in both],
            *[outmap(down_adapter_outmaps, a).T for a in both],
            outmap(output_adapter_outmaps, own_adapter).T,
            *thirds(attention_norm_gain),
            *thirds(feedfwd_norm_gain),
        ],
        axis=1,
    )

    row_maps = lax.all_gather(row_pack, "row", axis=0, tiled=True)
    in_qkv = row_maps[:, : 3 * rank]
    in_gate = row_maps[:, 3 * rank : 5 * rank]
    in_up = row_maps[:, 5 * rank : 7 * rank]
    out_down = row_maps[:, 7 * rank : 9 * rank]
    out_o = lane_pad(row_maps[:, 9 * rank : 10 * rank])
    gain_parts = row_maps[:, 10 * rank :].astype(F32)
    gain_one = (gain_parts[:, 0] + (gain_parts[:, 1] + gain_parts[:, 2])).reshape(1, -1)
    gain_two = (gain_parts[:, 3] + (gain_parts[:, 4] + gain_parts[:, 5])).reshape(1, -1)

    own_tokens = lax.all_to_all(tokens, "row", 0, 1, tiled=True)
    own_cotangent = lax.all_to_all(cotangent, "row", 0, 1, tiled=True)
    other_cotangent = lax.ppermute(own_cotangent, "dp", swap)
    own_tokens, other_cotangent, own_output_weights = lax.optimization_barrier(
        (own_tokens, other_cotangent, own_output_weights)
    )
    other_output_weights = lax.ppermute(own_output_weights, "dp", swap)
    head_gains = jnp.stack([query_norm_gain, key_norm_gain], axis=0)
    token_start = (col * rows + row) * own
    positions = lax.dynamic_slice_in_dim(depth, token_start, own, 0).astype(F32)
    half = HEAD_SIZE // 2
    freqs = THETA ** (-2.0 * jnp.arange(half).astype(F32) / HEAD_SIZE)
    angle = positions[:, None] * freqs[None, :]
    cosine = jnp.tile(jnp.cos(angle), (1, 2))
    sine = jnp.concatenate([-jnp.sin(angle), jnp.sin(angle)], axis=1)

    masked_qkv, pre, sent = qkv_forward(
        own_tokens, gain_one, in_qkv, cosine, sine, head_gains, attention_weights
    )

    def to_heads(sent):
        if repeat > 1:
            sent = jnp.repeat(sent, repeat, axis=0)
        return lax.all_to_all(sent, PLANE, 0, 0, tiled=True).reshape(length, sent.shape[2])

    def to_tokens(lines):
        got = lax.all_to_all(
            lines.reshape(devices, own, lines.shape[1]), PLANE, 0, 0, tiled=True
        )
        return got[::repeat] if repeat > 1 else got

    got, other_output_weights = lax.optimization_barrier((to_heads(sent), other_output_weights))
    output_weights = (own_output_weights, other_output_weights)
    theirs = lax.ppermute(got[:, HEAD_SIZE:], "row", pairs)
    flag = (1 - (row // repeat) % 2).astype(jnp.int32).reshape(1)

    block_node = segment.reshape(-1, SEG_LEN)[:, 0]
    nodes = jnp.arange(parent.shape[1])
    node_parent = jnp.sum(jnp.where(block_node[:, None] == nodes, parent.reshape(1, -1), 0), axis=1)
    block_index = jnp.arange(block_node.shape[0])
    parent_block = jnp.max(
        jnp.where(node_parent[:, None] == block_node[None, :], block_index[None, :], 0), axis=1
    )
    parent_block = jnp.where(node_parent > 0, parent_block, -1).astype(jnp.int32)
    head_attended, head_low, totals = attention_forward(parent_block, flag, got, theirs)
    attended = to_tokens(head_low)

    middle, hidden_ffn, masked_o = output_forward(
        plane_flag, attended, own_tokens, gain_two, in_o, out_o, output_weights
    )

    other_ffn = lax.ppermute(hidden_ffn, "dp", swap)
    tables = (in_gate, in_up, out_down)
    column_tree = jnp.arange(2 * rank)[None, :] // rank

    def masks_of(hidden, cot, tree):
        mask = jnp.broadcast_to((column_tree == tree).astype(F32), (own, 2 * rank))
        return (
            (dot(hidden, in_gate) * mask).astype(BF),
            (dot(hidden, in_up) * mask).astype(BF),
            (ADAPTER_FACTOR * dot(cot, out_down) * mask).astype(BF),
            mask,
        )

    parts = []

    def run(chunk, side, masks, accs):
        hidden, cot = side
        maps = col_maps[:, chunk * slabs : (chunk + 1) * slabs].reshape(cols * slabs, -1, LANES)
        last = chunk == chunks - 1
        return feed_forward_chunk(
            hidden,
            cot,
            masks,
            tables,
            ffn_weights[chunk],
            maps,
            accs,
            last,
            F32 if side is own_side else BF,
        )

    own_side = (hidden_ffn, own_cotangent)
    own_masks = masks_of(*own_side, 0)
    here, own_part = run(0, own_side, own_masks, None)
    other_ffn, here = lax.optimization_barrier((other_ffn, here))
    other_side = (other_ffn, other_cotangent)
    other_masks = masks_of(*other_side, 1)
    there, other_part = run(0, other_side, other_masks, None)
    parts = [(own_part, other_part)]
    for chunk in range(1, chunks):
        there, other_part = run(chunk, other_side, other_masks, there)
        here, own_part = run(chunk, own_side, own_masks, here)
        parts.append((own_part, other_part))

    def slab_order(part):
        part = [first + second for first, second in zip(*part)]
        part = jnp.stack(part, axis=1).reshape(cols, slabs, 6 * rank, LANES)
        return jnp.transpose(part, (0, 2, 1, 3)).reshape(cols, 6 * rank, width)

    parts = [slab_order(part) for part in parts]
    gh_other = lax.ppermute(there[0], "dp", swap)

    grad_middle, sent, grad_o_rows, grad_o_cols = output_backward(
        plane_flag,
        here[0],
        gh_other,
        own_cotangent,
        middle,
        gain_two,
        in_o,
        out_o,
        attended,
        masked_o,
        output_weights,
    )
    out_sent, sent = lax.optimization_barrier((there[1], sent))
    out_other = lax.ppermute(out_sent, "dp", swap)
    head_grad = to_heads(sent)

    def pieces_of(row_table, col_table):
        row_table = jnp.swapaxes(row_table.astype(BF).reshape(rows, cols, -1, LANES), 0, 1)
        col_table = col_table.astype(BF).reshape(cols, rows, -1, LANES)
        return jnp.concatenate([row_table, col_table], axis=2).reshape(devices, -1, LANES)

    def gathered(values, axis, at):
        size = lax.axis_size(axis)
        whole = jnp.zeros((2, size, *values.shape[1:]), values.dtype)
        for k in range(size):
            block = values
            if k:
                block = lax.ppermute(values, axis, [(i, i ^ k) for i in range(size)])
            whole = lax.dynamic_update_index_in_dim(whole, block, at ^ k, 1)
        return whole

    def summed(pieces):
        mine = jnp.sum(pieces.astype(F32), axis=0).astype(BF)
        return jnp.stack([mine, lax.ppermute(mine, "dp", swap)], axis=0)

    def gathered_tables(pieces, row_highs, col_highs):
        row_parts = [high * features // (cols * LANES) for high in row_highs]
        row_pieces = [piece[:, :part] for piece, part in zip(pieces, row_parts)]
        col_pieces = [piece[:, part:] for piece, part in zip(pieces, row_parts)]
        row_whole = gathered(jnp.concatenate(row_pieces, axis=1), "col", col)
        col_whole = gathered(jnp.concatenate(col_pieces, axis=1), "row", row)
        tables = []
        row_at = col_at = 0
        for i, (row_high, col_high) in enumerate(zip(row_highs, col_highs)):
            row_size, col_size = row_pieces[i].shape[1], col_pieces[i].shape[1]
            tables.append(
                (
                    row_whole[:, :, row_at : row_at + row_size].reshape(2, row_high, features),
                    col_whole[:, :, col_at : col_at + col_size].reshape(2, col_high, -1),
                )
            )
            row_at, col_at = row_at + row_size, col_at + col_size
        return tables

    def to_own_features(lines):
        blocks = lines.reshape(own, rows, features)
        whole = jnp.zeros((rows, own, features), lines.dtype)
        for k in range(rows):
            block = lax.dynamic_index_in_dim(blocks, row ^ k, 1, False)
            if k:
                block = lax.ppermute(block, "row", [(r, r ^ k) for r in range(rows)])
            whole = lax.dynamic_update_index_in_dim(whole, block, row ^ k, 0)
        return whole.reshape(rows * own, features)

    def to_map_width(table):
        return jnp.pad(table, ((0, 0), (0, 0), (0, map_width - table.shape[2])))

    mid_pieces = pieces_of(
        jnp.concatenate([here[2] + there[2], grad_o_rows], axis=1),
        jnp.concatenate(
            [to_map_width(jnp.concatenate(parts, axis=2)), to_map_width(grad_o_cols)], axis=1
        ),
    )
    head_grad, mid_pieces = lax.optimization_barrier((head_grad, mid_pieces))
    mid_pieces = lax.all_to_all(mid_pieces, PLANE, 0, 0, tiled=True)

    lines, kept, given = attention_backward(
        parent_block, flag, got, head_grad, head_attended, totals, theirs
    )
    lines, kept, given, mid_pieces, out_other = lax.optimization_barrier(
        (lines, kept, given, mid_pieces, out_other)
    )
    returned = to_tokens(merge(lines, kept, lax.ppermute(given, "row", pairs)))
    output = (middle + here[1] + out_other.astype(F32)).astype(BF)
    output = to_own_features(output)
    returned, output, mid_pieces = lax.optimization_barrier(
        (returned, output, summed(mid_pieces))
    )

    grads_qkv, inner_qkv, row_end, col_end = qkv_unshape(
        returned,
        pre,
        masked_qkv,
        own_tokens,
        gain_one,
        cosine,
        sine,
        head_gains,
        attention_weights,
    )
    end_pieces = lax.all_to_all(pieces_of(row_end, col_end), PLANE, 0, 0, tiled=True)
    grad_low = qkv_backward(
        grads_qkv, inner_qkv, own_tokens, grad_middle, gain_one, in_qkv, attention_weights
    )
    grad_low, end_pieces = lax.optimization_barrier((grad_low, end_pieces))
    input_gradient = lax.all_to_all(grad_low, "row", 1, 0, tiled=True).astype(F32)
    mid_tables, end_tables = gathered_tables(
        (mid_pieces, summed(end_pieces)), (7 * rank, 3 * rank), (7 * rank, rank)
    )
    ids = jnp.stack([own_adapter, other_adapter, plane]).astype(jnp.int32)
    down_rows = down_matrix.shape[0]
    wide_a, wide_o, wide_d = (features, columns), (o_rows, columns), (down_rows, columns)
    finished = finish(
        finish_middle_kernel,
        ids,
        *mid_tables,
        [
            wide_o,
            (columns, features),
            wide_a,
            (columns, down_rows),
            wide_a,
            (columns, down_rows),
            wide_d,
            (columns, features),
        ],
        "finish_middle",
    )
    finished_qkv = finish(
        finish_end_kernel,
        ids,
        *end_tables,
        [wide_a, (columns, q_local), wide_a, (columns, kv_local), wide_a, (columns, kv_local)],
        "finish_end",
    )

    return (output, input_gradient, *finished_qkv, *finished)


def solution(mesh):
    return jax.shard_map(
        on_device,
        mesh=mesh,
        in_specs=(
            P(("dp", "col"), "row"),
            P(("dp", "col"), "row"),
            P("row"),
            P("row"),
            P(),
            P(),
            P("row", "col"),
            P("row", "col"),
            P("row", "col"),
            P("col", "row"),
            P("row", "col"),
            P("row", "col"),
            P("col", "row"),
            P("row", None),
            P(None, "col"),
            P("row", None),
            P(None, "col"),
            P("row", None),
            P(None, "col"),
            P("col", None),
            P(None, "row"),
            P("row", None),
            P(None, "col"),
            P("row", None),
            P(None, "col"),
            P("col", None),
            P(None, "row"),
            P("dp"),
            P("dp"),
            P("dp", None),
            P("dp"),
        ),
        out_specs=(
            P(("dp", "col"), "row"),
            P(("dp", "col"), "row"),
            P("row", None),
            P(None, "col"),
            P("row", None),
            P(None, "col"),
            P("row", None),
            P(None, "col"),
            P("col", None),
            P(None, "row"),
            P("row", None),
            P(None, "col"),
            P("row", None),
            P(None, "col"),
            P("col", None),
            P(None, "row"),
        ),
        check_vma=False,
    )
```

```python
import functools
import math

import jax
import jax.numpy as jnp
from jax import lax
from jax.experimental import pallas as pl
from jax.experimental.pallas import tpu as pltpu
from jax.sharding import PartitionSpec as P

MODEL_WIDTH = 2048
QUERY_HEADS = 16
KEY_VALUE_HEADS = 8
HEAD_SIZE = 128
ADAPTER_RANK = 16
TREE_LEN = 5120
TRUNK = 2048
SEG_LEN = 256
QUERY_BLOCK = 512
KEY_BLOCK = 1024

EPSILON = 1e-06
THETA = 1000000.0
ADAPTER_FACTOR = 2.0
BF = jnp.bfloat16
F32 = jnp.float32
SCALE = HEAD_SIZE ** (-0.5)
SCALE_LOG2 = SCALE * math.log2(math.e)
PLANE = ("col", "row")
LANES = 128
VMEM_LIMIT = 63 * 1024 * 1024


def dot(left, right):
    return jnp.dot(left, right, preferred_element_type=F32)


def dot_nt(left, right):
    return lax.dot_general(left, right, (((1,), (1,)), ((), ())), preferred_element_type=F32)


def dot_tn(left, right):
    return lax.dot_general(left, right, (((0,), (0,)), ((), ())), preferred_element_type=F32)


def walk_keys(index, parent_ref, step):
    trunk_blocks = TRUNK // QUERY_BLOCK

    @pl.when(index < trunk_blocks)
    def _():
        @pl.loop(0, index)
        def _(block):
            step(pl.multiple_of(block * QUERY_BLOCK, QUERY_BLOCK), QUERY_BLOCK)

        step(pl.multiple_of(index * QUERY_BLOCK, QUERY_BLOCK), QUERY_BLOCK, causal=True)

    @pl.when(index >= trunk_blocks)
    def _():
        for part in range(TRUNK // KEY_BLOCK):
            step(part * KEY_BLOCK, KEY_BLOCK)
        for side in range(QUERY_BLOCK // SEG_LEN):
            block = index * (QUERY_BLOCK // SEG_LEN) + side
            first = side * SEG_LEN
            start = pl.multiple_of(block * SEG_LEN, SEG_LEN)
            step(start, SEG_LEN, first, SEG_LEN, True)
            above = parent_ref[block]

            @pl.when(above >= 0)
            def _():
                step(pl.multiple_of(above * SEG_LEN, SEG_LEN), SEG_LEN, first, SEG_LEN)


def attention_forward_kernel(
    parent_ref, flag_ref, q_ref, mine_ref, theirs_ref, o_ref, low_ref, l_ref, k_ref, v_ref, acc_ref
):
    index = pl.program_id(0)

    @pl.when(index == 0)
    def _():
        lane = lax.broadcasted_iota(jnp.int32, (v_ref.shape[0], HEAD_SIZE), 1)
        v_ref[:, HEAD_SIZE:] = jnp.where(lane == 0, 1.0, 0.0).astype(BF)

        @pl.when(flag_ref[0] == 1)
        def _():
            k_ref[...] = mine_ref[...]
            v_ref[:, :HEAD_SIZE] = theirs_ref[...]

        @pl.when(flag_ref[0] != 1)
        def _():
            k_ref[...] = theirs_ref[...]
            v_ref[:, :HEAD_SIZE] = mine_ref[...]

    acc_ref[...] = jnp.zeros_like(acc_ref)

    def step(start, size, first=0, count=QUERY_BLOCK, causal=False):
        rows = pl.ds(start, size)
        at = pl.ds(first, count)
        scores = dot_nt(q_ref[at, :], k_ref[rows, :])
        probs = jnp.exp2(scores * SCALE_LOG2)
        if causal:
            ahead = lax.broadcasted_iota(jnp.int32, probs.shape, 0)
            behind = lax.broadcasted_iota(jnp.int32, probs.shape, 1)
            probs = jnp.where(behind <= ahead, probs, 0.0)
        acc_ref[at, :] += dot(probs.astype(BF), v_ref[rows, :])

    walk_keys(index, parent_ref, step)
    total = acc_ref[:, HEAD_SIZE : HEAD_SIZE + 1]
    attended = acc_ref[:, :HEAD_SIZE] / total
    o_ref[...] = attended
    low_ref[...] = attended.astype(BF)
    spread = jnp.broadcast_to(total, (QUERY_BLOCK, LANES))
    l_ref[0] = jnp.transpose(spread)[:8, :]


def attention_forward(parent_block, flag, got, theirs):
    length = theirs.shape[0]
    blocks = length // QUERY_BLOCK
    whole = lambda i, p, f: (0, 0)
    part = lambda i, p, f: (i, 0)
    return pl.pallas_call(
        attention_forward_kernel,
        grid_spec=pltpu.PrefetchScalarGridSpec(
            num_scalar_prefetch=2,
            grid=(blocks,),
            in_specs=[
                pl.BlockSpec((QUERY_BLOCK, HEAD_SIZE), part),
                pl.BlockSpec((length, HEAD_SIZE), lambda i, p, f: (0, 1)),
                pl.BlockSpec((length, HEAD_SIZE), whole),
            ],
            out_specs=[
                pl.BlockSpec((QUERY_BLOCK, HEAD_SIZE), part),
                pl.BlockSpec((QUERY_BLOCK, HEAD_SIZE), part),
                pl.BlockSpec((1, 8, QUERY_BLOCK), lambda i, p, f: (i, 0, 0)),
            ],
            scratch_shapes=[
                pltpu.VMEM((length, HEAD_SIZE), BF),
                pltpu.VMEM((length, 2 * HEAD_SIZE), BF),
                pltpu.VMEM((QUERY_BLOCK, 2 * HEAD_SIZE), F32),
            ],
        ),
        out_shape=[
            jax.ShapeDtypeStruct((length, HEAD_SIZE), F32),
            jax.ShapeDtypeStruct((length, HEAD_SIZE), BF),
            jax.ShapeDtypeStruct((blocks, 8, QUERY_BLOCK), F32),
        ],
        compiler_params=pltpu.CompilerParams(vmem_limit_bytes=VMEM_LIMIT),
        cost_estimate=pl.CostEstimate(
            flops=160 * SEG_LEN * SEG_LEN * HEAD_SIZE * 4,
            bytes_accessed=length * HEAD_SIZE * 12,
            transcendentals=160 * SEG_LEN * SEG_LEN,
        ),
        name="attention_forward",
    )(parent_block, flag, got, got, theirs)


def attention_backward_kernel(
    parent_ref,
    flag_ref,
    q_ref,
    g_ref,
    o_ref,
    l_ref,
    mine_ref,
    theirs_ref,
    dq_ref,
    kept_ref,
    given_ref,
    k_ref,
    v_ref,
    kt_ref,
    dk_ref,
    dv_ref,
    acc_ref,
    delta_ref,
    inverse_ref,
):
    index = pl.program_id(0)

    @pl.when(index == 0)
    def _():
        dk_ref[...] = jnp.zeros_like(dk_ref)
        dv_ref[...] = jnp.zeros_like(dv_ref)

        @pl.when(flag_ref[0] == 1)
        def _():
            k_ref[...] = mine_ref[...]
            v_ref[...] = theirs_ref[...]

        @pl.when(flag_ref[0] != 1)
        def _():
            k_ref[...] = theirs_ref[...]
            v_ref[...] = mine_ref[...]

        @pl.loop(0, k_ref.shape[0] // SEG_LEN)
        def _(block):
            rows = pl.ds(pl.multiple_of(block * SEG_LEN, SEG_LEN), SEG_LEN)
            kt_ref[:, rows] = jnp.transpose(k_ref[rows, :])

    delta = jnp.sum(g_ref[...].astype(F32) * o_ref[...], axis=1, keepdims=True)
    delta_ref[...] = jnp.transpose(jnp.broadcast_to(delta, (QUERY_BLOCK, LANES)))[:8, :]
    inverse_ref[...] = 1.0 / l_ref[0]
    acc_ref[...] = jnp.zeros_like(acc_ref)

    def step(start, size, first=0, count=QUERY_BLOCK, causal=False):
        rows = pl.ds(start, size)
        at = pl.ds(first, count)
        query = q_ref[at, :]
        grad = g_ref[at, :]
        probs = jnp.exp2(dot_nt(k_ref[rows, :], query) * SCALE_LOG2) * inverse_ref[:1, at]
        if causal:
            behind = lax.broadcasted_iota(jnp.int32, probs.shape, 0)
            ahead = lax.broadcasted_iota(jnp.int32, probs.shape, 1)
            probs = jnp.where(behind <= ahead, probs, 0.0)
        dprobs = dot_nt(v_ref[rows, :], grad)
        dscores = (probs * (dprobs - delta_ref[:1, at])).astype(BF)
        dv_ref[rows, :] += dot(probs.astype(BF), grad)
        dk_ref[rows, :] += dot(dscores, query)
        acc_ref[:, at] += dot(kt_ref[:, rows], dscores)

    walk_keys(index, parent_ref, step)
    dq_ref[...] = (jnp.transpose(acc_ref[...]) * SCALE).astype(BF)

    @pl.when(index == pl.num_programs(0) - 1)
    def _():
        @pl.when(flag_ref[0] == 1)
        def _():
            kept_ref[...] = dk_ref[...] * SCALE
            given_ref[...] = dv_ref[...].astype(BF)

        @pl.when(flag_ref[0] != 1)
        def _():
            kept_ref[...] = dv_ref[...]
            given_ref[...] = (dk_ref[...] * SCALE).astype(BF)


def attention_backward(parent_block, flag, got, grad, attended, totals, theirs):
    length = theirs.shape[0]
    blocks = length // QUERY_BLOCK
    whole = lambda i, p, f: (0, 0)
    part = lambda i, p, f: (i, 0)
    return pl.pallas_call(
        attention_backward_kernel,
        grid_spec=pltpu.PrefetchScalarGridSpec(
            num_scalar_prefetch=2,
            grid=(blocks,),
            in_specs=[
                pl.BlockSpec((QUERY_BLOCK, HEAD_SIZE), part),
                pl.BlockSpec((QUERY_BLOCK, HEAD_SIZE), part),
                pl.BlockSpec((QUERY_BLOCK, HEAD_SIZE), part),
                pl.BlockSpec((1, 8, QUERY_BLOCK), lambda i, p, f: (i, 0, 0)),
                pl.BlockSpec((length, HEAD_SIZE), lambda i, p, f: (0, 1)),
                pl.BlockSpec((length, HEAD_SIZE), whole),
            ],
            out_specs=[
                pl.BlockSpec((QUERY_BLOCK, HEAD_SIZE), part),
                pl.BlockSpec((length, HEAD_SIZE), whole),
                pl.BlockSpec((length, HEAD_SIZE), whole),
            ],
            scratch_shapes=[
                pltpu.VMEM((length, HEAD_SIZE), BF),
                pltpu.VMEM((length, HEAD_SIZE), BF),
                pltpu.VMEM((HEAD_SIZE, length), BF),
                pltpu.VMEM((length, HEAD_SIZE), F32),
                pltpu.VMEM((length, HEAD_SIZE), F32),
                pltpu.VMEM((HEAD_SIZE, QUERY_BLOCK), F32),
                pltpu.VMEM((8, QUERY_BLOCK), F32),
                pltpu.VMEM((8, QUERY_BLOCK), F32),
            ],
        ),
        out_shape=[
            jax.ShapeDtypeStruct((length, 2 * HEAD_SIZE), BF),
            jax.ShapeDtypeStruct((length, HEAD_SIZE), F32),
            jax.ShapeDtypeStruct((length, HEAD_SIZE), BF),
        ],
        compiler_params=pltpu.CompilerParams(vmem_limit_bytes=VMEM_LIMIT),
        cost_estimate=pl.CostEstimate(
            flops=160 * SEG_LEN * SEG_LEN * HEAD_SIZE * 10,
            bytes_accessed=length * HEAD_SIZE * 24,
            transcendentals=160 * SEG_LEN * SEG_LEN,
        ),
        name="attention_backward",
    )(parent_block, flag, got, grad, attended, totals, got, theirs)


def merge_kernel(lines_ref, kept_ref, got_ref, out_ref):
    out_ref[...] = (kept_ref[...] + got_ref[...].astype(F32)).astype(BF)


def merge(lines, kept, got):
    length = kept.shape[0]
    rows = 4 * SEG_LEN
    part = pl.BlockSpec((rows, HEAD_SIZE), lambda i: (i, 0))
    return pl.pallas_call(
        merge_kernel,
        grid=(length // rows,),
        in_specs=[pl.BlockSpec(memory_space=pl.ANY), part, part],
        out_specs=pl.BlockSpec((rows, HEAD_SIZE), lambda i: (i, 1)),
        out_shape=jax.ShapeDtypeStruct(lines.shape, lines.dtype),
        input_output_aliases={0: 0},
        cost_estimate=pl.CostEstimate(
            flops=length * HEAD_SIZE, bytes_accessed=length * HEAD_SIZE * 10, transcendentals=0
        ),
        name="merge",
    )(lines, kept, got)


def norm_scale(values):
    return lax.rsqrt(jnp.mean(values * values, axis=1, keepdims=True) + EPSILON)


def norm_back(values, scale, gain, gradient):
    weighted = gain * gradient
    inner_sum = jnp.sum(weighted * values, axis=1, keepdims=True)
    return scale * weighted - values * (scale**3 * (inner_sum * (1.0 / MODEL_WIDTH)))


def outmaps_of(w_ref, pieces, piece, used):
    at = pieces * piece
    return jnp.concatenate(
        [w_ref[0, 0, at + p * used : at + (p + 1) * used, :] for p in range(pieces)], axis=1
    )


def qkv_forward_kernel(
    x_ref,
    gain_ref,
    a_ref,
    cos_ref,
    sin_ref,
    hg_ref,
    w_ref,
    m_ref,
    pre_ref,
    sent_ref,
    hidden_ref,
):
    row_blocks = w_ref.shape[1]
    piece = w_ref.shape[3]
    pieces = w_ref.shape[2] // piece
    heads = sent_ref.shape[0]
    used = m_ref.shape[1]

    @pl.when(pl.program_id(0) == 0)
    def _():
        resid = x_ref[...].astype(F32)
        hidden_ref[...] = (resid * norm_scale(resid) * gain_ref[...]).astype(BF)
        m_ref[...] = dot(hidden_ref[...], a_ref[...]).astype(BF)

    hidden = hidden_ref[...]
    whole = jnp.concatenate(
        [
            dot(
                hidden,
                jnp.concatenate(
                    [w_ref[0, r, p * piece : (p + 1) * piece, :] for r in range(row_blocks)], axis=0
                ),
            )
            for p in range(pieces)
        ],
        axis=1,
    ) + ADAPTER_FACTOR * dot(m_ref[...], outmaps_of(w_ref, pieces, piece, used))
    pre_ref[0] = whole[:, : pre_ref.shape[2]]
    cosine = cos_ref[...]
    sine = sin_ref[...]

    def shaped(at, gain):
        lines = whole[:, at : at + HEAD_SIZE]
        normed = lines * norm_scale(lines) * gain
        return (normed * cosine + pltpu.roll(normed, HEAD_SIZE // 2, 1) * sine).astype(BF)

    for head in range(heads):
        sent_ref[head, :, :HEAD_SIZE] = shaped(head * HEAD_SIZE, hg_ref[0:1, :])
    key_at = heads * HEAD_SIZE
    value_at = key_at + heads // 2 * HEAD_SIZE
    for pair in range(heads // 2):
        at = pair * HEAD_SIZE
        sent_ref[2 * pair, :, HEAD_SIZE:] = shaped(key_at + at, hg_ref[1:2, :])
        sent_ref[2 * pair + 1, :, HEAD_SIZE:] = whole[
            :, value_at + at : value_at + at + HEAD_SIZE
        ].astype(BF)


def qkv_forward(x, gain, inmaps, cosine, sine, head_gains, weights):
    own = x.shape[0]
    cols, row_blocks, tall, piece = weights.shape
    wide = tall // piece * piece
    used = inmaps.shape[1]
    heads = QUERY_HEADS // cols
    whole = lambda c: (0, 0)
    step = lambda c: (c, 0, 0)
    return pl.pallas_call(
        qkv_forward_kernel,
        grid=(cols,),
        in_specs=[
            pl.BlockSpec(x.shape, whole),
            pl.BlockSpec(gain.shape, whole),
            pl.BlockSpec(inmaps.shape, whole),
            pl.BlockSpec(cosine.shape, whole),
            pl.BlockSpec(sine.shape, whole),
            pl.BlockSpec(head_gains.shape, whole),
            pl.BlockSpec((1, row_blocks, tall, piece), lambda c: (c, 0, 0, 0)),
        ],
        out_specs=[
            pl.BlockSpec((own, used), whole),
            pl.BlockSpec((1, own, wide * 3 // 4), step),
            pl.BlockSpec((heads, own, 2 * HEAD_SIZE), step),
        ],
        out_shape=[
            jax.ShapeDtypeStruct((own, used), BF),
            jax.ShapeDtypeStruct((cols, own, wide * 3 // 4), F32),
            jax.ShapeDtypeStruct((QUERY_HEADS, own, 2 * HEAD_SIZE), BF),
        ],
        scratch_shapes=[pltpu.VMEM((own, MODEL_WIDTH), BF)],
        compiler_params=pltpu.CompilerParams(vmem_limit_bytes=VMEM_LIMIT),
        cost_estimate=pl.CostEstimate(
            flops=2 * own * MODEL_WIDTH * cols * wide,
            bytes_accessed=cols * wide * MODEL_WIDTH * 2,
            transcendentals=own * cols * 8,
        ),
        name="qkv_forward",
    )(x, gain, inmaps, cosine, sine, head_gains, weights)


def qkv_unshape_kernel(
    ret_ref,
    pre_ref,
    m_ref,
    x_ref,
    gain_ref,
    cos_ref,
    sin_ref,
    hg_ref,
    w_ref,
    grads_ref,
    inner_ref,
    ga_ref,
    gb_ref,
    in_acc_ref,
):
    step = pl.program_id(0)
    row_blocks, used, piece = ga_ref.shape
    heads = ret_ref.shape[0]
    pieces = grads_ref.shape[2] // piece
    cosine = cos_ref[...]
    sine = sin_ref[...]

    @pl.when(step == 0)
    def _():
        in_acc_ref[...] = jnp.zeros_like(in_acc_ref)

    def unshaped(grad, at, gain):
        grad = grad.astype(F32)
        lines = pre_ref[0, :, at : at + HEAD_SIZE]
        turned = gain * (grad * cosine + pltpu.roll(grad * sine, HEAD_SIZE // 2, 1))
        scale = norm_scale(lines)
        inner_mean = jnp.mean(turned * lines, axis=1, keepdims=True)
        return (scale * turned - lines * (scale**3 * inner_mean)).astype(BF)

    parts = []
    for head in range(heads):
        parts.append(unshaped(ret_ref[head, :, :HEAD_SIZE], head * HEAD_SIZE, hg_ref[0:1, :]))
    for pair in range(heads // 2):
        at = (heads + pair) * HEAD_SIZE
        parts.append(unshaped(ret_ref[2 * pair, :, HEAD_SIZE:], at, hg_ref[1:2, :]))
    for pair in range(heads // 2):
        parts.append(ret_ref[2 * pair + 1, :, HEAD_SIZE:])
    grads = jnp.concatenate(parts, axis=1)
    grads_ref[0] = grads
    outmaps = jnp.concatenate(
        [w_ref[0, 0, p * used : (p + 1) * used, :] for p in range(pieces)], axis=1
    )
    in_acc_ref[...] += dot_nt(grads, outmaps)
    outer = ADAPTER_FACTOR * dot_tn(m_ref[...], grads)
    rank = ADAPTER_RANK
    edges = (0, heads * HEAD_SIZE, heads * HEAD_SIZE * 3 // 2, heads * HEAD_SIZE * 2)
    for i in range(3):
        gb_ref[0, :, edges[i] : edges[i + 1]] = outer[
            i * rank : (i + 1) * rank, edges[i] : edges[i + 1]
        ]

    @pl.when(step == pl.num_programs(0) - 1)
    def _():
        inner = (ADAPTER_FACTOR * in_acc_ref[...]).astype(BF)
        inner_ref[...] = inner
        resid = x_ref[...].astype(F32)
        hidden = (resid * norm_scale(resid) * gain_ref[...]).astype(BF)
        for r in range(row_blocks):
            ga_ref[r] = dot_tn(inner, hidden[:, r * piece : (r + 1) * piece])


def qkv_unshape(returned, pre, masked, x, gain, cosine, sine, head_gains, weights):
    own = x.shape[0]
    cols, row_blocks, tall, piece = weights.shape
    pieces = tall // piece
    wide = pieces * piece
    heads = QUERY_HEADS // cols
    used = 3 * ADAPTER_RANK
    map_rows = tall - wide
    at = wide // map_rows if wide % map_rows == 0 else None
    maps = weights[:, :1, wide:] if at is None else weights
    first = 0 if at is None else at
    whole = lambda c: (0, 0)
    step = lambda c: (c, 0, 0)
    return pl.pallas_call(
        qkv_unshape_kernel,
        grid=(cols,),
        in_specs=[
            pl.BlockSpec((heads, own, 2 * HEAD_SIZE), step),
            pl.BlockSpec((1, own, pre.shape[2]), step),
            pl.BlockSpec(masked.shape, whole),
            pl.BlockSpec(x.shape, whole),
            pl.BlockSpec(gain.shape, whole),
            pl.BlockSpec(cosine.shape, whole),
            pl.BlockSpec(sine.shape, whole),
            pl.BlockSpec(head_gains.shape, whole),
            pl.BlockSpec((1, 1, map_rows, piece), lambda c: (c, 0, first, 0)),
        ],
        out_specs=[
            pl.BlockSpec((1, own, wide), step),
            pl.BlockSpec((own, used), whole),
            pl.BlockSpec((row_blocks, used, piece), lambda c: (0, 0, 0)),
            pl.BlockSpec((1, ADAPTER_RANK, wide), step),
        ],
        out_shape=[
            jax.ShapeDtypeStruct((cols, own, wide), BF),
            jax.ShapeDtypeStruct((own, used), BF),
            jax.ShapeDtypeStruct((row_blocks, used, piece), F32),
            jax.ShapeDtypeStruct((cols, ADAPTER_RANK, wide), F32),
        ],
        scratch_shapes=[pltpu.VMEM((own, used), F32)],
        compiler_params=pltpu.CompilerParams(vmem_limit_bytes=VMEM_LIMIT),
        cost_estimate=pl.CostEstimate(
            flops=4 * own * 64 * cols * wide,
            bytes_accessed=cols * own * wide * 8,
            transcendentals=own * cols * 8,
        ),
        name="qkv_unshape",
    )(returned, pre, masked, x, gain, cosine, sine, head_gains, maps)


def qkv_backward_kernel(
    grads_ref, inner_ref, x_ref, gm_ref, gain_ref, a_ref, w_ref, grad_ref, acc_ref
):
    step = pl.program_id(0)
    row_blocks = w_ref.shape[1]
    piece = w_ref.shape[3]
    pieces = w_ref.shape[2] // piece

    @pl.when(step == 0)
    def _():
        acc_ref[...] = dot_nt(inner_ref[...], a_ref[...])

    for r in range(row_blocks):
        weights = jnp.concatenate(
            [w_ref[0, r, p * piece : (p + 1) * piece, :] for p in range(pieces)], axis=1
        )
        acc_ref[:, r * piece : (r + 1) * piece] += dot_nt(grads_ref[0], weights)

    @pl.when(step == pl.num_programs(0) - 1)
    def _():
        resid = x_ref[...].astype(F32)
        grad_ref[...] = (
            gm_ref[...] + norm_back(resid, norm_scale(resid), gain_ref[...], acc_ref[...])
        ).astype(BF)


def qkv_backward(grads, inner, x, grad_middle, gain, inmaps, weights):
    own = x.shape[0]
    cols, row_blocks, tall, piece = weights.shape
    wide = tall // piece * piece
    whole = lambda c: (0, 0)
    once = pl.Buffered(1)
    return pl.pallas_call(
        qkv_backward_kernel,
        grid=(cols,),
        in_specs=[
            pl.BlockSpec((1, own, wide), lambda c: (c, 0, 0)),
            pl.BlockSpec(inner.shape, whole),
            pl.BlockSpec(x.shape, whole, pipeline_mode=once),
            pl.BlockSpec(grad_middle.shape, whole, pipeline_mode=once),
            pl.BlockSpec(gain.shape, whole),
            pl.BlockSpec(inmaps.shape, whole),
            pl.BlockSpec((1, row_blocks, wide, piece), lambda c: (c, 0, 0, 0)),
        ],
        out_specs=pl.BlockSpec((own, MODEL_WIDTH), whole),
        out_shape=jax.ShapeDtypeStruct((own, MODEL_WIDTH), BF),
        scratch_shapes=[pltpu.VMEM((own, MODEL_WIDTH), F32)],
        compiler_params=pltpu.CompilerParams(vmem_limit_bytes=VMEM_LIMIT),
        cost_estimate=pl.CostEstimate(
            flops=2 * own * MODEL_WIDTH * cols * wide,
            bytes_accessed=cols * wide * MODEL_WIDTH * 2,
            transcendentals=own,
        ),
        name="qkv_backward",
    )(grads, inner, x, grad_middle, gain, inmaps, weights)


def whole_output_weights(flag_ref, own_ref, other_ref):
    own, other = (
        jnp.concatenate([ref[0, r] for r in range(ref.shape[1])], axis=1)
        for ref in (own_ref, other_ref)
    )
    first = flag_ref[0] == 0
    return jnp.concatenate(
        [jnp.where(first, own, other), jnp.where(first, other, own)], axis=0
    )


def output_forward_kernel(
    flag_ref,
    att_ref,
    x_ref,
    gain_ref,
    a_ref,
    b_ref,
    own_ref,
    other_ref,
    middle_ref,
    hidden_ref,
    m_ref,
    acc_ref,
    m_acc_ref,
):
    step = pl.program_id(0)
    heads = att_ref.shape[0]

    @pl.when(step == 0)
    def _():
        acc_ref[...] = x_ref[...].astype(F32)
        m_acc_ref[...] = jnp.zeros_like(m_acc_ref)

    attended = jnp.concatenate([att_ref[h] for h in range(heads)], axis=1)
    acc_ref[...] += dot(attended, whole_output_weights(flag_ref, own_ref, other_ref))
    m_acc_ref[...] += dot_nt(attended, a_ref[0])

    @pl.when(step == pl.num_programs(0) - 1)
    def _():
        masked = m_acc_ref[...].astype(BF)
        m_ref[...] = masked
        middle = acc_ref[...] + ADAPTER_FACTOR * dot_nt(masked, b_ref[...])
        middle_ref[...] = middle
        hidden_ref[...] = (middle * norm_scale(middle) * gain_ref[...]).astype(BF)


def output_forward(flag, attended, x, gain, inmaps, outmaps, weights):
    own = x.shape[0]
    cols = weights[0].shape[0]
    heads = QUERY_HEADS // cols
    o_rows = heads * HEAD_SIZE
    half = pl.BlockSpec((1, *weights[0].shape[1:]), lambda c: (c, 0, 0, 0))
    whole = lambda c: (0, 0)
    step = lambda c: (c, 0, 0)
    return pl.pallas_call(
        output_forward_kernel,
        grid=(cols,),
        in_specs=[
            pl.BlockSpec(memory_space=pltpu.SMEM),
            pl.BlockSpec((heads, own, HEAD_SIZE), step),
            pl.BlockSpec(x.shape, whole),
            pl.BlockSpec(gain.shape, whole),
            pl.BlockSpec((1, LANES, o_rows), step),
            pl.BlockSpec(outmaps.shape, whole),
            half,
            half,
        ],
        out_specs=[
            pl.BlockSpec((own, MODEL_WIDTH), whole),
            pl.BlockSpec((own, MODEL_WIDTH), whole),
            pl.BlockSpec((own, LANES), whole),
        ],
        out_shape=[
            jax.ShapeDtypeStruct((own, MODEL_WIDTH), F32),
            jax.ShapeDtypeStruct((own, MODEL_WIDTH), BF),
            jax.ShapeDtypeStruct((own, LANES), BF),
        ],
        scratch_shapes=[pltpu.VMEM((own, MODEL_WIDTH), F32), pltpu.VMEM((own, LANES), F32)],
        compiler_params=pltpu.CompilerParams(vmem_limit_bytes=VMEM_LIMIT),
        cost_estimate=pl.CostEstimate(
            flops=2 * own * MODEL_WIDTH * MODEL_WIDTH,
            bytes_accessed=2 * MODEL_WIDTH * MODEL_WIDTH,
            transcendentals=own,
        ),
        name="output_forward",
    )(flag, attended, x, gain, inmaps, outmaps, *weights)


def output_backward_kernel(
    flag_ref,
    gh_ref,
    got_ref,
    cot_ref,
    middle_ref,
    gain_ref,
    a_ref,
    b_ref,
    att_ref,
    m_ref,
    own_ref,
    other_ref,
    gm_ref,
    sent_ref,
    gb_ref,
    ga_ref,
    low_ref,
    inner_ref,
):
    heads = sent_ref.shape[0]
    row_blocks, rank, features = gb_ref.shape

    @pl.when(pl.program_id(0) == 0)
    def _():
        grad_hidden = gh_ref[...] + got_ref[...].astype(F32)
        middle = middle_ref[...]
        grad = cot_ref[...].astype(F32) + norm_back(
            middle, norm_scale(middle), gain_ref[...], grad_hidden
        )
        gm_ref[...] = grad
        low_ref[...] = grad.astype(BF)
        inner_ref[...] = (ADAPTER_FACTOR * dot(low_ref[...], b_ref[...])).astype(BF)
        outer = ADAPTER_FACTOR * dot_tn(m_ref[...], low_ref[...])
        for r in range(row_blocks):
            gb_ref[r] = outer[:rank, r * features : (r + 1) * features]

    attended = jnp.concatenate([att_ref[h] for h in range(heads)], axis=1)
    ga_ref[0] = dot_tn(inner_ref[...], attended)[:rank, :]
    weights = whole_output_weights(flag_ref, own_ref, other_ref)
    grad = (dot_nt(low_ref[...], weights) + dot(inner_ref[...], a_ref[0])).astype(BF)
    for head in range(heads):
        sent_ref[head] = grad[:, head * HEAD_SIZE : (head + 1) * HEAD_SIZE]


def output_backward(
    flag, grad_hidden, got, cotangent, middle, gain, inmaps, outmaps, attended, masked, weights
):
    own = middle.shape[0]
    cols, row_blocks = weights[0].shape[:2]
    features = MODEL_WIDTH // row_blocks
    heads = QUERY_HEADS // cols
    o_rows = heads * HEAD_SIZE
    half = pl.BlockSpec((1, *weights[0].shape[1:]), lambda c: (c, 0, 0, 0))
    whole = lambda c: (0, 0)
    step = lambda c: (c, 0, 0)
    once = pl.Buffered(1)
    return pl.pallas_call(
        output_backward_kernel,
        grid=(cols,),
        in_specs=[
            pl.BlockSpec(memory_space=pltpu.SMEM),
            pl.BlockSpec((own, MODEL_WIDTH), whole, pipeline_mode=once),
            pl.BlockSpec((own, MODEL_WIDTH), whole, pipeline_mode=once),
            pl.BlockSpec((own, MODEL_WIDTH), whole, pipeline_mode=once),
            pl.BlockSpec((own, MODEL_WIDTH), whole, pipeline_mode=once),
            pl.BlockSpec(gain.shape, whole),
            pl.BlockSpec((1, LANES, o_rows), step),
            pl.BlockSpec(outmaps.shape, whole),
            pl.BlockSpec((heads, own, HEAD_SIZE), step),
            pl.BlockSpec(masked.shape, whole),
            half,
            half,
        ],
        out_specs=[
            pl.BlockSpec((own, MODEL_WIDTH), whole),
            pl.BlockSpec((heads, own, HEAD_SIZE), step),
            pl.BlockSpec((row_blocks, ADAPTER_RANK, features), lambda c: (0, 0, 0)),
            pl.BlockSpec((1, ADAPTER_RANK, o_rows), step),
        ],
        out_shape=[
            jax.ShapeDtypeStruct((own, MODEL_WIDTH), F32),
            jax.ShapeDtypeStruct((QUERY_HEADS, own, HEAD_SIZE), BF),
            jax.ShapeDtypeStruct((row_blocks, ADAPTER_RANK, features), F32),
            jax.ShapeDtypeStruct((cols, ADAPTER_RANK, o_rows), F32),
        ],
        scratch_shapes=[pltpu.VMEM((own, MODEL_WIDTH), BF), pltpu.VMEM((own, LANES), BF)],
        compiler_params=pltpu.CompilerParams(vmem_limit_bytes=VMEM_LIMIT),
        cost_estimate=pl.CostEstimate(
            flops=2 * own * MODEL_WIDTH * MODEL_WIDTH,
            bytes_accessed=2 * MODEL_WIDTH * MODEL_WIDTH,
            transcendentals=own,
        ),
        name="output_backward",
    )(
        flag,
        grad_hidden,
        got,
        cotangent,
        middle,
        gain,
        inmaps,
        outmaps,
        attended,
        masked,
        *weights,
    )


def feed_forward_kernel(
    first, last, group, h_ref, c_ref, mg_ref, mu_ref, nd_ref, mask_ref, ag_ref, au_ref, od_ref, *refs
):
    weight_refs, map_refs, refs = refs[:group], refs[group : 2 * group], refs[2 * group :]
    if first:
        previous = None
    else:
        previous, refs = refs[:5], refs[5:]
    if last:
        (gh_ref, out_ref, rows_ref), refs = refs[:3], refs[3:]
    else:
        accs, refs = refs[:5], refs[5:]
    grads_refs, refs = refs[:group], refs[group:]
    gh_acc, out_acc, md_acc, ig_acc, iu_acc = scratch = refs[:5]
    sems = refs[5]
    step = pl.program_id(0)
    row_blocks = weight_refs[0].shape[1]
    deep = MODEL_WIDTH // row_blocks
    used = mg_ref.shape[1]

    @pl.when(step == 0)
    def _():
        if first:
            for ref in scratch:
                ref[...] = jnp.zeros_like(ref)
        else:
            for i in range(5):
                pltpu.make_async_copy(previous[i], scratch[i], sems.at[i]).start()

    def side(kind, row):
        return jnp.concatenate([ref[0, row, kind] for ref in weight_refs], axis=1)

    def tall_side(kind):
        return jnp.concatenate([side(kind, row) for row in range(row_blocks)], axis=0)

    def down_side(row):
        return jnp.concatenate(
            [
                jnp.concatenate(
                    [ref[0, row, 2, at : at + LANES, :] for at in range(0, deep, LANES)], axis=1
                )
                for ref in weight_refs
            ],
            axis=0,
        )

    def maps(kind):
        return jnp.concatenate(
            [ref[0, kind * used : (kind + 1) * used, :] for ref in map_refs], axis=1
        )

    gate_map, up_map, down_map = maps(0), maps(1), maps(2)
    units = group * LANES
    gate_up = dot(h_ref[...], jnp.concatenate([tall_side(0), tall_side(1)], axis=1))
    gate = gate_up[:, :units] + ADAPTER_FACTOR * dot(mg_ref[...], gate_map)
    upward = gate_up[:, units:] + ADAPTER_FACTOR * dot(mu_ref[...], up_map)
    down = jnp.concatenate([down_side(row) for row in range(row_blocks)], axis=1)
    grad_act = dot_nt(c_ref[...], down) + dot(nd_ref[...], down_map)
    sigma = 1.0 / (1.0 + jnp.exp(-gate))
    swish = gate * sigma
    act = (swish * upward).astype(BF)
    grad_gate = (grad_act * upward * (sigma * (1.0 + gate * (1.0 - sigma)))).astype(BF)
    grad_up = (grad_act * swish).astype(BF)
    both = jnp.concatenate([grad_gate, grad_up], axis=1)
    if not first:

        @pl.when(step == 0)
        def _():
            for i in range(5):
                pltpu.make_async_copy(previous[i], scratch[i], sems.at[i]).wait()

    for row in range(row_blocks):
        at = slice(row * deep, (row + 1) * deep)
        gh_acc[:, at] += dot_nt(both, jnp.concatenate([side(0, row), side(1, row)], axis=1))
        out_acc[:, at] += dot(act, down_side(row))
    md_acc[...] += dot_nt(act, down_map)
    ig_acc[...] += dot_nt(grad_gate, gate_map)
    iu_acc[...] += dot_nt(grad_up, up_map)
    partial = (
        ADAPTER_FACTOR * dot_tn(mg_ref[...], grad_gate),
        ADAPTER_FACTOR * dot_tn(mu_ref[...], grad_up),
        dot_tn(nd_ref[...], act),
    )
    for kind in range(3):
        for i, ref in enumerate(grads_refs):
            ref[0, kind * used : (kind + 1) * used, :] = partial[kind][
                :, i * LANES : (i + 1) * LANES
            ]

    @pl.when(step == pl.num_programs(0) - 1)
    def _():
        if last:
            mask = mask_ref[...]
            inner_g = (ADAPTER_FACTOR * ig_acc[...] * mask).astype(BF)
            inner_u = (ADAPTER_FACTOR * iu_acc[...] * mask).astype(BF)
            masked = (md_acc[...] * mask).astype(BF)
            gh_ref[...] = (
                gh_acc[...] + dot_nt(inner_g, ag_ref[...]) + dot_nt(inner_u, au_ref[...])
            ).astype(gh_ref.dtype)
            out_ref[...] = (out_acc[...] + ADAPTER_FACTOR * dot_nt(masked, od_ref[...])).astype(
                out_ref.dtype
            )
            for row in range(row_blocks):
                at = slice(row * deep, (row + 1) * deep)
                rows_ref[row, :used, :] = dot_tn(inner_g, h_ref[:, at])
                rows_ref[row, used : 2 * used, :] = dot_tn(inner_u, h_ref[:, at])
                rows_ref[row, 2 * used :, :] = ADAPTER_FACTOR * dot_tn(masked, c_ref[:, at])
        else:
            copies = [pltpu.make_async_copy(scratch[i], accs[i], sems.at[i]) for i in range(5)]
            for copy in copies:
                copy.start()
            for copy in copies:
                copy.wait()


def slab_group(count):
    return 4 if count % 4 == 0 else 2


def feed_forward_chunk(hidden, cotangent, masks, tables, weights, maps, previous, last, dtype):
    first = previous is None
    cols, row_blocks, _, deep, _ = weights.shape
    slabs = maps.shape[0] // cols
    count, used = masks[0].shape
    whole = lambda i: (0, 0)
    once = pl.Buffered(1)
    group = slab_group(cols * slabs)
    steps = cols * slabs // group
    acc_shapes = [(count, MODEL_WIDTH)] * 2 + [(count, used)] * 3

    def weight_spec(side):
        def at(i):
            return ((group * i + side) // slabs, 0, (group * i + side) % slabs, 0, 0)

        return pl.BlockSpec((1, row_blocks, 3, deep, LANES), at)

    def slab_spec(side):
        return pl.BlockSpec((1, 3 * used, LANES), lambda i: (group * i + side, 0, 0))

    step_spec = pl.BlockSpec((1, 3 * used, LANES), lambda i: (i, 0, 0))
    in_specs = (
        [pl.BlockSpec((count, MODEL_WIDTH), whole, pipeline_mode=once)] * 2
        + [pl.BlockSpec((count, used), whole)] * 4
        + [pl.BlockSpec((MODEL_WIDTH, used), whole, pipeline_mode=once)] * 3
        + [weight_spec(side) for side in range(group)]
        + [slab_spec(side) for side in range(group)]
    )
    operands = [hidden, cotangent, *masks, *tables] + [weights] * group + [maps] * group
    if not first:
        in_specs = in_specs + [pl.BlockSpec(memory_space=pl.ANY)] * 5
        operands = operands + list(previous)
    if last:
        out_specs = [pl.BlockSpec((count, MODEL_WIDTH), whole)] * 2 + [
            pl.BlockSpec((row_blocks, 3 * used, deep), lambda i: (0, 0, 0))
        ]
        out_shape = [jax.ShapeDtypeStruct(s, dtype) for s in acc_shapes[:2]] + [
            jax.ShapeDtypeStruct((row_blocks, 3 * used, deep), F32)
        ]
    else:
        out_specs = [pl.BlockSpec(memory_space=pl.ANY)] * 5
        out_shape = [jax.ShapeDtypeStruct(s, F32) for s in acc_shapes]
    outs = pl.pallas_call(
        functools.partial(feed_forward_kernel, first, last, group),
        grid=(steps,),
        in_specs=in_specs,
        out_specs=out_specs + [step_spec] * group,
        out_shape=out_shape + [jax.ShapeDtypeStruct((steps, 3 * used, LANES), F32)] * group,
        scratch_shapes=[pltpu.VMEM(s, F32) for s in acc_shapes]
        + [pltpu.SemaphoreType.DMA((5,))],
        compiler_params=pltpu.CompilerParams(vmem_limit_bytes=VMEM_LIMIT),
        cost_estimate=pl.CostEstimate(
            flops=12 * count * MODEL_WIDTH * cols * slabs * LANES,
            bytes_accessed=cols * slabs * row_blocks * 3 * deep * LANES * 2,
            transcendentals=count * cols * slabs * LANES,
        ),
        name="feed_forward",
    )(*operands)
    return outs[:-group], outs[-group:]


def placed(ids_ref, first, second, count):
    zero = jnp.zeros_like(first)
    blocks = []
    for slot in range(count):
        blocks.append(
            jnp.where(ids_ref[0] == slot, first, zero)
            + jnp.where(ids_ref[1] == slot, second, zero)
        )
    return jnp.concatenate(blocks, axis=0)


def finish_middle_kernel(
    ids_ref, row_ref, col_ref, a_o, b_o, a_gate, b_gate, a_up, b_up, a_down, b_down
):
    rank = ADAPTER_RANK
    count = b_o.shape[0] // rank
    half = b_gate.shape[1] // 2

    def part(ref, tree, at):
        return ref[tree, at * rank : (at + 1) * rank, :].astype(F32)

    def both_planes(at):
        first = part(row_ref, 0, at) + part(row_ref, 1, at + 1)
        second = part(row_ref, 0, at + 1) + part(row_ref, 1, at)
        return placed(ids_ref, first, second, count)

    a_gate[...] = jnp.transpose(both_planes(0))
    a_up[...] = jnp.transpose(both_planes(2))
    b_down[...] = both_planes(4)
    b_o[...] = placed(ids_ref, part(row_ref, 0, 6), part(row_ref, 1, 6), count)
    o_rows = a_o.shape[0]
    a_o[...] = jnp.transpose(
        placed(ids_ref, part(col_ref, 0, 6)[:, :o_rows], part(col_ref, 1, 6)[:, :o_rows], count)
    )
    low_plane = ids_ref[2] == 0

    def halves(at):
        mine = placed(ids_ref, part(col_ref, 0, at), part(col_ref, 0, at + 1), count)[:, :half]
        theirs = placed(ids_ref, part(col_ref, 1, at + 1), part(col_ref, 1, at), count)[:, :half]
        return jnp.where(low_plane, mine, theirs), jnp.where(low_plane, theirs, mine)

    for at, out in ((0, b_gate), (2, b_up)):
        low, high = halves(at)
        out[:, :half] = low
        out[:, half:] = high
    low, high = halves(4)
    a_down[:half, :] = jnp.transpose(low)
    a_down[half:, :] = jnp.transpose(high)


def finish_end_kernel(ids_ref, row_ref, col_ref, a_q, b_q, a_k, b_k, a_v, b_v):
    rank = ADAPTER_RANK
    count = b_q.shape[0] // rank
    for at, out in enumerate((a_q, a_k, a_v)):
        rows = slice(at * rank, (at + 1) * rank)
        out[...] = jnp.transpose(
            placed(ids_ref, row_ref[0, rows, :].astype(F32), row_ref[1, rows, :].astype(F32), count)
        )
    start = 0
    for out in (b_q, b_k, b_v):
        lanes = slice(start, start + out.shape[1])
        out[...] = placed(
            ids_ref, col_ref[0, :, lanes].astype(F32), col_ref[1, :, lanes].astype(F32), count
        )
        start = start + out.shape[1]


def finish(kernel, ids, row_table, col_table, shapes, name):
    size = sum(shape[0] * shape[1] for shape in shapes)
    return pl.pallas_call(
        kernel,
        in_specs=[
            pl.BlockSpec(memory_space=pltpu.SMEM),
            pl.BlockSpec(memory_space=pltpu.VMEM),
            pl.BlockSpec(memory_space=pltpu.VMEM),
        ],
        out_specs=[pl.BlockSpec(memory_space=pltpu.VMEM)] * len(shapes),
        out_shape=[jax.ShapeDtypeStruct(shape, F32) for shape in shapes],
        cost_estimate=pl.CostEstimate(flops=size, bytes_accessed=8 * size, transcendentals=0),
        name=name,
    )(ids, row_table, col_table)


def lane_pad(values):
    return jnp.pad(values, ((0, 0),) * (values.ndim - 1) + ((0, LANES - values.shape[-1]),))


def row_pad(values):
    return jnp.pad(
        values, ((0, 0),) * (values.ndim - 2) + ((0, LANES - values.shape[-2]), (0, 0))
    )


def thirds(values):
    parts = []
    for _ in range(3):
        part = lax.reduce_precision(values, 8, 7)
        parts.append(part.astype(BF)[:, None])
        values = values - part
    return parts


def on_device(
    tokens,
    cotangent,
    attention_norm_gain,
    feedfwd_norm_gain,
    query_norm_gain,
    key_norm_gain,
    query_matrix,
    key_matrix,
    value_matrix,
    output_matrix,
    gate_matrix,
    up_matrix,
    down_matrix,
    query_adapter_inmaps,
    query_adapter_outmaps,
    key_adapter_inmaps,
    key_adapter_outmaps,
    value_adapter_inmaps,
    value_adapter_outmaps,
    output_adapter_inmaps,
    output_adapter_outmaps,
    gate_adapter_inmaps,
    gate_adapter_outmaps,
    up_adapter_inmaps,
    up_adapter_outmaps,
    down_adapter_inmaps,
    down_adapter_outmaps,
    segment,
    depth,
    parent,
    adapter,
):
    rows = lax.axis_size("row")
    cols = lax.axis_size("col")
    devices = rows * cols
    repeat = devices // QUERY_HEADS
    plane = lax.axis_index("dp")
    row = lax.axis_index("row")
    col = lax.axis_index("col")
    length = segment.shape[0]
    own = tokens.shape[0] // rows
    columns = query_adapter_inmaps.shape[1]
    rank = ADAPTER_RANK
    swap = [(0, 1), (1, 0)]
    pairs = [(r, r ^ repeat) for r in range(rows)]
    q_local = query_matrix.shape[1]
    kv_local = key_matrix.shape[1]
    wide = q_local + 2 * kv_local
    features = gate_matrix.shape[0]

    own_adapter = adapter[0]
    other_adapter = lax.ppermute(adapter, "dp", swap)[0]
    both = (own_adapter, other_adapter)

    def inmap(table, at):
        return lax.dynamic_slice_in_dim(table, at * rank, rank, 1)

    def outmap(table, at):
        return lax.dynamic_slice_in_dim(table, at * rank, rank, 0)

    qkv_local = jnp.concatenate([query_matrix, key_matrix, value_matrix], axis=1)

    def block_of(table, before, after):
        return jnp.pad(outmap(table, own_adapter), ((0, 0), (before, after)))

    qkv_maps = jnp.concatenate(
        [
            block_of(query_adapter_outmaps, 0, 2 * kv_local),
            block_of(key_adapter_outmaps, q_local, kv_local),
            block_of(value_adapter_outmaps, q_local + kv_local, 0),
        ],
        axis=0,
    )
    attention_pack = jnp.concatenate(
        [
            table[:, at : at + features]
            for table in (qkv_local, qkv_maps)
            for at in range(0, wide, features)
        ]
        + [
            lax.dynamic_slice_in_dim(
                output_matrix, plane * (output_matrix.shape[0] // 2), output_matrix.shape[0] // 2, 0
            )
        ],
        axis=0,
    )
    attention_weights = lax.all_gather(attention_pack, PLANE, axis=0, tiled=True).reshape(
        cols, rows, -1, features
    )
    o_rows = output_matrix.shape[0]
    own_output_weights = attention_weights[:, :, -(o_rows // 2) :]
    plane_flag = plane.astype(jnp.int32).reshape(1)
    ffn_half = gate_matrix.shape[1] // 2
    half_start = plane * ffn_half
    chunks = 2 if ffn_half % 256 == 0 else 3
    width = ffn_half // chunks
    slabs = width // LANES

    def plates(table):
        return [table[:, at : at + LANES] for at in range(0, table.shape[1], LANES)]

    def half_of(table):
        return lax.dynamic_slice_in_dim(table, half_start, ffn_half, 1)

    map_width = max(ffn_half, o_rows)

    def to_width(table):
        return jnp.pad(table, ((0, 0), (0, map_width - table.shape[1])))

    col_pack = jnp.concatenate(
        [
            *[to_width(half_of(outmap(gate_adapter_outmaps, a))) for a in both],
            *[to_width(half_of(outmap(up_adapter_outmaps, a))) for a in both],
            *[to_width(half_of(inmap(down_adapter_inmaps, a).T)) for a in both],
            to_width(inmap(output_adapter_inmaps, own_adapter).T),
            jnp.zeros((rank, map_width), BF),
        ],
        axis=0,
    )
    map_rows = col_pack.shape[0] // rows
    map_plates = plates(lax.dynamic_slice_in_dim(col_pack, row * map_rows, map_rows, 0))
    ffn_weights = []
    for chunk in range(chunks):
        pack = []
        for slab in range(slabs):
            start = half_start + (chunk * slabs + slab) * LANES
            pack.append(lax.dynamic_slice_in_dim(gate_matrix, start, LANES, 1))
            pack.append(lax.dynamic_slice_in_dim(up_matrix, start, LANES, 1))
            pack.extend(plates(lax.dynamic_slice_in_dim(down_matrix, start, LANES, 0)))
        if chunk == 0:
            spare = features - map_rows * len(map_plates)
            pack = pack + map_plates + [jnp.zeros((spare, LANES), BF)]
        pack = jnp.concatenate(pack, axis=0)
        ffn_weights.append(
            lax.all_gather(pack, PLANE, axis=0, tiled=True).reshape(
                cols, rows, -1, features, LANES
            )
        )
    col_maps = ffn_weights[0][:, :, -1, : map_rows * len(map_plates)].reshape(
        cols, rows, len(map_plates), map_rows, LANES
    )
    col_maps = jnp.transpose(col_maps, (0, 2, 1, 3, 4)).reshape(
        cols, len(map_plates), rows * map_rows, LANES
    )
    in_o = jnp.transpose(col_maps[:, : o_rows // LANES, 6 * rank : 7 * rank], (0, 2, 1, 3))
    in_o = row_pad(in_o.reshape(cols, rank, o_rows))

    row_pack = jnp.concatenate(
        [
            inmap(query_adapter_inmaps, own_adapter),
            inmap(key_adapter_inmaps, own_adapter),
            inmap(value_adapter_inmaps, own_adapter),
            *[inmap(gate_adapter_inmaps, a) for a in both],
            *[inmap(up_adapter_inmaps, a) for a in both],
            *[outmap(down_adapter_outmaps, a).T for a in both],
            outmap(output_adapter_outmaps, own_adapter).T,
            *thirds(attention_norm_gain),
            *thirds(feedfwd_norm_gain),
        ],
        axis=1,
    )

    row_maps = lax.all_gather(row_pack, "row", axis=0, tiled=True)
    in_qkv = row_maps[:, : 3 * rank]
    in_gate = row_maps[:, 3 * rank : 5 * rank]
    in_up = row_maps[:, 5 * rank : 7 * rank]
    out_down = row_maps[:, 7 * rank : 9 * rank]
    out_o = lane_pad(row_maps[:, 9 * rank : 10 * rank])
    gain_parts = row_maps[:, 10 * rank :].astype(F32)
    gain_one = (gain_parts[:, 0] + (gain_parts[:, 1] + gain_parts[:, 2])).reshape(1, -1)
    gain_two = (gain_parts[:, 3] + (gain_parts[:, 4] + gain_parts[:, 5])).reshape(1, -1)

    own_tokens = lax.all_to_all(tokens, "row", 0, 1, tiled=True)
    own_cotangent = lax.all_to_all(cotangent, "row", 0, 1, tiled=True)
    other_cotangent = lax.ppermute(own_cotangent, "dp", swap)
    own_tokens, other_cotangent, own_output_weights = lax.optimization_barrier(
        (own_tokens, other_cotangent, own_output_weights)
    )
    other_output_weights = lax.ppermute(own_output_weights, "dp", swap)
    head_gains = jnp.stack([query_norm_gain, key_norm_gain], axis=0)
    token_start = (col * rows + row) * own
    positions = lax.dynamic_slice_in_dim(depth, token_start, own, 0).astype(F32)
    half = HEAD_SIZE // 2
    freqs = THETA ** (-2.0 * jnp.arange(half).astype(F32) / HEAD_SIZE)
    angle = positions[:, None] * freqs[None, :]
    cosine = jnp.tile(jnp.cos(angle), (1, 2))
    sine = jnp.concatenate([-jnp.sin(angle), jnp.sin(angle)], axis=1)

    masked_qkv, pre, sent = qkv_forward(
        own_tokens, gain_one, in_qkv, cosine, sine, head_gains, attention_weights
    )

    def to_heads(sent):
        if repeat > 1:
            sent = jnp.repeat(sent, repeat, axis=0)
        return lax.all_to_all(sent, PLANE, 0, 0, tiled=True).reshape(length, sent.shape[2])

    def to_tokens(lines):
        got = lax.all_to_all(
            lines.reshape(devices, own, lines.shape[1]), PLANE, 0, 0, tiled=True
        )
        return got[::repeat] if repeat > 1 else got

    got, other_output_weights = lax.optimization_barrier((to_heads(sent), other_output_weights))
    output_weights = (own_output_weights, other_output_weights)
    theirs = lax.ppermute(got[:, HEAD_SIZE:], "row", pairs)
    flag = (1 - (row // repeat) % 2).astype(jnp.int32).reshape(1)

    block_node = segment.reshape(-1, SEG_LEN)[:, 0]
    nodes = jnp.arange(parent.shape[1])
    node_parent = jnp.sum(jnp.where(block_node[:, None] == nodes, parent.reshape(1, -1), 0), axis=1)
    block_index = jnp.arange(block_node.shape[0])
    parent_block = jnp.max(
        jnp.where(node_parent[:, None] == block_node[None, :], block_index[None, :], 0), axis=1
    )
    parent_block = jnp.where(node_parent > 0, parent_block, -1).astype(jnp.int32)
    head_attended, head_low, totals = attention_forward(parent_block, flag, got, theirs)
    attended = to_tokens(head_low)

    middle, hidden_ffn, masked_o = output_forward(
        plane_flag, attended, own_tokens, gain_two, in_o, out_o, output_weights
    )

    other_ffn = lax.ppermute(hidden_ffn, "dp", swap)
    tables = (in_gate, in_up, out_down)
    column_tree = jnp.arange(2 * rank)[None, :] // rank

    def masks_of(hidden, cot, tree):
        mask = jnp.broadcast_to((column_tree == tree).astype(F32), (own, 2 * rank))
        return (
            (dot(hidden, in_gate) * mask).astype(BF),
            (dot(hidden, in_up) * mask).astype(BF),
            (ADAPTER_FACTOR * dot(cot, out_down) * mask).astype(BF),
            mask,
        )

    parts = []

    def run(chunk, side, masks, accs):
        hidden, cot = side
        maps = col_maps[:, chunk * slabs : (chunk + 1) * slabs].reshape(cols * slabs, -1, LANES)
        last = chunk == chunks - 1
        return feed_forward_chunk(
            hidden,
            cot,
            masks,
            tables,
            ffn_weights[chunk],
            maps,
            accs,
            last,
            F32 if side is own_side else BF,
        )

    own_side = (hidden_ffn, own_cotangent)
    own_masks = masks_of(*own_side, 0)
    here, own_part = run(0, own_side, own_masks, None)
    other_ffn, here = lax.optimization_barrier((other_ffn, here))
    other_side = (other_ffn, other_cotangent)
    other_masks = masks_of(*other_side, 1)
    there, other_part = run(0, other_side, other_masks, None)
    parts = [(own_part, other_part)]
    for chunk in range(1, chunks):
        there, other_part = run(chunk, other_side, other_masks, there)
        here, own_part = run(chunk, own_side, own_masks, here)
        parts.append((own_part, other_part))

    def slab_order(part):
        part = [first + second for first, second in zip(*part)]
        part = jnp.stack(part, axis=1).reshape(cols, slabs, 6 * rank, LANES)
        return jnp.transpose(part, (0, 2, 1, 3)).reshape(cols, 6 * rank, width)

    parts = [slab_order(part) for part in parts]
    gh_other = lax.ppermute(there[0], "dp", swap)

    grad_middle, sent, grad_o_rows, grad_o_cols = output_backward(
        plane_flag,
        here[0],
        gh_other,
        own_cotangent,
        middle,
        gain_two,
        in_o,
        out_o,
        attended,
        masked_o,
        output_weights,
    )
    out_sent, sent = lax.optimization_barrier((there[1], sent))
    out_other = lax.ppermute(out_sent, "dp", swap)
    head_grad = to_heads(sent)

    def pieces_of(row_table, col_table):
        row_table = jnp.swapaxes(row_table.astype(BF).reshape(rows, cols, -1, LANES), 0, 1)
        col_table = col_table.astype(BF).reshape(cols, rows, -1, LANES)
        return jnp.concatenate([row_table, col_table], axis=2).reshape(devices, -1, LANES)

    def gathered(values, axis, at):
        size = lax.axis_size(axis)
        whole = jnp.zeros((2, size, *values.shape[1:]), values.dtype)
        for k in range(size):
            block = values
            if k:
                block = lax.ppermute(values, axis, [(i, i ^ k) for i in range(size)])
            whole = lax.dynamic_update_index_in_dim(whole, block, at ^ k, 1)
        return whole

    def summed(pieces):
        mine = jnp.sum(pieces.astype(F32), axis=0).astype(BF)
        return jnp.stack([mine, lax.ppermute(mine, "dp", swap)], axis=0)

    def gathered_tables(pieces, row_highs, col_highs):
        row_parts = [high * features // (cols * LANES) for high in row_highs]
        row_pieces = [piece[:, :part] for piece, part in zip(pieces, row_parts)]
        col_pieces = [piece[:, part:] for piece, part in zip(pieces, row_parts)]
        row_whole = gathered(jnp.concatenate(row_pieces, axis=1), "col", col)
        col_whole = gathered(jnp.concatenate(col_pieces, axis=1), "row", row)
        tables = []
        row_at = col_at = 0
        for i, (row_high, col_high) in enumerate(zip(row_highs, col_highs)):
            row_size, col_size = row_pieces[i].shape[1], col_pieces[i].shape[1]
            tables.append(
                (
                    row_whole[:, :, row_at : row_at + row_size].reshape(2, row_high, features),
                    col_whole[:, :, col_at : col_at + col_size].reshape(2, col_high, -1),
                )
            )
            row_at, col_at = row_at + row_size, col_at + col_size
        return tables

    def to_own_features(lines):
        blocks = lines.reshape(own, rows, features)
        whole = jnp.zeros((rows, own, features), lines.dtype)
        for k in range(rows):
            block = lax.dynamic_index_in_dim(blocks, row ^ k, 1, False)
            if k:
                block = lax.ppermute(block, "row", [(r, r ^ k) for r in range(rows)])
            whole = lax.dynamic_update_index_in_dim(whole, block, row ^ k, 0)
        return whole.reshape(rows * own, features)

    def to_map_width(table):
        return jnp.pad(table, ((0, 0), (0, 0), (0, map_width - table.shape[2])))

    mid_pieces = pieces_of(
        jnp.concatenate([here[2] + there[2], grad_o_rows], axis=1),
        jnp.concatenate(
            [to_map_width(jnp.concatenate(parts, axis=2)), to_map_width(grad_o_cols)], axis=1
        ),
    )
    head_grad, mid_pieces = lax.optimization_barrier((head_grad, mid_pieces))
    mid_pieces = lax.all_to_all(mid_pieces, PLANE, 0, 0, tiled=True)

    lines, kept, given = attention_backward(
        parent_block, flag, got, head_grad, head_attended, totals, theirs
    )
    lines, kept, given, mid_pieces, out_other = lax.optimization_barrier(
        (lines, kept, given, mid_pieces, out_other)
    )
    returned = to_tokens(merge(lines, kept, lax.ppermute(given, "row", pairs)))
    output = (middle + here[1] + out_other.astype(F32)).astype(BF)
    output = to_own_features(output)
    returned, output, mid_pieces = lax.optimization_barrier(
        (returned, output, summed(mid_pieces))
    )

    grads_qkv, inner_qkv, row_end, col_end = qkv_unshape(
        returned,
        pre,
        masked_qkv,
        own_tokens,
        gain_one,
        cosine,
        sine,
        head_gains,
        attention_weights,
    )
    end_pieces = lax.all_to_all(pieces_of(row_end, col_end), PLANE, 0, 0, tiled=True)
    grad_low = qkv_backward(
        grads_qkv, inner_qkv, own_tokens, grad_middle, gain_one, in_qkv, attention_weights
    )
    grad_low, end_pieces = lax.optimization_barrier((grad_low, end_pieces))
    input_gradient = lax.all_to_all(grad_low, "row", 1, 0, tiled=True).astype(F32)
    mid_tables, end_tables = gathered_tables(
        (mid_pieces, summed(end_pieces)), (7 * rank, 3 * rank), (7 * rank, rank)
    )
    ids = jnp.stack([own_adapter, other_adapter, plane]).astype(jnp.int32)
    down_rows = down_matrix.shape[0]
    wide_a, wide_o, wide_d = (features, columns), (o_rows, columns), (down_rows, columns)
    finished = finish(
        finish_middle_kernel,
        ids,
        *mid_tables,
        [
            wide_o,
            (columns, features),
            wide_a,
            (columns, down_rows),
            wide_a,
            (columns, down_rows),
            wide_d,
            (columns, features),
        ],
        "finish_middle",
    )
    finished_qkv = finish(
        finish_end_kernel,
        ids,
        *end_tables,
        [wide_a, (columns, q_local), wide_a, (columns, kv_local), wide_a, (columns, kv_local)],
        "finish_end",
    )

    return (output, input_gradient, *finished_qkv, *finished)


def solution(mesh):
    return jax.shard_map(
        on_device,
        mesh=mesh,
        in_specs=(
            P(("dp", "col"), "row"),
            P(("dp", "col"), "row"),
            P("row"),
            P("row"),
            P(),
            P(),
            P("row", "col"),
            P("row", "col"),
            P("row", "col"),
            P("col", "row"),
            P("row", "col"),
            P("row", "col"),
            P("col", "row"),
            P("row", None),
            P(None, "col"),
            P("row", None),
            P(None, "col"),
            P("row", None),
            P(None, "col"),
            P("col", None),
            P(None, "row"),
            P("row", None),
            P(None, "col"),
            P("row", None),
            P(None, "col"),
            P("col", None),
            P(None, "row"),
            P("dp"),
            P("dp"),
            P("dp", None),
            P("dp"),
        ),
        out_specs=(
            P(("dp", "col"), "row"),
            P(("dp", "col"), "row"),
            P("row", None),
            P(None, "col"),
            P("row", None),
            P(None, "col"),
            P("row", None),
            P(None, "col"),
            P("col", None),
            P(None, "row"),
            P("row", None),
            P(None, "col"),
            P("row", None),
            P(None, "col"),
            P("col", None),
            P(None, "row"),
        ),
        check_vma=False,
    )
```

```python
import functools
import math

import jax
import jax.numpy as jnp
from jax import lax
from jax.experimental import pallas as pl
from jax.experimental.pallas import tpu as pltpu
from jax.sharding import PartitionSpec as P

MODEL_WIDTH = 2048
QUERY_HEADS = 16
KEY_VALUE_HEADS = 8
HEAD_SIZE = 128
ADAPTER_RANK = 16
TREE_LEN = 5120
TRUNK = 2048
SEG_LEN = 256
QUERY_BLOCK = 512
KEY_BLOCK = 1024

EPSILON = 1e-06
THETA = 1000000.0
ADAPTER_FACTOR = 2.0
BF = jnp.bfloat16
F32 = jnp.float32
SCALE = HEAD_SIZE ** (-0.5)
SCALE_LOG2 = SCALE * math.log2(math.e)
PLANE = ("col", "row")
LANES = 128
VMEM_LIMIT = 63 * 1024 * 1024


def dot(left, right):
    return jnp.dot(left, right, preferred_element_type=F32)


def dot_nt(left, right):
    return lax.dot_general(left, right, (((1,), (1,)), ((), ())), preferred_element_type=F32)


def dot_tn(left, right):
    return lax.dot_general(left, right, (((0,), (0,)), ((), ())), preferred_element_type=F32)


def walk_keys(index, parent_ref, step):
    trunk_blocks = TRUNK // QUERY_BLOCK

    @pl.when(index < trunk_blocks)
    def _():
        @pl.loop(0, index)
        def _(block):
            step(pl.multiple_of(block * QUERY_BLOCK, QUERY_BLOCK), QUERY_BLOCK)

        step(pl.multiple_of(index * QUERY_BLOCK, QUERY_BLOCK), QUERY_BLOCK, causal=True)

    @pl.when(index >= trunk_blocks)
    def _():
        for part in range(TRUNK // KEY_BLOCK):
            step(part * KEY_BLOCK, KEY_BLOCK)
        for side in range(QUERY_BLOCK // SEG_LEN):
            block = index * (QUERY_BLOCK // SEG_LEN) + side
            first = side * SEG_LEN
            start = pl.multiple_of(block * SEG_LEN, SEG_LEN)
            step(start, SEG_LEN, first, SEG_LEN, True)
            above = parent_ref[block]

            @pl.when(above >= 0)
            def _():
                step(pl.multiple_of(above * SEG_LEN, SEG_LEN), SEG_LEN, first, SEG_LEN)


def attention_forward_kernel(
    parent_ref, flag_ref, q_ref, mine_ref, theirs_ref, o_ref, low_ref, l_ref, k_ref, v_ref, acc_ref
):
    index = pl.program_id(0)

    @pl.when(index == 0)
    def _():
        lane = lax.broadcasted_iota(jnp.int32, (v_ref.shape[0], HEAD_SIZE), 1)
        v_ref[:, HEAD_SIZE:] = jnp.where(lane == 0, 1.0, 0.0).astype(BF)

        @pl.when(flag_ref[0] == 1)
        def _():
            k_ref[...] = mine_ref[...]
            v_ref[:, :HEAD_SIZE] = theirs_ref[...]

        @pl.when(flag_ref[0] != 1)
        def _():
            k_ref[...] = theirs_ref[...]
            v_ref[:, :HEAD_SIZE] = mine_ref[...]

    acc_ref[...] = jnp.zeros_like(acc_ref)

    def step(start, size, first=0, count=QUERY_BLOCK, causal=False):
        rows = pl.ds(start, size)
        at = pl.ds(first, count)
        scores = dot_nt(q_ref[at, :], k_ref[rows, :])
        probs = jnp.exp2(scores * SCALE_LOG2)
        if causal:
            ahead = lax.broadcasted_iota(jnp.int32, probs.shape, 0)
            behind = lax.broadcasted_iota(jnp.int32, probs.shape, 1)
            probs = jnp.where(behind <= ahead, probs, 0.0)
        acc_ref[at, :] += dot(probs.astype(BF), v_ref[rows, :])

    walk_keys(index, parent_ref, step)
    total = acc_ref[:, HEAD_SIZE : HEAD_SIZE + 1]
    attended = acc_ref[:, :HEAD_SIZE] / total
    o_ref[...] = attended
    low_ref[...] = attended.astype(BF)
    spread = jnp.broadcast_to(total, (QUERY_BLOCK, LANES))
    l_ref[0] = jnp.transpose(spread)[:8, :]


def attention_forward(parent_block, flag, got, theirs):
    length = theirs.shape[0]
    blocks = length // QUERY_BLOCK
    whole = lambda i, p, f: (0, 0)
    part = lambda i, p, f: (i, 0)
    return pl.pallas_call(
        attention_forward_kernel,
        grid_spec=pltpu.PrefetchScalarGridSpec(
            num_scalar_prefetch=2,
            grid=(blocks,),
            in_specs=[
                pl.BlockSpec((QUERY_BLOCK, HEAD_SIZE), part),
                pl.BlockSpec((length, HEAD_SIZE), lambda i, p, f: (0, 1)),
                pl.BlockSpec((length, HEAD_SIZE), whole),
            ],
            out_specs=[
                pl.BlockSpec((QUERY_BLOCK, HEAD_SIZE), part),
                pl.BlockSpec((QUERY_BLOCK, HEAD_SIZE), part),
                pl.BlockSpec((1, 8, QUERY_BLOCK), lambda i, p, f: (i, 0, 0)),
            ],
            scratch_shapes=[
                pltpu.VMEM((length, HEAD_SIZE), BF),
                pltpu.VMEM((length, 2 * HEAD_SIZE), BF),
                pltpu.VMEM((QUERY_BLOCK, 2 * HEAD_SIZE), F32),
            ],
        ),
        out_shape=[
            jax.ShapeDtypeStruct((length, HEAD_SIZE), F32),
            jax.ShapeDtypeStruct((length, HEAD_SIZE), BF),
            jax.ShapeDtypeStruct((blocks, 8, QUERY_BLOCK), F32),
        ],
        compiler_params=pltpu.CompilerParams(vmem_limit_bytes=VMEM_LIMIT),
        cost_estimate=pl.CostEstimate(
            flops=160 * SEG_LEN * SEG_LEN * HEAD_SIZE * 4,
            bytes_accessed=length * HEAD_SIZE * 12,
            transcendentals=160 * SEG_LEN * SEG_LEN,
        ),
        name="attention_forward",
    )(parent_block, flag, got, got, theirs)


def attention_backward_kernel(
    parent_ref,
    flag_ref,
    q_ref,
    g_ref,
    o_ref,
    l_ref,
    mine_ref,
    theirs_ref,
    dq_ref,
    kept_ref,
    given_ref,
    k_ref,
    v_ref,
    kt_ref,
    dk_ref,
    dv_ref,
    acc_ref,
    delta_ref,
    inverse_ref,
):
    index = pl.program_id(0)

    @pl.when(index == 0)
    def _():
        dk_ref[...] = jnp.zeros_like(dk_ref)
        dv_ref[...] = jnp.zeros_like(dv_ref)

        @pl.when(flag_ref[0] == 1)
        def _():
            k_ref[...] = mine_ref[...]
            v_ref[...] = theirs_ref[...]

        @pl.when(flag_ref[0] != 1)
        def _():
            k_ref[...] = theirs_ref[...]
            v_ref[...] = mine_ref[...]

        @pl.loop(0, k_ref.shape[0] // SEG_LEN)
        def _(block):
            rows = pl.ds(pl.multiple_of(block * SEG_LEN, SEG_LEN), SEG_LEN)
            kt_ref[:, rows] = jnp.transpose(k_ref[rows, :])

    delta = jnp.sum(g_ref[...].astype(F32) * o_ref[...], axis=1, keepdims=True)
    delta_ref[...] = jnp.transpose(jnp.broadcast_to(delta, (QUERY_BLOCK, LANES)))[:8, :]
    inverse_ref[...] = 1.0 / l_ref[0]
    acc_ref[...] = jnp.zeros_like(acc_ref)

    def step(start, size, first=0, count=QUERY_BLOCK, causal=False):
        rows = pl.ds(start, size)
        at = pl.ds(first, count)
        query = q_ref[at, :]
        grad = g_ref[at, :]
        probs = jnp.exp2(dot_nt(k_ref[rows, :], query) * SCALE_LOG2) * inverse_ref[:1, at]
        if causal:
            behind = lax.broadcasted_iota(jnp.int32, probs.shape, 0)
            ahead = lax.broadcasted_iota(jnp.int32, probs.shape, 1)
            probs = jnp.where(behind <= ahead, probs, 0.0)
        dprobs = dot_nt(v_ref[rows, :], grad)
        dscores = (probs * (dprobs - delta_ref[:1, at])).astype(BF)
        dv_ref[rows, :] += dot(probs.astype(BF), grad)
        dk_ref[rows, :] += dot(dscores, query)
        acc_ref[:, at] += dot(kt_ref[:, rows], dscores)

    walk_keys(index, parent_ref, step)
    dq_ref[...] = (jnp.transpose(acc_ref[...]) * SCALE).astype(BF)

    @pl.when(index == pl.num_programs(0) - 1)
    def _():
        @pl.when(flag_ref[0] == 1)
        def _():
            kept_ref[...] = dk_ref[...] * SCALE
            given_ref[...] = dv_ref[...].astype(BF)

        @pl.when(flag_ref[0] != 1)
        def _():
            kept_ref[...] = dv_ref[...]
            given_ref[...] = (dk_ref[...] * SCALE).astype(BF)


def attention_backward(parent_block, flag, got, grad, attended, totals, theirs):
    length = theirs.shape[0]
    blocks = length // QUERY_BLOCK
    whole = lambda i, p, f: (0, 0)
    part = lambda i, p, f: (i, 0)
    return pl.pallas_call(
        attention_backward_kernel,
        grid_spec=pltpu.PrefetchScalarGridSpec(
            num_scalar_prefetch=2,
            grid=(blocks,),
            in_specs=[
                pl.BlockSpec((QUERY_BLOCK, HEAD_SIZE), part),
                pl.BlockSpec((QUERY_BLOCK, HEAD_SIZE), part),
                pl.BlockSpec((QUERY_BLOCK, HEAD_SIZE), part),
                pl.BlockSpec((1, 8, QUERY_BLOCK), lambda i, p, f: (i, 0, 0)),
                pl.BlockSpec((length, HEAD_SIZE), lambda i, p, f: (0, 1)),
                pl.BlockSpec((length, HEAD_SIZE), whole),
            ],
            out_specs=[
                pl.BlockSpec((QUERY_BLOCK, HEAD_SIZE), part),
                pl.BlockSpec((length, HEAD_SIZE), whole),
                pl.BlockSpec((length, HEAD_SIZE), whole),
            ],
            scratch_shapes=[
                pltpu.VMEM((length, HEAD_SIZE), BF),
                pltpu.VMEM((length, HEAD_SIZE), BF),
                pltpu.VMEM((HEAD_SIZE, length), BF),
                pltpu.VMEM((length, HEAD_SIZE), F32),
                pltpu.VMEM((length, HEAD_SIZE), F32),
                pltpu.VMEM((HEAD_SIZE, QUERY_BLOCK), F32),
                pltpu.VMEM((8, QUERY_BLOCK), F32),
                pltpu.VMEM((8, QUERY_BLOCK), F32),
            ],
        ),
        out_shape=[
            jax.ShapeDtypeStruct((length, 2 * HEAD_SIZE), BF),
            jax.ShapeDtypeStruct((length, HEAD_SIZE), F32),
            jax.ShapeDtypeStruct((length, HEAD_SIZE), BF),
        ],
        compiler_params=pltpu.CompilerParams(vmem_limit_bytes=VMEM_LIMIT),
        cost_estimate=pl.CostEstimate(
            flops=160 * SEG_LEN * SEG_LEN * HEAD_SIZE * 10,
            bytes_accessed=length * HEAD_SIZE * 24,
            transcendentals=160 * SEG_LEN * SEG_LEN,
        ),
        name="attention_backward",
    )(parent_block, flag, got, grad, attended, totals, got, theirs)


def merge_kernel(lines_ref, kept_ref, got_ref, out_ref):
    out_ref[...] = (kept_ref[...] + got_ref[...].astype(F32)).astype(BF)


def merge(lines, kept, got):
    length = kept.shape[0]
    rows = 4 * SEG_LEN
    part = pl.BlockSpec((rows, HEAD_SIZE), lambda i: (i, 0))
    return pl.pallas_call(
        merge_kernel,
        grid=(length // rows,),
        in_specs=[pl.BlockSpec(memory_space=pl.ANY), part, part],
        out_specs=pl.BlockSpec((rows, HEAD_SIZE), lambda i: (i, 1)),
        out_shape=jax.ShapeDtypeStruct(lines.shape, lines.dtype),
        input_output_aliases={0: 0},
        cost_estimate=pl.CostEstimate(
            flops=length * HEAD_SIZE, bytes_accessed=length * HEAD_SIZE * 10, transcendentals=0
        ),
        name="merge",
    )(lines, kept, got)


def norm_scale(values):
    return lax.rsqrt(jnp.mean(values * values, axis=1, keepdims=True) + EPSILON)


def norm_back(values, scale, gain, gradient):
    weighted = gain * gradient
    inner_sum = jnp.sum(weighted * values, axis=1, keepdims=True)
    return scale * weighted - values * (scale**3 * (inner_sum * (1.0 / MODEL_WIDTH)))


def outmaps_of(w_ref, at, pieces):
    rank = ADAPTER_RANK
    table = jnp.concatenate(
        [w_ref[0, 0, at + p * rank : at + (p + 1) * rank, :] for p in range(pieces)], axis=1
    ).astype(F32)
    wide = table.shape[1]
    lane = lax.broadcasted_iota(jnp.int32, table.shape, 1)
    edges = (0, wide // 2, wide * 3 // 4, wide)
    return jnp.concatenate(
        [
            jnp.where((lane >= edges[i]) & (lane < edges[i + 1]), table, 0.0).astype(BF)
            for i in range(3)
        ],
        axis=0,
    )


def qkv_forward_kernel(
    x_ref,
    gain_ref,
    a_ref,
    cos_ref,
    sin_ref,
    hg_ref,
    w_ref,
    m_ref,
    pre_ref,
    sent_ref,
    hidden_ref,
):
    row_blocks = w_ref.shape[1]
    piece = w_ref.shape[3]
    pieces = w_ref.shape[2] // piece
    heads = sent_ref.shape[0]

    @pl.when(pl.program_id(0) == 0)
    def _():
        resid = x_ref[...].astype(F32)
        hidden_ref[...] = (resid * norm_scale(resid) * gain_ref[...]).astype(BF)
        m_ref[...] = dot(hidden_ref[...], a_ref[...]).astype(BF)

    hidden = hidden_ref[...]
    whole = jnp.concatenate(
        [
            dot(
                hidden,
                jnp.concatenate(
                    [w_ref[0, r, p * piece : (p + 1) * piece, :] for r in range(row_blocks)], axis=0
                ),
            )
            for p in range(pieces)
        ],
        axis=1,
    ) + ADAPTER_FACTOR * dot(m_ref[...], outmaps_of(w_ref, pieces * piece, pieces))
    pre_ref[0] = whole[:, : pre_ref.shape[2]]
    cosine = cos_ref[...]
    sine = sin_ref[...]

    def shaped(at, gain):
        lines = whole[:, at : at + HEAD_SIZE]
        normed = lines * norm_scale(lines) * gain
        return (normed * cosine + pltpu.roll(normed, HEAD_SIZE // 2, 1) * sine).astype(BF)

    for head in range(heads):
        sent_ref[head, :, :HEAD_SIZE] = shaped(head * HEAD_SIZE, hg_ref[0:1, :])
    key_at = heads * HEAD_SIZE
    value_at = key_at + heads // 2 * HEAD_SIZE
    for pair in range(heads // 2):
        at = pair * HEAD_SIZE
        sent_ref[2 * pair, :, HEAD_SIZE:] = shaped(key_at + at, hg_ref[1:2, :])
        sent_ref[2 * pair + 1, :, HEAD_SIZE:] = whole[
            :, value_at + at : value_at + at + HEAD_SIZE
        ].astype(BF)


def qkv_forward(x, gain, inmaps, cosine, sine, head_gains, weights):
    own = x.shape[0]
    cols, row_blocks, tall, piece = weights.shape
    wide = tall // piece * piece
    used = inmaps.shape[1]
    heads = QUERY_HEADS // cols
    whole = lambda c: (0, 0)
    step = lambda c: (c, 0, 0)
    return pl.pallas_call(
        qkv_forward_kernel,
        grid=(cols,),
        in_specs=[
            pl.BlockSpec(x.shape, whole),
            pl.BlockSpec(gain.shape, whole),
            pl.BlockSpec(inmaps.shape, whole),
            pl.BlockSpec(cosine.shape, whole),
            pl.BlockSpec(sine.shape, whole),
            pl.BlockSpec(head_gains.shape, whole),
            pl.BlockSpec((1, row_blocks, tall, piece), lambda c: (c, 0, 0, 0)),
        ],
        out_specs=[
            pl.BlockSpec((own, used), whole),
            pl.BlockSpec((1, own, wide * 3 // 4), step),
            pl.BlockSpec((heads, own, 2 * HEAD_SIZE), step),
        ],
        out_shape=[
            jax.ShapeDtypeStruct((own, used), BF),
            jax.ShapeDtypeStruct((cols, own, wide * 3 // 4), F32),
            jax.ShapeDtypeStruct((QUERY_HEADS, own, 2 * HEAD_SIZE), BF),
        ],
        scratch_shapes=[pltpu.VMEM((own, MODEL_WIDTH), BF)],
        compiler_params=pltpu.CompilerParams(vmem_limit_bytes=VMEM_LIMIT),
        cost_estimate=pl.CostEstimate(
            flops=2 * own * MODEL_WIDTH * cols * wide,
            bytes_accessed=cols * wide * MODEL_WIDTH * 2,
            transcendentals=own * cols * 8,
        ),
        name="qkv_forward",
    )(x, gain, inmaps, cosine, sine, head_gains, weights)


def qkv_unshape_kernel(
    ret_ref,
    pre_ref,
    m_ref,
    x_ref,
    gain_ref,
    cos_ref,
    sin_ref,
    hg_ref,
    w_ref,
    grads_ref,
    inner_ref,
    ga_ref,
    gb_ref,
    in_acc_ref,
):
    step = pl.program_id(0)
    row_blocks, used, piece = ga_ref.shape
    heads = ret_ref.shape[0]
    pieces = grads_ref.shape[2] // piece
    cosine = cos_ref[...]
    sine = sin_ref[...]

    @pl.when(step == 0)
    def _():
        in_acc_ref[...] = jnp.zeros_like(in_acc_ref)

    def unshaped(grad, at, gain):
        grad = grad.astype(F32)
        lines = pre_ref[0, :, at : at + HEAD_SIZE]
        turned = gain * (grad * cosine + pltpu.roll(grad * sine, HEAD_SIZE // 2, 1))
        scale = norm_scale(lines)
        inner_mean = jnp.mean(turned * lines, axis=1, keepdims=True)
        return (scale * turned - lines * (scale**3 * inner_mean)).astype(BF)

    parts = []
    for head in range(heads):
        parts.append(unshaped(ret_ref[head, :, :HEAD_SIZE], head * HEAD_SIZE, hg_ref[0:1, :]))
    for pair in range(heads // 2):
        at = (heads + pair) * HEAD_SIZE
        parts.append(unshaped(ret_ref[2 * pair, :, HEAD_SIZE:], at, hg_ref[1:2, :]))
    for pair in range(heads // 2):
        parts.append(ret_ref[2 * pair + 1, :, HEAD_SIZE:])
    grads = jnp.concatenate(parts, axis=1)
    grads_ref[0] = grads
    outmaps = outmaps_of(w_ref, 0, pieces)
    in_acc_ref[...] += dot_nt(grads, outmaps)
    outer = ADAPTER_FACTOR * dot_tn(m_ref[...], grads)
    rank = ADAPTER_RANK
    edges = (0, heads * HEAD_SIZE, heads * HEAD_SIZE * 3 // 2, heads * HEAD_SIZE * 2)
    for i in range(3):
        gb_ref[0, :, edges[i] : edges[i + 1]] = outer[
            i * rank : (i + 1) * rank, edges[i] : edges[i + 1]
        ]

    @pl.when(step == pl.num_programs(0) - 1)
    def _():
        inner = (ADAPTER_FACTOR * in_acc_ref[...]).astype(BF)
        inner_ref[...] = inner
        resid = x_ref[...].astype(F32)
        hidden = (resid * norm_scale(resid) * gain_ref[...]).astype(BF)
        for r in range(row_blocks):
            ga_ref[r] = dot_tn(inner, hidden[:, r * piece : (r + 1) * piece])


def qkv_unshape(returned, pre, masked, x, gain, cosine, sine, head_gains, weights):
    own = x.shape[0]
    cols, row_blocks, tall, piece = weights.shape
    pieces = tall // piece
    wide = pieces * piece
    heads = QUERY_HEADS // cols
    used = 3 * ADAPTER_RANK
    map_rows = tall - wide
    at = wide // map_rows if wide % map_rows == 0 else None
    maps = weights[:, :1, wide:] if at is None else weights
    first = 0 if at is None else at
    whole = lambda c: (0, 0)
    step = lambda c: (c, 0, 0)
    return pl.pallas_call(
        qkv_unshape_kernel,
        grid=(cols,),
        in_specs=[
            pl.BlockSpec((heads, own, 2 * HEAD_SIZE), step),
            pl.BlockSpec((1, own, pre.shape[2]), step),
            pl.BlockSpec(masked.shape, whole),
            pl.BlockSpec(x.shape, whole),
            pl.BlockSpec(gain.shape, whole),
            pl.BlockSpec(cosine.shape, whole),
            pl.BlockSpec(sine.shape, whole),
            pl.BlockSpec(head_gains.shape, whole),
            pl.BlockSpec((1, 1, map_rows, piece), lambda c: (c, 0, first, 0)),
        ],
        out_specs=[
            pl.BlockSpec((1, own, wide), step),
            pl.BlockSpec((own, used), whole),
            pl.BlockSpec((row_blocks, used, piece), lambda c: (0, 0, 0)),
            pl.BlockSpec((1, ADAPTER_RANK, wide), step),
        ],
        out_shape=[
            jax.ShapeDtypeStruct((cols, own, wide), BF),
            jax.ShapeDtypeStruct((own, used), BF),
            jax.ShapeDtypeStruct((row_blocks, used, piece), F32),
            jax.ShapeDtypeStruct((cols, ADAPTER_RANK, wide), F32),
        ],
        scratch_shapes=[pltpu.VMEM((own, used), F32)],
        compiler_params=pltpu.CompilerParams(vmem_limit_bytes=VMEM_LIMIT),
        cost_estimate=pl.CostEstimate(
            flops=4 * own * 64 * cols * wide,
            bytes_accessed=cols * own * wide * 8,
            transcendentals=own * cols * 8,
        ),
        name="qkv_unshape",
    )(returned, pre, masked, x, gain, cosine, sine, head_gains, maps)


def qkv_backward_kernel(
    grads_ref, inner_ref, x_ref, gm_ref, gain_ref, a_ref, w_ref, grad_ref, acc_ref
):
    step = pl.program_id(0)
    row_blocks = w_ref.shape[1]
    piece = w_ref.shape[3]
    pieces = w_ref.shape[2] // piece

    @pl.when(step == 0)
    def _():
        acc_ref[...] = dot_nt(inner_ref[...], a_ref[...])

    for r in range(row_blocks):
        weights = jnp.concatenate(
            [w_ref[0, r, p * piece : (p + 1) * piece, :] for p in range(pieces)], axis=1
        )
        acc_ref[:, r * piece : (r + 1) * piece] += dot_nt(grads_ref[0], weights)

    @pl.when(step == pl.num_programs(0) - 1)
    def _():
        resid = x_ref[...].astype(F32)
        grad_ref[...] = (
            gm_ref[...] + norm_back(resid, norm_scale(resid), gain_ref[...], acc_ref[...])
        ).astype(BF)


def qkv_backward(grads, inner, x, grad_middle, gain, inmaps, weights):
    own = x.shape[0]
    cols, row_blocks, tall, piece = weights.shape
    wide = tall // piece * piece
    whole = lambda c: (0, 0)
    once = pl.Buffered(1)
    return pl.pallas_call(
        qkv_backward_kernel,
        grid=(cols,),
        in_specs=[
            pl.BlockSpec((1, own, wide), lambda c: (c, 0, 0)),
            pl.BlockSpec(inner.shape, whole),
            pl.BlockSpec(x.shape, whole, pipeline_mode=once),
            pl.BlockSpec(grad_middle.shape, whole, pipeline_mode=once),
            pl.BlockSpec(gain.shape, whole),
            pl.BlockSpec(inmaps.shape, whole),
            pl.BlockSpec((1, row_blocks, wide, piece), lambda c: (c, 0, 0, 0)),
        ],
        out_specs=pl.BlockSpec((own, MODEL_WIDTH), whole),
        out_shape=jax.ShapeDtypeStruct((own, MODEL_WIDTH), BF),
        scratch_shapes=[pltpu.VMEM((own, MODEL_WIDTH), F32)],
        compiler_params=pltpu.CompilerParams(vmem_limit_bytes=VMEM_LIMIT),
        cost_estimate=pl.CostEstimate(
            flops=2 * own * MODEL_WIDTH * cols * wide,
            bytes_accessed=cols * wide * MODEL_WIDTH * 2,
            transcendentals=own,
        ),
        name="qkv_backward",
    )(grads, inner, x, grad_middle, gain, inmaps, weights)


def whole_output_weights(flag_ref, own_ref, other_ref):
    own, other = (
        jnp.concatenate([ref[0, r] for r in range(ref.shape[1])], axis=1)
        for ref in (own_ref, other_ref)
    )
    first = flag_ref[0] == 0
    return jnp.concatenate(
        [jnp.where(first, own, other), jnp.where(first, other, own)], axis=0
    )


def output_forward_kernel(
    flag_ref,
    att_ref,
    x_ref,
    gain_ref,
    a_ref,
    b_ref,
    own_ref,
    other_ref,
    middle_ref,
    hidden_ref,
    m_ref,
    acc_ref,
    m_acc_ref,
):
    step = pl.program_id(0)
    heads = att_ref.shape[0]

    @pl.when(step == 0)
    def _():
        acc_ref[...] = x_ref[...].astype(F32)
        m_acc_ref[...] = jnp.zeros_like(m_acc_ref)

    attended = jnp.concatenate([att_ref[h] for h in range(heads)], axis=1)
    acc_ref[...] += dot(attended, whole_output_weights(flag_ref, own_ref, other_ref))
    m_acc_ref[...] += dot_nt(attended, a_ref[0])

    @pl.when(step == pl.num_programs(0) - 1)
    def _():
        masked = m_acc_ref[...].astype(BF)
        m_ref[...] = masked
        middle = acc_ref[...] + ADAPTER_FACTOR * dot_nt(masked, b_ref[...])
        middle_ref[...] = middle
        hidden_ref[...] = (middle * norm_scale(middle) * gain_ref[...]).astype(BF)


def output_forward(flag, attended, x, gain, inmaps, outmaps, weights):
    own = x.shape[0]
    cols = weights[0].shape[0]
    heads = QUERY_HEADS // cols
    o_rows = heads * HEAD_SIZE
    half = pl.BlockSpec((1, *weights[0].shape[1:]), lambda c: (c, 0, 0, 0))
    whole = lambda c: (0, 0)
    step = lambda c: (c, 0, 0)
    return pl.pallas_call(
        output_forward_kernel,
        grid=(cols,),
        in_specs=[
            pl.BlockSpec(memory_space=pltpu.SMEM),
            pl.BlockSpec((heads, own, HEAD_SIZE), step),
            pl.BlockSpec(x.shape, whole),
            pl.BlockSpec(gain.shape, whole),
            pl.BlockSpec((1, LANES, o_rows), step),
            pl.BlockSpec(outmaps.shape, whole),
            half,
            half,
        ],
        out_specs=[
            pl.BlockSpec((own, MODEL_WIDTH), whole),
            pl.BlockSpec((own, MODEL_WIDTH), whole),
            pl.BlockSpec((own, LANES), whole),
        ],
        out_shape=[
            jax.ShapeDtypeStruct((own, MODEL_WIDTH), F32),
            jax.ShapeDtypeStruct((own, MODEL_WIDTH), BF),
            jax.ShapeDtypeStruct((own, LANES), BF),
        ],
        scratch_shapes=[pltpu.VMEM((own, MODEL_WIDTH), F32), pltpu.VMEM((own, LANES), F32)],
        compiler_params=pltpu.CompilerParams(vmem_limit_bytes=VMEM_LIMIT),
        cost_estimate=pl.CostEstimate(
            flops=2 * own * MODEL_WIDTH * MODEL_WIDTH,
            bytes_accessed=2 * MODEL_WIDTH * MODEL_WIDTH,
            transcendentals=own,
        ),
        name="output_forward",
    )(flag, attended, x, gain, inmaps, outmaps, *weights)


def output_backward_kernel(
    flag_ref,
    gh_ref,
    got_ref,
    cot_ref,
    middle_ref,
    gain_ref,
    a_ref,
    b_ref,
    att_ref,
    m_ref,
    own_ref,
    other_ref,
    gm_ref,
    sent_ref,
    gb_ref,
    ga_ref,
    low_ref,
    inner_ref,
):
    heads = sent_ref.shape[0]
    row_blocks, rank, features = gb_ref.shape

    @pl.when(pl.program_id(0) == 0)
    def _():
        grad_hidden = gh_ref[...] + got_ref[...].astype(F32)
        middle = middle_ref[...]
        grad = cot_ref[...].astype(F32) + norm_back(
            middle, norm_scale(middle), gain_ref[...], grad_hidden
        )
        gm_ref[...] = grad
        low_ref[...] = grad.astype(BF)
        inner_ref[...] = (ADAPTER_FACTOR * dot(low_ref[...], b_ref[...])).astype(BF)
        outer = ADAPTER_FACTOR * dot_tn(m_ref[...], low_ref[...])
        for r in range(row_blocks):
            gb_ref[r] = outer[:rank, r * features : (r + 1) * features]

    attended = jnp.concatenate([att_ref[h] for h in range(heads)], axis=1)
    ga_ref[0] = dot_tn(inner_ref[...], attended)[:rank, :]
    weights = whole_output_weights(flag_ref, own_ref, other_ref)
    grad = (dot_nt(low_ref[...], weights) + dot(inner_ref[...], a_ref[0])).astype(BF)
    for head in range(heads):
        sent_ref[head] = grad[:, head * HEAD_SIZE : (head + 1) * HEAD_SIZE]


def output_backward(
    flag, grad_hidden, got, cotangent, middle, gain, inmaps, outmaps, attended, masked, weights
):
    own = middle.shape[0]
    cols, row_blocks = weights[0].shape[:2]
    features = MODEL_WIDTH // row_blocks
    heads = QUERY_HEADS // cols
    o_rows = heads * HEAD_SIZE
    half = pl.BlockSpec((1, *weights[0].shape[1:]), lambda c: (c, 0, 0, 0))
    whole = lambda c: (0, 0)
    step = lambda c: (c, 0, 0)
    once = pl.Buffered(1)
    return pl.pallas_call(
        output_backward_kernel,
        grid=(cols,),
        in_specs=[
            pl.BlockSpec(memory_space=pltpu.SMEM),
            pl.BlockSpec((own, MODEL_WIDTH), whole, pipeline_mode=once),
            pl.BlockSpec((own, MODEL_WIDTH), whole, pipeline_mode=once),
            pl.BlockSpec((own, MODEL_WIDTH), whole, pipeline_mode=once),
            pl.BlockSpec((own, MODEL_WIDTH), whole, pipeline_mode=once),
            pl.BlockSpec(gain.shape, whole),
            pl.BlockSpec((1, LANES, o_rows), step),
            pl.BlockSpec(outmaps.shape, whole),
            pl.BlockSpec((heads, own, HEAD_SIZE), step),
            pl.BlockSpec(masked.shape, whole),
            half,
            half,
        ],
        out_specs=[
            pl.BlockSpec((own, MODEL_WIDTH), whole),
            pl.BlockSpec((heads, own, HEAD_SIZE), step),
            pl.BlockSpec((row_blocks, ADAPTER_RANK, features), lambda c: (0, 0, 0)),
            pl.BlockSpec((1, ADAPTER_RANK, o_rows), step),
        ],
        out_shape=[
            jax.ShapeDtypeStruct((own, MODEL_WIDTH), F32),
            jax.ShapeDtypeStruct((QUERY_HEADS, own, HEAD_SIZE), BF),
            jax.ShapeDtypeStruct((row_blocks, ADAPTER_RANK, features), F32),
            jax.ShapeDtypeStruct((cols, ADAPTER_RANK, o_rows), F32),
        ],
        scratch_shapes=[pltpu.VMEM((own, MODEL_WIDTH), BF), pltpu.VMEM((own, LANES), BF)],
        compiler_params=pltpu.CompilerParams(vmem_limit_bytes=VMEM_LIMIT),
        cost_estimate=pl.CostEstimate(
            flops=2 * own * MODEL_WIDTH * MODEL_WIDTH,
            bytes_accessed=2 * MODEL_WIDTH * MODEL_WIDTH,
            transcendentals=own,
        ),
        name="output_backward",
    )(
        flag,
        grad_hidden,
        got,
        cotangent,
        middle,
        gain,
        inmaps,
        outmaps,
        attended,
        masked,
        *weights,
    )


def feed_forward_kernel(
    first, last, group, h_ref, c_ref, mg_ref, mu_ref, nd_ref, mask_ref, ag_ref, au_ref, od_ref, *refs
):
    weight_refs, map_refs, refs = refs[:group], refs[group : 2 * group], refs[2 * group :]
    if first:
        previous = None
    else:
        previous, refs = refs[:5], refs[5:]
    if last:
        (gh_ref, out_ref, rows_ref), refs = refs[:3], refs[3:]
    else:
        accs, refs = refs[:5], refs[5:]
    grads_refs, refs = refs[:group], refs[group:]
    gh_acc, out_acc, md_acc, ig_acc, iu_acc = scratch = refs[:5]
    sems = refs[5]
    step = pl.program_id(0)
    row_blocks = weight_refs[0].shape[1]
    deep = MODEL_WIDTH // row_blocks
    used = mg_ref.shape[1]

    @pl.when(step == 0)
    def _():
        if first:
            for ref in scratch:
                ref[...] = jnp.zeros_like(ref)
        else:
            for i in range(5):
                pltpu.make_async_copy(previous[i], scratch[i], sems.at[i]).start()

    def side(kind, row):
        return jnp.concatenate(
            [ref[0, row, kind * deep : (kind + 1) * deep, :] for ref in weight_refs], axis=1
        )

    def tall_side(kind):
        return jnp.concatenate([side(kind, row) for row in range(row_blocks)], axis=0)

    def down_side(row):
        return jnp.concatenate(
            [
                jnp.concatenate(
                    [
                        ref[0, row, 2 * deep + at : 2 * deep + at + LANES, :]
                        for at in range(0, deep, LANES)
                    ],
                    axis=1,
                )
                for ref in weight_refs
            ],
            axis=0,
        )

    def maps(kind):
        return jnp.concatenate(
            [ref[0, kind * used : (kind + 1) * used, :] for ref in map_refs], axis=1
        )

    gate_map, up_map, down_map = maps(0), maps(1), maps(2)
    units = group * LANES
    gate_up = dot(h_ref[...], jnp.concatenate([tall_side(0), tall_side(1)], axis=1))
    gate = gate_up[:, :units] + ADAPTER_FACTOR * dot(mg_ref[...], gate_map)
    upward = gate_up[:, units:] + ADAPTER_FACTOR * dot(mu_ref[...], up_map)
    down = jnp.concatenate([down_side(row) for row in range(row_blocks)], axis=1)
    grad_act = dot_nt(c_ref[...], down) + dot(nd_ref[...], down_map)
    sigma = 1.0 / (1.0 + jnp.exp(-gate))
    swish = gate * sigma
    act = (swish * upward).astype(BF)
    grad_gate = (grad_act * upward * (sigma * (1.0 + gate * (1.0 - sigma)))).astype(BF)
    grad_up = (grad_act * swish).astype(BF)
    both = jnp.concatenate([grad_gate, grad_up], axis=1)
    if not first:

        @pl.when(step == 0)
        def _():
            for i in range(5):
                pltpu.make_async_copy(previous[i], scratch[i], sems.at[i]).wait()

    for row in range(row_blocks):
        at = slice(row * deep, (row + 1) * deep)
        gh_acc[:, at] += dot_nt(both, jnp.concatenate([side(0, row), side(1, row)], axis=1))
        out_acc[:, at] += dot(act, down_side(row))
    md_acc[...] += dot_nt(act, down_map)
    ig_acc[...] += dot_nt(grad_gate, gate_map)
    iu_acc[...] += dot_nt(grad_up, up_map)
    partial = (
        ADAPTER_FACTOR * dot_tn(mg_ref[...], grad_gate),
        ADAPTER_FACTOR * dot_tn(mu_ref[...], grad_up),
        dot_tn(nd_ref[...], act),
    )
    for kind in range(3):
        for i, ref in enumerate(grads_refs):
            ref[0, kind * used : (kind + 1) * used, :] = partial[kind][
                :, i * LANES : (i + 1) * LANES
            ]

    @pl.when(step == pl.num_programs(0) - 1)
    def _():
        if last:
            mask = mask_ref[...]
            inner_g = (ADAPTER_FACTOR * ig_acc[...] * mask).astype(BF)
            inner_u = (ADAPTER_FACTOR * iu_acc[...] * mask).astype(BF)
            masked = (md_acc[...] * mask).astype(BF)
            gh_ref[...] = (
                gh_acc[...] + dot_nt(inner_g, ag_ref[...]) + dot_nt(inner_u, au_ref[...])
            ).astype(gh_ref.dtype)
            out_ref[...] = (out_acc[...] + ADAPTER_FACTOR * dot_nt(masked, od_ref[...])).astype(
                out_ref.dtype
            )
            for row in range(row_blocks):
                at = slice(row * deep, (row + 1) * deep)
                rows_ref[row, :used, :] = dot_tn(inner_g, h_ref[:, at])
                rows_ref[row, used : 2 * used, :] = dot_tn(inner_u, h_ref[:, at])
                rows_ref[row, 2 * used :, :] = ADAPTER_FACTOR * dot_tn(masked, c_ref[:, at])
        else:
            copies = [pltpu.make_async_copy(scratch[i], accs[i], sems.at[i]) for i in range(5)]
            for copy in copies:
                copy.start()
            for copy in copies:
                copy.wait()


def slab_group(count):
    return 4 if count % 4 == 0 else 2


def feed_forward_chunk(hidden, cotangent, masks, tables, weights, maps, previous, last, dtype):
    first = previous is None
    cols, row_blocks = weights.shape[:2]
    deep = MODEL_WIDTH // row_blocks
    slabs = maps.shape[0] // cols
    count, used = masks[0].shape
    whole = lambda i: (0, 0)
    once = pl.Buffered(1)
    group = slab_group(cols * slabs)
    steps = cols * slabs // group
    acc_shapes = [(count, MODEL_WIDTH)] * 2 + [(count, used)] * 3

    def weight_spec(side):
        def at(i):
            return ((group * i + side) // slabs, 0, (group * i + side) % slabs, 0)

        return pl.BlockSpec((1, row_blocks, 3 * deep, LANES), at)

    def slab_spec(side):
        return pl.BlockSpec((1, 3 * used, LANES), lambda i: (group * i + side, 0, 0))

    step_spec = pl.BlockSpec((1, 3 * used, LANES), lambda i: (i, 0, 0))
    in_specs = (
        [pl.BlockSpec((count, MODEL_WIDTH), whole, pipeline_mode=once)] * 2
        + [pl.BlockSpec((count, used), whole)] * 4
        + [pl.BlockSpec((MODEL_WIDTH, used), whole, pipeline_mode=once)] * 3
        + [weight_spec(side) for side in range(group)]
        + [slab_spec(side) for side in range(group)]
    )
    operands = [hidden, cotangent, *masks, *tables] + [weights] * group + [maps] * group
    if not first:
        in_specs = in_specs + [pl.BlockSpec(memory_space=pl.ANY)] * 5
        operands = operands + list(previous)
    if last:
        out_specs = [pl.BlockSpec((count, MODEL_WIDTH), whole)] * 2 + [
            pl.BlockSpec((row_blocks, 3 * used, deep), lambda i: (0, 0, 0))
        ]
        out_shape = [jax.ShapeDtypeStruct(s, dtype) for s in acc_shapes[:2]] + [
            jax.ShapeDtypeStruct((row_blocks, 3 * used, deep), F32)
        ]
    else:
        out_specs = [pl.BlockSpec(memory_space=pl.ANY)] * 5
        out_shape = [jax.ShapeDtypeStruct(s, F32) for s in acc_shapes]
    outs = pl.pallas_call(
        functools.partial(feed_forward_kernel, first, last, group),
        grid=(steps,),
        in_specs=in_specs,
        out_specs=out_specs + [step_spec] * group,
        out_shape=out_shape + [jax.ShapeDtypeStruct((steps, 3 * used, LANES), F32)] * group,
        scratch_shapes=[pltpu.VMEM(s, F32) for s in acc_shapes]
        + [pltpu.SemaphoreType.DMA((5,))],
        compiler_params=pltpu.CompilerParams(vmem_limit_bytes=VMEM_LIMIT),
        cost_estimate=pl.CostEstimate(
            flops=12 * count * MODEL_WIDTH * cols * slabs * LANES,
            bytes_accessed=cols * slabs * row_blocks * 3 * deep * LANES * 2,
            transcendentals=count * cols * slabs * LANES,
        ),
        name="feed_forward",
    )(*operands)
    return outs[:-group], outs[-group:]


def placed(ids_ref, first, second, count):
    zero = jnp.zeros_like(first)
    blocks = []
    for slot in range(count):
        blocks.append(
            jnp.where(ids_ref[0] == slot, first, zero)
            + jnp.where(ids_ref[1] == slot, second, zero)
        )
    return jnp.concatenate(blocks, axis=0)


def finish_middle_kernel(
    ids_ref, row_ref, col_ref, a_o, b_o, a_gate, b_gate, a_up, b_up, a_down, b_down
):
    rank = ADAPTER_RANK
    count = b_o.shape[0] // rank
    half = b_gate.shape[1] // 2

    def part(ref, tree, at):
        return ref[tree, at * rank : (at + 1) * rank, :].astype(F32)

    def both_planes(at):
        first = part(row_ref, 0, at) + part(row_ref, 1, at + 1)
        second = part(row_ref, 0, at + 1) + part(row_ref, 1, at)
        return placed(ids_ref, first, second, count)

    a_gate[...] = jnp.transpose(both_planes(0))
    a_up[...] = jnp.transpose(both_planes(2))
    b_down[...] = both_planes(4)
    b_o[...] = placed(ids_ref, part(row_ref, 0, 6), part(row_ref, 1, 6), count)
    o_rows = a_o.shape[0]
    a_o[...] = jnp.transpose(
        placed(ids_ref, part(col_ref, 0, 6)[:, :o_rows], part(col_ref, 1, 6)[:, :o_rows], count)
    )
    low_plane = ids_ref[2] == 0

    def halves(at):
        mine = placed(ids_ref, part(col_ref, 0, at), part(col_ref, 0, at + 1), count)[:, :half]
        theirs = placed(ids_ref, part(col_ref, 1, at + 1), part(col_ref, 1, at), count)[:, :half]
        return jnp.where(low_plane, mine, theirs), jnp.where(low_plane, theirs, mine)

    for at, out in ((0, b_gate), (2, b_up)):
        low, high = halves(at)
        out[:, :half] = low
        out[:, half:] = high
    low, high = halves(4)
    a_down[:half, :] = jnp.transpose(low)
    a_down[half:, :] = jnp.transpose(high)


def finish_end_kernel(ids_ref, row_ref, col_ref, a_q, b_q, a_k, b_k, a_v, b_v):
    rank = ADAPTER_RANK
    count = b_q.shape[0] // rank
    for at, out in enumerate((a_q, a_k, a_v)):
        rows = slice(at * rank, (at + 1) * rank)
        out[...] = jnp.transpose(
            placed(ids_ref, row_ref[0, rows, :].astype(F32), row_ref[1, rows, :].astype(F32), count)
        )
    start = 0
    for out in (b_q, b_k, b_v):
        lanes = slice(start, start + out.shape[1])
        out[...] = placed(
            ids_ref, col_ref[0, :, lanes].astype(F32), col_ref[1, :, lanes].astype(F32), count
        )
        start = start + out.shape[1]


def finish(kernel, ids, row_table, col_table, shapes, name):
    size = sum(shape[0] * shape[1] for shape in shapes)
    return pl.pallas_call(
        kernel,
        in_specs=[
            pl.BlockSpec(memory_space=pltpu.SMEM),
            pl.BlockSpec(memory_space=pltpu.VMEM),
            pl.BlockSpec(memory_space=pltpu.VMEM),
        ],
        out_specs=[pl.BlockSpec(memory_space=pltpu.VMEM)] * len(shapes),
        out_shape=[jax.ShapeDtypeStruct(shape, F32) for shape in shapes],
        cost_estimate=pl.CostEstimate(flops=size, bytes_accessed=8 * size, transcendentals=0),
        name=name,
    )(ids, row_table, col_table)


def lane_pad(values):
    return jnp.pad(values, ((0, 0),) * (values.ndim - 1) + ((0, LANES - values.shape[-1]),))


def row_pad(values):
    return jnp.pad(
        values, ((0, 0),) * (values.ndim - 2) + ((0, LANES - values.shape[-2]), (0, 0))
    )


def thirds(values):
    parts = []
    for _ in range(3):
        part = lax.reduce_precision(values, 8, 7)
        parts.append(part.astype(BF)[:, None])
        values = values - part
    return parts


def on_device(
    tokens,
    cotangent,
    attention_norm_gain,
    feedfwd_norm_gain,
    query_norm_gain,
    key_norm_gain,
    query_matrix,
    key_matrix,
    value_matrix,
    output_matrix,
    gate_matrix,
    up_matrix,
    down_matrix,
    query_adapter_inmaps,
    query_adapter_outmaps,
    key_adapter_inmaps,
    key_adapter_outmaps,
    value_adapter_inmaps,
    value_adapter_outmaps,
    output_adapter_inmaps,
    output_adapter_outmaps,
    gate_adapter_inmaps,
    gate_adapter_outmaps,
    up_adapter_inmaps,
    up_adapter_outmaps,
    down_adapter_inmaps,
    down_adapter_outmaps,
    segment,
    depth,
    parent,
    adapter,
):
    rows = lax.axis_size("row")
    cols = lax.axis_size("col")
    devices = rows * cols
    repeat = devices // QUERY_HEADS
    plane = lax.axis_index("dp")
    row = lax.axis_index("row")
    col = lax.axis_index("col")
    length = segment.shape[0]
    own = tokens.shape[0] // rows
    columns = query_adapter_inmaps.shape[1]
    rank = ADAPTER_RANK
    swap = [(0, 1), (1, 0)]
    pairs = [(r, r ^ repeat) for r in range(rows)]
    q_local = query_matrix.shape[1]
    kv_local = key_matrix.shape[1]
    wide = q_local + 2 * kv_local
    features = gate_matrix.shape[0]

    own_adapter = adapter[0]
    other_adapter = lax.ppermute(adapter, "dp", swap)[0]
    both = (own_adapter, other_adapter)

    def inmap(table, at):
        return lax.dynamic_slice_in_dim(table, at * rank, rank, 1)

    def outmap(table, at):
        return lax.dynamic_slice_in_dim(table, at * rank, rank, 0)

    qkv_local = jnp.concatenate([query_matrix, key_matrix, value_matrix], axis=1)

    qkv_maps = jnp.concatenate(
        [
            outmap(query_adapter_outmaps, own_adapter),
            outmap(key_adapter_outmaps, own_adapter),
            outmap(value_adapter_outmaps, own_adapter),
        ],
        axis=1,
    )
    attention_pack = jnp.concatenate(
        [
            table[:, at : at + features]
            for table in (qkv_local, qkv_maps)
            for at in range(0, wide, features)
        ]
        + [
            lax.dynamic_slice_in_dim(
                output_matrix, plane * (output_matrix.shape[0] // 2), output_matrix.shape[0] // 2, 0
            )
        ],
        axis=0,
    )
    attention_weights = lax.all_gather(attention_pack, PLANE, axis=0, tiled=True).reshape(
        cols, rows, -1, features
    )
    o_rows = output_matrix.shape[0]
    own_output_weights = attention_weights[:, :, -(o_rows // 2) :]
    plane_flag = plane.astype(jnp.int32).reshape(1)
    ffn_half = gate_matrix.shape[1] // 2
    half_start = plane * ffn_half
    chunks = 2 if ffn_half % 256 == 0 else 3
    width = ffn_half // chunks
    slabs = width // LANES

    def plates(table):
        return [table[:, at : at + LANES] for at in range(0, table.shape[1], LANES)]

    def half_of(table):
        return lax.dynamic_slice_in_dim(table, half_start, ffn_half, 1)

    map_width = max(ffn_half, o_rows)

    def to_width(table):
        return jnp.pad(table, ((0, 0), (0, map_width - table.shape[1])))

    col_pack = jnp.concatenate(
        [
            *[to_width(half_of(outmap(gate_adapter_outmaps, a))) for a in both],
            *[to_width(half_of(outmap(up_adapter_outmaps, a))) for a in both],
            *[to_width(half_of(inmap(down_adapter_inmaps, a).T)) for a in both],
            to_width(inmap(output_adapter_inmaps, own_adapter).T),
            jnp.zeros((rank, map_width), BF),
        ],
        axis=0,
    )
    map_rows = col_pack.shape[0] // rows
    map_plates = plates(lax.dynamic_slice_in_dim(col_pack, row * map_rows, map_rows, 0))
    ffn_weights = []
    for chunk in range(chunks):
        pack = []
        for slab in range(slabs):
            start = half_start + (chunk * slabs + slab) * LANES
            pack.append(lax.dynamic_slice_in_dim(gate_matrix, start, LANES, 1))
            pack.append(lax.dynamic_slice_in_dim(up_matrix, start, LANES, 1))
            pack.extend(plates(lax.dynamic_slice_in_dim(down_matrix, start, LANES, 0)))
        if chunk == 0:
            pack = pack + map_plates
        pack = jnp.concatenate(pack, axis=0)
        ffn_weights.append(
            lax.all_gather(pack, PLANE, axis=0, tiled=True).reshape(cols, rows, -1, LANES)
        )
    col_maps = ffn_weights[0][:, :, 3 * slabs * features :].reshape(
        cols, rows, len(map_plates), map_rows, LANES
    )
    col_maps = jnp.transpose(col_maps, (0, 2, 1, 3, 4)).reshape(
        cols, len(map_plates), rows * map_rows, LANES
    )
    in_o = jnp.transpose(col_maps[:, : o_rows // LANES, 6 * rank : 7 * rank], (0, 2, 1, 3))
    in_o = row_pad(in_o.reshape(cols, rank, o_rows))

    row_pack = jnp.concatenate(
        [
            inmap(query_adapter_inmaps, own_adapter),
            inmap(key_adapter_inmaps, own_adapter),
            inmap(value_adapter_inmaps, own_adapter),
            *[inmap(gate_adapter_inmaps, a) for a in both],
            *[inmap(up_adapter_inmaps, a) for a in both],
            *[outmap(down_adapter_outmaps, a).T for a in both],
            outmap(output_adapter_outmaps, own_adapter).T,
            *thirds(attention_norm_gain),
            *thirds(feedfwd_norm_gain),
        ],
        axis=1,
    )

    row_maps = lax.all_gather(row_pack, "row", axis=0, tiled=True)
    in_qkv = row_maps[:, : 3 * rank]
    in_gate = row_maps[:, 3 * rank : 5 * rank]
    in_up = row_maps[:, 5 * rank : 7 * rank]
    out_down = row_maps[:, 7 * rank : 9 * rank]
    out_o = lane_pad(row_maps[:, 9 * rank : 10 * rank])
    gain_parts = row_maps[:, 10 * rank :].astype(F32)
    gain_one = (gain_parts[:, 0] + (gain_parts[:, 1] + gain_parts[:, 2])).reshape(1, -1)
    gain_two = (gain_parts[:, 3] + (gain_parts[:, 4] + gain_parts[:, 5])).reshape(1, -1)

    own_tokens = lax.all_to_all(tokens, "row", 0, 1, tiled=True)
    own_cotangent = lax.all_to_all(cotangent, "row", 0, 1, tiled=True)
    other_cotangent = lax.ppermute(own_cotangent, "dp", swap)
    own_tokens, other_cotangent, own_output_weights = lax.optimization_barrier(
        (own_tokens, other_cotangent, own_output_weights)
    )
    other_output_weights = lax.ppermute(own_output_weights, "dp", swap)
    head_gains = jnp.stack([query_norm_gain, key_norm_gain], axis=0)
    token_start = (col * rows + row) * own
    positions = lax.dynamic_slice_in_dim(depth, token_start, own, 0).astype(F32)
    half = HEAD_SIZE // 2
    freqs = THETA ** (-2.0 * jnp.arange(half).astype(F32) / HEAD_SIZE)
    angle = positions[:, None] * freqs[None, :]
    cosine = jnp.tile(jnp.cos(angle), (1, 2))
    sine = jnp.concatenate([-jnp.sin(angle), jnp.sin(angle)], axis=1)

    masked_qkv, pre, sent = qkv_forward(
        own_tokens, gain_one, in_qkv, cosine, sine, head_gains, attention_weights
    )

    def to_heads(sent):
        if repeat > 1:
            sent = jnp.repeat(sent, repeat, axis=0)
        return lax.all_to_all(sent, PLANE, 0, 0, tiled=True).reshape(length, sent.shape[2])

    def to_tokens(lines):
        got = lax.all_to_all(
            lines.reshape(devices, own, lines.shape[1]), PLANE, 0, 0, tiled=True
        )
        return got[::repeat] if repeat > 1 else got

    got, other_output_weights = lax.optimization_barrier((to_heads(sent), other_output_weights))
    output_weights = (own_output_weights, other_output_weights)
    theirs = lax.ppermute(got[:, HEAD_SIZE:], "row", pairs)
    flag = (1 - (row // repeat) % 2).astype(jnp.int32).reshape(1)

    block_node = segment.reshape(-1, SEG_LEN)[:, 0]
    nodes = jnp.arange(parent.shape[1])
    node_parent = jnp.sum(jnp.where(block_node[:, None] == nodes, parent.reshape(1, -1), 0), axis=1)
    block_index = jnp.arange(block_node.shape[0])
    parent_block = jnp.max(
        jnp.where(node_parent[:, None] == block_node[None, :], block_index[None, :], 0), axis=1
    )
    parent_block = jnp.where(node_parent > 0, parent_block, -1).astype(jnp.int32)
    head_attended, head_low, totals = attention_forward(parent_block, flag, got, theirs)
    attended = to_tokens(head_low)

    middle, hidden_ffn, masked_o = output_forward(
        plane_flag, attended, own_tokens, gain_two, in_o, out_o, output_weights
    )

    other_ffn = lax.ppermute(hidden_ffn, "dp", swap)
    tables = (in_gate, in_up, out_down)
    column_tree = jnp.arange(2 * rank)[None, :] // rank

    def masks_of(hidden, cot, tree):
        mask = jnp.broadcast_to((column_tree == tree).astype(F32), (own, 2 * rank))
        return (
            (dot(hidden, in_gate) * mask).astype(BF),
            (dot(hidden, in_up) * mask).astype(BF),
            (ADAPTER_FACTOR * dot(cot, out_down) * mask).astype(BF),
            mask,
        )

    parts = []

    def run(chunk, side, masks, accs):
        hidden, cot = side
        maps = col_maps[:, chunk * slabs : (chunk + 1) * slabs].reshape(cols * slabs, -1, LANES)
        last = chunk == chunks - 1
        return feed_forward_chunk(
            hidden,
            cot,
            masks,
            tables,
            ffn_weights[chunk],
            maps,
            accs,
            last,
            F32 if side is own_side else BF,
        )

    own_side = (hidden_ffn, own_cotangent)
    own_masks = masks_of(*own_side, 0)
    here, own_part = run(0, own_side, own_masks, None)
    other_ffn, here = lax.optimization_barrier((other_ffn, here))
    other_side = (other_ffn, other_cotangent)
    other_masks = masks_of(*other_side, 1)
    there, other_part = run(0, other_side, other_masks, None)
    parts = [(own_part, other_part)]
    for chunk in range(1, chunks):
        there, other_part = run(chunk, other_side, other_masks, there)
        here, own_part = run(chunk, own_side, own_masks, here)
        parts.append((own_part, other_part))

    def slab_order(part):
        part = [first + second for first, second in zip(*part)]
        part = jnp.stack(part, axis=1).reshape(cols, slabs, 6 * rank, LANES)
        return jnp.transpose(part, (0, 2, 1, 3)).reshape(cols, 6 * rank, width)

    parts = [slab_order(part) for part in parts]
    gh_other = lax.ppermute(there[0], "dp", swap)

    grad_middle, sent, grad_o_rows, grad_o_cols = output_backward(
        plane_flag,
        here[0],
        gh_other,
        own_cotangent,
        middle,
        gain_two,
        in_o,
        out_o,
        attended,
        masked_o,
        output_weights,
    )
    out_sent, sent = lax.optimization_barrier((there[1], sent))
    out_other = lax.ppermute(out_sent, "dp", swap)
    head_grad = to_heads(sent)

    def pieces_of(row_table, col_table):
        row_table = jnp.swapaxes(row_table.astype(BF).reshape(rows, cols, -1, LANES), 0, 1)
        col_table = col_table.astype(BF).reshape(cols, rows, -1, LANES)
        return jnp.concatenate([row_table, col_table], axis=2).reshape(devices, -1, LANES)

    def gathered(values, axis, at):
        size = lax.axis_size(axis)
        whole = jnp.zeros((2, size, *values.shape[1:]), values.dtype)
        for k in range(size):
            block = values
            if k:
                block = lax.ppermute(values, axis, [(i, i ^ k) for i in range(size)])
            whole = lax.dynamic_update_index_in_dim(whole, block, at ^ k, 1)
        return whole

    def summed(pieces):
        mine = jnp.sum(pieces.astype(F32), axis=0).astype(BF)
        return jnp.stack([mine, lax.ppermute(mine, "dp", swap)], axis=0)

    def gathered_tables(pieces, row_highs, col_highs):
        row_parts = [high * features // (cols * LANES) for high in row_highs]
        row_pieces = [piece[:, :part] for piece, part in zip(pieces, row_parts)]
        col_pieces = [piece[:, part:] for piece, part in zip(pieces, row_parts)]
        row_whole = gathered(jnp.concatenate(row_pieces, axis=1), "col", col)
        col_whole = gathered(jnp.concatenate(col_pieces, axis=1), "row", row)
        tables = []
        row_at = col_at = 0
        for i, (row_high, col_high) in enumerate(zip(row_highs, col_highs)):
            row_size, col_size = row_pieces[i].shape[1], col_pieces[i].shape[1]
            tables.append(
                (
                    row_whole[:, :, row_at : row_at + row_size].reshape(2, row_high, features),
                    col_whole[:, :, col_at : col_at + col_size].reshape(2, col_high, -1),
                )
            )
            row_at, col_at = row_at + row_size, col_at + col_size
        return tables

    def to_own_features(lines):
        blocks = lines.reshape(own, rows, features)
        whole = jnp.zeros((rows, own, features), lines.dtype)
        for k in range(rows):
            block = lax.dynamic_index_in_dim(blocks, row ^ k, 1, False)
            if k:
                block = lax.ppermute(block, "row", [(r, r ^ k) for r in range(rows)])
            whole = lax.dynamic_update_index_in_dim(whole, block, row ^ k, 0)
        return whole.reshape(rows * own, features)

    def to_map_width(table):
        return jnp.pad(table, ((0, 0), (0, 0), (0, map_width - table.shape[2])))

    mid_pieces = pieces_of(
        jnp.concatenate([here[2] + there[2], grad_o_rows], axis=1),
        jnp.concatenate(
            [to_map_width(jnp.concatenate(parts, axis=2)), to_map_width(grad_o_cols)], axis=1
        ),
    )
    head_grad, mid_pieces = lax.optimization_barrier((head_grad, mid_pieces))
    mid_pieces = lax.all_to_all(mid_pieces, PLANE, 0, 0, tiled=True)

    lines, kept, given = attention_backward(
        parent_block, flag, got, head_grad, head_attended, totals, theirs
    )
    lines, kept, given, mid_pieces, out_other = lax.optimization_barrier(
        (lines, kept, given, mid_pieces, out_other)
    )
    returned = to_tokens(merge(lines, kept, lax.ppermute(given, "row", pairs)))
    output = (middle + here[1] + out_other.astype(F32)).astype(BF)
    output = to_own_features(output)
    returned, output, mid_pieces = lax.optimization_barrier(
        (returned, output, summed(mid_pieces))
    )

    grads_qkv, inner_qkv, row_end, col_end = qkv_unshape(
        returned,
        pre,
        masked_qkv,
        own_tokens,
        gain_one,
        cosine,
        sine,
        head_gains,
        attention_weights,
    )
    end_pieces = lax.all_to_all(pieces_of(row_end, col_end), PLANE, 0, 0, tiled=True)
    grad_low = qkv_backward(
        grads_qkv, inner_qkv, own_tokens, grad_middle, gain_one, in_qkv, attention_weights
    )
    grad_low, end_pieces = lax.optimization_barrier((grad_low, end_pieces))
    input_gradient = lax.all_to_all(grad_low, "row", 1, 0, tiled=True).astype(F32)
    mid_tables, end_tables = gathered_tables(
        (mid_pieces, summed(end_pieces)), (7 * rank, 3 * rank), (7 * rank, rank)
    )
    ids = jnp.stack([own_adapter, other_adapter, plane]).astype(jnp.int32)
    down_rows = down_matrix.shape[0]
    wide_a, wide_o, wide_d = (features, columns), (o_rows, columns), (down_rows, columns)
    finished = finish(
        finish_middle_kernel,
        ids,
        *mid_tables,
        [
            wide_o,
            (columns, features),
            wide_a,
            (columns, down_rows),
            wide_a,
            (columns, down_rows),
            wide_d,
            (columns, features),
        ],
        "finish_middle",
    )
    finished_qkv = finish(
        finish_end_kernel,
        ids,
        *end_tables,
        [wide_a, (columns, q_local), wide_a, (columns, kv_local), wide_a, (columns, kv_local)],
        "finish_end",
    )

    return (output, input_gradient, *finished_qkv, *finished)


def solution(mesh):
    return jax.shard_map(
        on_device,
        mesh=mesh,
        in_specs=(
            P(("dp", "col"), "row"),
            P(("dp", "col"), "row"),
            P("row"),
            P("row"),
            P(),
            P(),
            P("row", "col"),
            P("row", "col"),
            P("row", "col"),
            P("col", "row"),
            P("row", "col"),
            P("row", "col"),
            P("col", "row"),
            P("row", None),
            P(None, "col"),
            P("row", None),
            P(None, "col"),
            P("row", None),
            P(None, "col"),
            P("col", None),
            P(None, "row"),
            P("row", None),
            P(None, "col"),
            P("row", None),
            P(None, "col"),
            P("col", None),
            P(None, "row"),
            P("dp"),
            P("dp"),
            P("dp", None),
            P("dp"),
        ),
        out_specs=(
            P(("dp", "col"), "row"),
            P(("dp", "col"), "row"),
            P("row", None),
            P(None, "col"),
            P("row", None),
            P(None, "col"),
            P("row", None),
            P(None, "col"),
            P("col", None),
            P(None, "row"),
            P("row", None),
            P(None, "col"),
            P("row", None),
            P(None, "col"),
            P("col", None),
            P(None, "row"),
        ),
        check_vma=False,
    )
```
